32 devices in a mesh: dp: 8 (over z, y), tensor: 4 (over x, core).
Axes of the slice: x: 2, y: 2, z: 4, core: 2. Of those that a mesh axis runs over, the one named last changes fastest.
Arguments:
- embeddings: bfloat16 [16384, 768], P('dp'), may hold values from -6 to 6
- cotangent: bfloat16 [16384, 768], P('dp'), may hold values from -6 to 6
- species: int32 [8], P('dp'), may hold values from 0 to 2, as said below
- gene_ids: int32 [8, 2048], P('dp'), may hold values from 0 to 32767, as said below
- w_qkv: float32 [3, 768, 768], P(None, 'dp', 'tensor'), may hold values from -0.21875 to 0.21875
- w_out: float32 [768, 768], P('tensor', 'dp'), may hold values from -6 to 6
- w_up: float32 [768, 3072], P('dp', 'tensor'), may hold values from -0.21875 to 0.21875
- w_down: float32 [3072, 768], P('tensor', 'dp'), may hold values from -0.109375 to 0.109375
- norm_gains: float32 [2, 768], P(None, 'dp'), may hold values from 0.1 to 1.9
- norm_shifts: float32 [2, 768], P(None, 'dp'), may hold values from -1.8 to 1.8
Outputs:
- mixed: bfloat16 [16384, 768], P('dp')
- grad_input: bfloat16 [16384, 768], P('dp')
- grad_qkv: float32 [3, 768, 768], P(None, 'dp', 'tensor')
- grad_out: float32 [768, 768], P('tensor', 'dp')
- grad_up: float32 [768, 3072], P('dp', 'tensor')
- grad_down: float32 [3072, 768], P('tensor', 'dp')
- grad_gains: float32 [2, 768], P(None, 'dp')
- grad_shifts: float32 [2, 768], P(None, 'dp')
- grad_ffn_shift: float32 [768], P('dp')
The draws below stay inside these ranges and needn't reach their ends.
Inputs may be any that keep to these rules, and one draw needn't show every extreme that they name: `species`: 0 marks a human cell, 1 a mouse cell, 2 a padding cell; some cell is a padding cell. `gene_ids`: each cell holds gene ids 1 to 32767 in its first positions and 0 (padding) after them; a cell has 1024 to 2048 nonzero ids, and some cell has 2048.
All inputs are finite; a program needn't handle non-finite values.
Results may differ from the reference program's by a relative error of at most 0.017.
Values may be sent and summed in bfloat16 or wider, within the bound.
No kernel may reach another device: no remote copies, remote signals or barrier semaphores. Data moves between devices by JAX's collectives and lax.ppermute only.
A program may use at most 128 MiB of HBM per device.

```python
import math
import jax
import jax.numpy as jnp
from jax import lax

D = 768
HEADS = 12
HD = 64
FF = 3072
GENES = 2048
VOCAB = 32768
CELLS = 8
TOKENS = 16384
N_TENSOR = 4


def draw_species(key, part):
    first, second = jax.random.split(jax.random.fold_in(key, 11))
    ranks = jax.random.randint(first, (CELLS,), 0, 10)
    flags = (ranks >= 6).astype(jnp.int32) + (ranks >= 9).astype(jnp.int32)
    padded = jax.random.randint(second, (), 0, CELLS)
    return jnp.where(jnp.arange(CELLS) == padded, 2, flags).astype(jnp.int32)


def draw_gene_ids(key, part):
    first, second, third = jax.random.split(jax.random.fold_in(key, 23), 3)
    lengths = jax.random.randint(first, (CELLS,), GENES // 2, GENES + 1)
    filled = jax.random.randint(second, (), 0, CELLS)
    lengths = jnp.where(jnp.arange(CELLS) == filled, GENES, lengths)
    labels = jax.random.randint(third, (CELLS, GENES), 1, VOCAB)
    return jnp.where(jnp.arange(GENES)[None, :] < lengths[:, None], labels, 0).astype(jnp.int32)


def strengthened(array, stream_key, source, target, blocks, factor):
    owner, partner = [(jnp.arange(array.shape[position]) // (array.shape[position] // blocks)).reshape([-1 if axis == position else 1 for axis in range(array.ndim)]) for position in (source, target)]
    chosen = jax.random.permutation(stream_key, blocks)[partner]
    strong = (owner == chosen) | (owner == (partner + blocks // 2) % blocks)
    return jnp.where(strong, factor * array, array)


def block_scale(own_key, extent, cuts, low, high):
    level = 1.0
    for dim, blocks in cuts:
        draws = jax.random.uniform(jax.random.fold_in(jax.random.fold_in(own_key, 6), dim), (blocks,), jnp.float32, low / len(cuts), high / len(cuts))
        level = level * jnp.repeat(jnp.exp(draws), extent[dim] // blocks).reshape((-1,) + (1,) * (len(extent) - 1 - dim))
    return level


def normal_values(key, shape, deviation, bound, shards=(), held_as=jnp.bfloat16):
    entries = deviation * jax.random.normal(key, shape, jnp.float32)
    if shards:
        entries = entries * block_scale(key, shape, shards, -0.22, 0.18)
    return jnp.clip(entries, -bound, bound).astype(held_as)


def noise_with(rng, dims, deviation, reach, cuts, heavy, held_as=jnp.bfloat16):
    entries = deviation * jax.random.normal(rng, dims, jnp.float32)
    if cuts:
        entries = entries * block_scale(rng, dims, cuts, -0.22, 0.18)
    return jnp.clip(strengthened(entries, jax.random.fold_in(rng, 3), *heavy), -reach, reach).astype(held_as)


def setup_inputs(seed: int = 0) -> dict:
    arg_keys = jax.random.split(jax.random.key(seed), 11)
    return {
        "embeddings": noise_with(arg_keys[0], (TOKENS, D), 1.0, 6.0, ((0, 8),), (0, 1, 8, 2.0)),
        "cotangent": noise_with(arg_keys[1], (TOKENS, D), 1.0, 6.0, ((0, 8),), (0, 1, 8, 2.0)),
        "species": draw_species(jax.random.fold_in(arg_keys[10], 71), 0),
        "gene_ids": draw_gene_ids(jax.random.fold_in(arg_keys[10], 71), 0),
        "w_qkv": normal_values(arg_keys[4], (3, D, D), D ** -0.5, 0.21875, ((1, 8), (2, 4)), jnp.float32),
        "w_out": normal_values(arg_keys[5], (D, D), (max(1, 2 * D // GENES)) ** -0.5, 6.0, ((0, 4), (1, 8)), jnp.float32),
        "w_up": normal_values(arg_keys[6], (D, FF), D ** -0.5, 0.21875, ((0, 8), (1, 4)), jnp.float32),
        "w_down": normal_values(arg_keys[7], (FF, D), FF ** -0.5, 0.109375, ((0, 4), (1, 8)), jnp.float32),
        "norm_gains": jnp.clip(1.0 + 0.18 * jax.random.normal(arg_keys[8], (2, D), jnp.float32), 0.1, 1.9),
        "norm_shifts": normal_values(arg_keys[9], (2, D), 0.3, 1.8, ((1, 8),), jnp.float32),
    }


EPSILON = 1e-05
NEGATIVE = -1e+30
HIGHEST = lax.Precision.HIGHEST

@jax.custom_vjp
def low(v):
    return lax.optimization_barrier(v.astype(jnp.bfloat16)).astype(jnp.float32)

@jax.custom_vjp
def low_back(v):
    return v

def low_keep(v):
    return (low(v), None)

def low_pass(kept, grad):
    return (grad,)

def back_keep(v):
    return (v, None)

def back_low(kept, grad):
    return (low(grad),)
low.defvjp(low_keep, low_pass)
low_back.defvjp(back_keep, back_low)

def both_ways(value):
    return low_back(low(value))

def layer_norm(inputs, gain, shift):
    center = inputs - lax.optimization_barrier(jnp.mean(inputs, axis=-1, keepdims=True))
    variance = lax.optimization_barrier(jnp.mean(center * center, axis=-1, keepdims=True))
    return center * lax.rsqrt(variance + EPSILON) * gain + shift

def attention(queries, key_rows, value_rows, keep):
    length = queries.shape[0]
    blocksz = min(512, length)
    scale = 1.0 / math.sqrt(HD)

    def one_block(query_block):
        raw_scores = jnp.einsum('qhe,khe->hqk', query_block, key_rows, precision=HIGHEST) * scale
        scores = jnp.where(keep[None, None, :], low_back(raw_scores), NEGATIVE)
        weights = low(jax.nn.softmax(scores, axis=-1))
        return jnp.einsum('hqk,khe->qhe', weights, value_rows, precision=HIGHEST)
    blocks = queries.reshape(length // blocksz, blocksz, queries.shape[1], queries.shape[2])
    return lax.map(jax.checkpoint(one_block), blocks).reshape(queries.shape)

def split_product(left, right):
    width = left.shape[1] // N_TENSOR
    total = None
    for member in range(N_TENSOR):
        piece = low(jnp.dot(left[:, member * width:(member + 1) * width], right[member * width:(member + 1) * width], precision=HIGHEST))
        total = piece if total is None else total + piece
    return low_back(total)

def layer(params, inputs, keep):
    w_qkv, w_out, w_up, w_down, gains, shifts = [low(element) for element in params]
    length = inputs.shape[0]
    normed = low(layer_norm(inputs, gains[0], shifts[0]))
    projected = [both_ways(jnp.dot(normed, w_qkv[index], precision=HIGHEST)).reshape(length, HEADS, HD) for index in range(3)]
    heads_out = both_ways(attention(projected[0], projected[1], projected[2], keep).reshape(length, D))
    hidden = inputs + split_product(heads_out, w_out)
    second = low(layer_norm(hidden, gains[1], shifts[1]))
    before = low_back(jnp.dot(second, w_up, precision=HIGHEST))
    activated = low(jax.nn.gelu(before, approximate=False))
    return hidden + split_product(activated, w_down)

def reference(embeddings, cotangent, species, gene_ids, w_qkv, w_out, w_up, w_down, norm_gains, norm_shifts):
    params = (w_qkv, w_out, w_up, w_down, norm_gains, norm_shifts)
    inputs = embeddings.astype(jnp.float32).reshape(CELLS, GENES, D)
    seeds = cotangent.astype(jnp.float32).reshape(CELLS, GENES, D)
    keep_all = gene_ids != 0
    live = jnp.logical_and(keep_all, (species != 2)[:, None]).astype(jnp.float32)

    def one_cell(totals, element):
        cell_in, cell_seed, cell_keep, cell_live = element
        result, backward = jax.vjp(lambda weights, cell_rows: layer(weights, cell_rows, cell_keep), params, cell_in)
        grads_w, grads_in = backward(cell_seed * cell_live[:, None])
        totals = jax.tree.map(jnp.add, totals, grads_w)
        return (totals, (result.astype(jnp.bfloat16), grads_in.astype(jnp.bfloat16)))
    start = jax.tree.map(jnp.zeros_like, params)
    totals, (mixed, grad_rows) = lax.scan(one_cell, start, (inputs, seeds, keep_all, live))
    return (mixed.reshape(TOKENS, D), grad_rows.reshape(TOKENS, D), totals[0], totals[1], totals[2], totals[3], totals[4], totals[5], totals[5][1])
```

```python
import functools
import math

import jax
import jax.numpy as jnp
from jax import lax
from jax.experimental import pallas as pl
from jax.experimental.pallas import tpu as pltpu
from jax.sharding import PartitionSpec as P

HD = 64
EPSILON = 1e-05
NEGATIVE = -1e30
LOG2E = math.log2(math.e)
bf = jnp.bfloat16
f32 = jnp.float32
NN = ((1,), (0,))
NT = ((1,), (1,))
TN = ((0,), (0,))
ORDER = (0, 2, 1, 3)


def dot(a, b, dims):
    return lax.dot_general(a, b, (dims, ((), ())), preferred_element_type=f32)


def swap(value, axis, mask, size):
    return lax.ppermute(value, axis, [(i, i ^ mask) for i in range(size)])


def split3(v):
    a = v.astype(bf)
    rest = v - a.astype(f32)
    b = rest.astype(bf)
    c = (rest - b.astype(f32)).astype(bf)
    return [a.astype(f32), b.astype(f32), c.astype(f32)]


def with_tail(block, rows):
    q = block.shape[1]
    index = lax.broadcasted_iota(jnp.int32, (HD, q), 0)
    tail = jnp.zeros((HD, q), f32)
    for i, row in enumerate(rows):
        tail = jnp.where(index == i, row, tail)
    return jnp.concatenate([block, tail.astype(bf)], axis=0)


def project_kernel(heads, t_ref, x_ref, w_ref, norm_ref, a_ref, kp_ref, vp_ref, kt_ref, vt_ref, qt_ref, wt_scr, wk_scr, wv_scr):
    step = pl.program_id(0)
    rows = x_ref.shape[0]

    @pl.when(step == 0)
    def _():
        wt_scr[...] = w_ref[...].T
        zero = jnp.zeros((w_ref.shape[0], HD), bf)
        for h in range(heads):
            base = 3 * HD * h
            wk_scr[:, 2 * HD * h : 2 * HD * (h + 1)] = jnp.concatenate([w_ref[:, base + HD : base + 2 * HD], zero], axis=1)
            wv_scr[:, 2 * HD * h : 2 * HD * (h + 1)] = jnp.concatenate([w_ref[:, base + 2 * HD : base + 3 * HD], zero], axis=1)

    x = x_ref[...].astype(f32)
    center = x - jnp.mean(x, axis=-1, keepdims=True)
    variance = jnp.mean(center * center, axis=-1, keepdims=True)
    a = (center * lax.rsqrt(variance + EPSILON) * norm_ref[0:1, :] + norm_ref[2:3, :]).astype(bf)
    a_ref[...] = a
    block = step ^ t_ref[0]
    token = block * rows + lax.broadcasted_iota(jnp.int32, (rows, 2 * HD * heads), 0)
    lane = lax.broadcasted_iota(jnp.int32, (rows, 2 * HD * heads), 1) % (2 * HD)
    ones = jnp.where((lane > HD) & (lane < HD + 4), 1.0, 0.0)
    bias = jnp.where((lane == HD) & (token >= t_ref[1]), NEGATIVE, ones)
    kp_ref[...] = (dot(a, wk_scr[...], NN) + bias).astype(bf)
    vp_ref[...] = (dot(a, wv_scr[...], NN) + ones).astype(bf)
    both = dot(wt_scr[...], a, NT)
    for h in range(heads):
        base = 3 * HD * h
        at = slice(HD * h, HD * (h + 1))
        qt_ref[at, :] = (both[base : base + HD] * 0.125).astype(bf)
        kt_ref[at, :] = both[base + HD : base + 2 * HD].astype(bf)
        vt_ref[at, :] = both[base + 2 * HD : base + 3 * HD].astype(bf)


def project(scalars, x, w, norms):
    count, width = x.shape
    heads = w.shape[1] // (3 * HD)
    rows = count // 4
    block = lambda i, t: (i ^ t[0], 0)
    turned = lambda i, t: (0, i ^ t[0])
    whole = lambda i, t: (0, 0)
    wide = 2 * HD * heads
    spec = pltpu.PrefetchScalarGridSpec(
        num_scalar_prefetch=1,
        grid=(4,),
        in_specs=[
            pl.BlockSpec((rows, width), block),
            pl.BlockSpec(w.shape, whole),
            pl.BlockSpec(norms.shape, whole),
        ],
        out_specs=[
            pl.BlockSpec((rows, width), lambda i, t: (i, 0)),
            pl.BlockSpec((rows, wide), block),
            pl.BlockSpec((rows, wide), block),
            pl.BlockSpec((HD * heads, rows), turned),
            pl.BlockSpec((HD * heads, rows), turned),
            pl.BlockSpec((HD * heads, rows), turned),
        ],
        scratch_shapes=[
            pltpu.VMEM((w.shape[1], width), bf),
            pltpu.VMEM((width, wide), bf),
            pltpu.VMEM((width, wide), bf),
        ],
    )
    return pl.pallas_call(
        functools.partial(project_kernel, heads),
        grid_spec=spec,
        out_shape=[
            jax.ShapeDtypeStruct((count, width), bf),
            jax.ShapeDtypeStruct((count, wide), bf),
            jax.ShapeDtypeStruct((count, wide), bf),
            jax.ShapeDtypeStruct((HD * heads, count), bf),
            jax.ShapeDtypeStruct((HD * heads, count), bf),
            jax.ShapeDtypeStruct((HD * heads, count), bf),
        ],
        compiler_params=pltpu.CompilerParams(vmem_limit_bytes=48 << 20),
        cost_estimate=pl.CostEstimate(flops=2 * count * width * 5 * HD * heads, bytes_accessed=count * width * 8, transcendentals=0),
        name="project",
    )(scalars, x, w, norms)


def attend_kernel(chunk, t_ref, kp_ref, vt_ref, qt_ref, o_ref, lse_ref, s_scr):
    q = qt_ref.shape[1]
    keys = kp_ref.shape[0]
    queries = with_tail(qt_ref[...], [jnp.ones((1, q), f32)])
    top = None
    for i in range(keys // chunk):
        at = slice(i * chunk, (i + 1) * chunk)
        s = dot(kp_ref[at, :], queries, NN)
        s_scr[at, :] = s
        here = jnp.max(s, axis=0, keepdims=True)
        top = here if top is None else jnp.maximum(top, here)
    total = None
    out = None
    for i in range(keys // chunk):
        at = slice(i * chunk, (i + 1) * chunk)
        p = jnp.exp2((s_scr[at, :] - top) * LOG2E)
        here = jnp.sum(p, axis=0, keepdims=True)
        part = dot(vt_ref[:, at], p.astype(bf), NN)
        total = here if total is None else total + here
        out = part if out is None else out + part
    o_ref[0] = (out / total).astype(bf)
    lse_ref[0, 0] = jnp.broadcast_to(top + jnp.log(total), (8, q))


def attend(scalars, kp, vt, qt):
    count = kp.shape[0]
    heads = qt.shape[0] // HD
    q = count // 4
    spec = pltpu.PrefetchScalarGridSpec(
        num_scalar_prefetch=1,
        grid=(heads, 4),
        in_specs=[
            pl.BlockSpec((count, 2 * HD), lambda h, i, t: (0, h)),
            pl.BlockSpec((HD, count), lambda h, i, t: (h, 0)),
            pl.BlockSpec((HD, q), lambda h, i, t: (h, i ^ t[0])),
        ],
        out_specs=[
            pl.BlockSpec((1, HD, q), lambda h, i, t: (i, h, 0)),
            pl.BlockSpec((1, 1, 8, q), lambda h, i, t: (h, i, 0, 0)),
        ],
        scratch_shapes=[pltpu.VMEM((count, q), f32)],
    )
    return pl.pallas_call(
        functools.partial(attend_kernel, min(512, count)),
        grid_spec=spec,
        out_shape=[
            jax.ShapeDtypeStruct((4, heads * HD, q), bf),
            jax.ShapeDtypeStruct((heads, 4, 8, q), f32),
        ],
        compiler_params=pltpu.CompilerParams(vmem_limit_bytes=48 << 20),
        cost_estimate=pl.CostEstimate(flops=heads * 4 * count * count * 256, bytes_accessed=heads * count * 512, transcendentals=heads * count * count),
        name="attend",
    )(scalars, kp, vt, qt)


def attend_back_kernel(chunk, t_ref, kp_ref, vp_ref, kt_ref, qt_ref, o_ref, lse_ref, do_ref, out_ref, dk_scr, dv_scr):
    q = qt_ref.shape[1]
    keys = kp_ref.shape[0]
    step = pl.program_id(0)

    @pl.when(step == 0)
    def _():
        dk_scr[...] = jnp.zeros_like(dk_scr)
        dv_scr[...] = jnp.zeros_like(dv_scr)

    qt = qt_ref[...]
    do = do_ref[0]
    delta = jnp.sum(do.astype(f32) * o_ref[0].astype(f32), axis=0, keepdims=True)
    one = jnp.ones((1, q), f32)
    queries = with_tail(qt, [one] + [-v for v in split3(lse_ref[0, 0, 0:1])])
    grads = with_tail(do, [0.0 * one] + [-v for v in split3(delta)])
    dq = None
    for i in range(keys // chunk):
        at = slice(i * chunk, (i + 1) * chunk)
        p = jnp.exp2(dot(kp_ref[at, :], queries, NN) * LOG2E)
        dp = dot(vp_ref[at, :], grads, NN)
        ds = (p * dp).astype(bf)
        dv_scr[at, :] += dot(p.astype(bf), do, NT)
        dk_scr[at, :] += dot(ds, qt, NT)
        part = dot(kt_ref[:, at], ds, NN)
        dq = part if dq is None else dq + part
    out_ref[step, 0:HD, :] = (dq * 0.125).astype(bf)

    @pl.when(step == pl.num_programs(0) - 1)
    def _():
        for i in range(4):
            at = pl.ds(pl.multiple_of((i ^ t_ref[0]) * q, q), q)
            out_ref[i, HD : 2 * HD, :] = dk_scr[at, :].T.astype(bf)
            out_ref[i, 2 * HD : 3 * HD, :] = dv_scr[at, :].T.astype(bf)


def attend_back(scalars, kp, vp, kt, qt, o, lse, do, h):
    count = kp.shape[0]
    q = count // 4
    whole = lambda i, t: (0, h)
    spec = pltpu.PrefetchScalarGridSpec(
        num_scalar_prefetch=1,
        grid=(4,),
        in_specs=[
            pl.BlockSpec((count, 2 * HD), whole),
            pl.BlockSpec((count, 2 * HD), whole),
            pl.BlockSpec((HD, count), lambda i, t: (h, 0)),
            pl.BlockSpec((HD, q), lambda i, t: (h, i ^ t[0])),
            pl.BlockSpec((1, HD, q), lambda i, t: (i, h, 0)),
            pl.BlockSpec((1, 1, 8, q), lambda i, t: (h, i, 0, 0)),
            pl.BlockSpec((1, HD, q), lambda i, t: (i, h, 0)),
        ],
        out_specs=pl.BlockSpec((4, 3 * HD, q), lambda i, t: (0, 0, 0)),
        scratch_shapes=[pltpu.VMEM((count, HD), f32), pltpu.VMEM((count, HD), f32)],
    )
    return pl.pallas_call(
        functools.partial(attend_back_kernel, min(512, count)),
        grid_spec=spec,
        out_shape=jax.ShapeDtypeStruct((4, 3 * HD, q), bf),
        compiler_params=pltpu.CompilerParams(vmem_limit_bytes=48 << 20),
        cost_estimate=pl.CostEstimate(flops=10 * count * count * 256, bytes_accessed=count * 2048, transcendentals=count * count),
        name=f"attend_back{h}",
    )(scalars, kp, vp, kt, qt, o, lse, do)


def place(pieces, index, size):
    out = jnp.zeros((size,) + pieces[0].shape, pieces[0].dtype)
    for s, piece in enumerate(pieces):
        out = lax.dynamic_update_slice(out, piece[None], (index ^ s,) + (0,) * piece.ndim)
    return out


def gather_rows(piece, n):
    if n != 8:
        return lax.all_gather(piece, "dp", axis=0)
    d = lax.axis_index("dp")
    along_z = place([piece] + [swap(piece, "dp", 2 * s, n) for s in (1, 2, 3)], d // 2, 4)
    other = swap(along_z, "dp", 1, n)
    both = jnp.where(d % 2 == 0, jnp.stack([along_z, other], 1), jnp.stack([other, along_z], 1))
    return both.reshape((n,) + piece.shape)


def gather_all(piece, n):
    pair = jnp.stack([piece, swap(piece, "tensor", 2, 4)])
    rows = gather_rows(pair, n)
    mine = jnp.moveaxis(rows, 1, 0)
    return jnp.concatenate([mine, swap(mine, "tensor", 1, 4)])


def scatter_rows(value, n):
    if n != 8:
        return lax.psum_scatter(value, "dp", scatter_dimension=0, tiled=False).astype(f32)
    d = lax.axis_index("dp")
    pairs = value.reshape((4, 2) + value.shape[1:])
    keep = lax.dynamic_index_in_dim(pairs, d % 2, 1, False)
    send = lax.dynamic_index_in_dim(pairs, 1 - d % 2, 1, False)
    half = (keep.astype(f32) + swap(send, "dp", 1, n).astype(f32)).astype(bf)
    z = d // 2
    total = lax.dynamic_index_in_dim(half, z, 0, False).astype(f32)
    for s in (1, 2, 3):
        total = total + swap(lax.dynamic_index_in_dim(half, z ^ s, 0, False), "dp", 2 * s, n).astype(f32)
    return total


def scatter_all(mine, theirs, n):
    pair = (mine.astype(f32) + swap(theirs, "tensor", 1, 4).astype(f32)).astype(bf)
    one = (pair[0].astype(f32) + swap(pair[1], "tensor", 2, 4).astype(f32)).astype(bf)
    return scatter_rows(one, n)


def collect(block):
    t = lax.axis_index("tensor")
    across = swap(block, "tensor", 2, 4)
    pieces = [block, swap(block, "tensor", 1, 4), across, swap(across, "tensor", 1, 4)]
    return place(pieces, t, 4).reshape(4 * block.shape[0], block.shape[1])


def exchange(blocks):
    return [blocks[0]] + [swap(blocks[k], "tensor", k, 4) for k in (1, 2, 3)]


def sum_everywhere(value, n):
    value = value + swap(value, "tensor", 1, 4)
    value = value + swap(value, "tensor", 2, 4)
    if n != 8:
        return lax.psum(value, "dp")
    value = value + swap(value, "dp", 1, n)
    return value + swap(value, "dp", 2, n) + swap(value, "dp", 4, n) + swap(value, "dp", 6, n)


def normalize(v):
    center = v - jnp.mean(v, axis=-1, keepdims=True)
    variance = jnp.mean(center * center, axis=-1, keepdims=True)
    r = lax.rsqrt(variance + EPSILON)
    return center * r, r


def norm_back(dn, n, r, gain):
    scaled = dn * gain
    return r * (scaled - jnp.mean(scaled, axis=-1, keepdims=True) - n * jnp.mean(scaled * n, axis=-1, keepdims=True))


def body(n, embeddings, cotangent, species, gene_ids, w_qkv, w_out, w_up, w_down, norm_gains, norm_shifts):
    t = lax.axis_index("tensor")
    d = lax.axis_index("dp")
    count, width = embeddings.shape
    rows = count // 4
    r = width // n
    local = w_qkv.shape[2]
    heads = local // HD
    units = w_up.shape[1]
    length = jnp.sum((gene_ids != 0).astype(jnp.int32))
    alive = jnp.where(species[0] == 2, 0, length)
    scalars = jnp.stack([t.astype(jnp.int32), length])

    qkv_own = w_qkv.astype(bf).reshape(3, r, heads, HD).transpose(1, 2, 0, 3).reshape(r, 3 * local)
    norms_own = jnp.concatenate([norm_gains, norm_shifts]).astype(bf)
    norms_own = jnp.pad(norms_own, ((0, 12), (0, 3 * local - r)))
    first = gather_rows(jnp.concatenate([qkv_own, norms_own]), n)
    w_first = first[:, :r].reshape(width, 3 * local)
    norms = first[:, r : r + 4, :r].transpose(1, 0, 2).reshape(4, width).astype(f32)
    rest_own = jnp.concatenate([w_out.astype(bf).T, w_up.astype(bf), w_down.astype(bf).T], axis=1)
    rest = gather_all(rest_own, n).reshape(4, width, local + 2 * units)
    out_t, up, down_t = rest[:, :, :local], rest[:, :, local : local + units], rest[:, :, local + units :]
    pair = jnp.stack([w_first, swap(w_first, "tensor", 2, 4)])
    w_all = jnp.concatenate([pair, swap(pair, "tensor", 1, 4)])

    normed, kp, vp, kt, vt, qt = project(scalars, embeddings, w_first, norms)
    o_local, lse = attend(scalars, kp, vt, qt)
    o_here = exchange(o_local)
    o = jnp.stack([o_here[k] for k in ORDER])

    start = t * rows
    x = lax.dynamic_slice(embeddings, (start, 0), (rows, width)).astype(f32)
    g = lax.dynamic_slice(cotangent, (start, 0), (rows, width)).astype(f32)
    g = jnp.where(start + lax.broadcasted_iota(jnp.int32, (rows, 1), 0) < alive, g, 0.0)
    gb = g.astype(bf)
    h = x + jnp.einsum("kft,kdf->td", o, out_t, preferred_element_type=f32)
    n2, r2 = normalize(h)
    c = (n2 * norms[1:2] + norms[3:4]).astype(bf)
    u = jnp.einsum("td,kdu->ktu", c, up, preferred_element_type=f32)
    phi = 0.5 * (1.0 + lax.erf(u * math.sqrt(0.5)))
    e = (u * phi).astype(bf)
    de = jnp.einsum("td,kdu->ktu", gb, down_t, preferred_element_type=f32)
    du = (de * (phi + u * jnp.exp(-0.5 * u * u) * (1.0 / math.sqrt(2.0 * math.pi)))).astype(bf)
    dc = jnp.einsum("ktu,kdu->td", du, up, preferred_element_type=f32)
    dh = g + norm_back(dc, n2, r2, norms[1:2])
    dhb = dh.astype(bf)
    do = jnp.einsum("kdf,td->kft", out_t, dhb, preferred_element_type=f32).astype(bf)
    do_back = exchange([do[ORDER.index(k)] for k in range(4)])
    do_local = jnp.stack(do_back)
    mixed = collect((h + jnp.einsum("ktu,kdu->td", e, down_t, preferred_element_type=f32)).astype(bf))

    g_out = jnp.einsum("td,kft->kdf", dhb, o, preferred_element_type=f32).astype(bf)
    g_up = jnp.einsum("td,ktu->kdu", c, du, preferred_element_type=f32).astype(bf)
    g_down = jnp.einsum("td,ktu->kdu", gb, e, preferred_element_type=f32).astype(bf)
    cut = lambda v: v.reshape(2, n, r, v.shape[-1])
    s_down = scatter_all(cut(g_down[:2]), cut(g_down[2:]), n)
    s_up = scatter_all(cut(g_up[:2]), cut(g_up[2:]), n)
    s_out = scatter_all(cut(g_out[:2]), cut(g_out[2:]), n)

    parts, arrived = [], []
    for head in range(heads):
        grads = attend_back(scalars, kp, vp, kt, qt, o_local, lse, do_local, head)
        parts.append(grads)
        arrived.append(exchange(grads))
    normed = normed.reshape(4, rows, width)
    g_first = jnp.concatenate([jnp.einsum("ktd,kft->df", normed, p, preferred_element_type=f32).astype(bf) for p in parts], axis=1)
    s_first = scatter_rows(g_first.reshape(n, r, 3 * local), n)
    dqkv = jnp.stack([jnp.concatenate([a[k] for a in arrived], axis=0) for k in ORDER])
    da = jnp.einsum("kft,kdf->td", dqkv, w_all, preferred_element_type=f32)
    n1, r1 = normalize(x)
    dx = dh + norm_back(da, n1, r1, norms[0:1])
    grad_input = collect(dx.astype(bf))
    sums = jnp.stack([jnp.sum(da * n1, 0), jnp.sum(dc * n2, 0), jnp.sum(da, 0), jnp.sum(dc, 0)])
    sums = lax.dynamic_slice(sum_everywhere(sums, n), (0, d * r), (4, r))
    s_qkv = s_first.reshape(r, heads, 3, HD).transpose(2, 0, 1, 3).reshape(3, r, local)
    return (mixed, grad_input, s_qkv, s_out.T, s_up, s_down.T, sums[:2], sums[2:], sums[3])


def solution(mesh):
    return jax.shard_map(
        functools.partial(body, mesh.shape["dp"]),
        mesh=mesh,
        in_specs=(
            P("dp", None),
            P("dp", None),
            P("dp"),
            P("dp", None),
            P(None, "dp", "tensor"),
            P("tensor", "dp"),
            P("dp", "tensor"),
            P("tensor", "dp"),
            P(None, "dp"),
            P(None, "dp"),
        ),
        out_specs=(
            P("dp", None),
            P("dp", None),
            P(None, "dp", "tensor"),
            P("tensor", "dp"),
            P("dp", "tensor"),
            P("tensor", "dp"),
            P(None, "dp"),
            P(None, "dp"),
            P("dp"),
        ),
        check_vma=False,
    )
```

```python
import functools
import math

import jax
import jax.numpy as jnp
from jax import lax
from jax.experimental import pallas as pl
from jax.experimental.pallas import tpu as pltpu
from jax.sharding import PartitionSpec as P

HD = 64
EPSILON = 1e-05
NEGATIVE = -1e30
LOG2E = math.log2(math.e)
bf = jnp.bfloat16
f32 = jnp.float32
NN = ((1,), (0,))
NT = ((1,), (1,))
ANY = pl.BlockSpec(memory_space=pl.ANY)
SDS = jax.ShapeDtypeStruct


def dot(a, b, dims=NN):
    return lax.dot_general(a, b, (dims, ((), ())), preferred_element_type=f32)


def swap(value, axis, mask, size):
    return lax.ppermute(value, axis, [(i, i ^ mask) for i in range(size)])


def core_swap(value):
    return swap(value, "tensor", 1, 4)


def x_swap(value):
    return swap(value, "tensor", 2, 4)


def after(value, *others):
    return lax.optimization_barrier((value,) + others)[0]


def params(mib=48):
    return pltpu.CompilerParams(vmem_limit_bytes=mib << 20)


def cost(flops, moved, exps=0):
    return pl.CostEstimate(flops=int(flops), bytes_accessed=int(moved), transcendentals=int(exps))


def whole(shape):
    return pl.BlockSpec(shape, lambda *_: (0,) * len(shape))


def row_copies(refs, d, count, dst, columns, sem):
    copies = []
    if len(refs) == 1:
        copies.append(pltpu.make_async_copy(refs[0].at[:, columns], dst, sem))
        return copies
    r = count // 8
    for y, ref in enumerate(refs):
        for s in range(4):
            at = pl.multiple_of((d ^ (2 * s + y)) * r, r)
            copies.append(pltpu.make_async_copy(ref.at[s, 0:r, columns], dst.at[pl.ds(at, r), :], sem))
    return copies


def wait_for(dst, sem):
    pltpu.make_async_copy(dst, dst, sem).wait()


def split3(v):
    a = v.astype(bf)
    rest = v - a.astype(f32)
    b = rest.astype(bf)
    c = (rest - b.astype(f32)).astype(bf)
    return [a.astype(f32), b.astype(f32), c.astype(f32)]


def with_tail(block, rows):
    q = block.shape[1]
    index = lax.broadcasted_iota(jnp.int32, (HD, q), 0)
    tail = jnp.zeros((HD, q), f32)
    for i, row in enumerate(rows):
        tail = jnp.where(index == i, row, tail)
    return jnp.concatenate([block, tail.astype(bf)], axis=0)


def normalize(v):
    center = v - jnp.mean(v, axis=-1, keepdims=True)
    variance = jnp.mean(center * center, axis=-1, keepdims=True)
    r = lax.rsqrt(variance + EPSILON)
    return center * r, r


def norm_back(dn, n, r, gain):
    scaled = dn * gain
    return r * (scaled - jnp.mean(scaled, axis=-1, keepdims=True) - n * jnp.mean(scaled * n, axis=-1, keepdims=True))


def project_kernel(heads, pieces, c_ref, x_ref, *refs):
    w_refs = refs[:pieces]
    n_ref = refs[pieces] if pieces == 1 else None
    a_ref, kp_ref, vp_ref, kt_ref, vt_ref, qt_ref, norm_ref, w_scr, n_scr, wt_scr, wk_scr, wv_scr, sems = refs[pieces + (pieces == 1) :]
    step = pl.program_id(0)
    rows, width = x_ref.shape
    local = HD * heads

    @pl.when(step == 0)
    def _():
        copies = row_copies(w_refs, c_ref[1], width, w_scr, slice(0, 3 * local), sems.at[0])
        if pieces == 1:
            copies.append(pltpu.make_async_copy(n_ref, n_scr.at[0], sems.at[1]))
        else:
            r = width // 8
            for y, ref in enumerate(w_refs):
                for s in range(4):
                    copies.append(pltpu.make_async_copy(ref.at[s, r : r + 16, :], n_scr.at[4 * y + s], sems.at[1]))
        for copy in copies:
            copy.start()
        wait_for(n_scr, sems.at[1])
        found = jnp.sum(n_scr[...].astype(f32), axis=0)
        norm_ref[0:4, :] = jnp.concatenate([found[0:4, 0 : width // 2], found[4:8, 0 : width // 2]], axis=1)
        wait_for(w_scr, sems.at[0])
        wt_scr[...] = w_scr[...].T
        zero = jnp.zeros((width, HD), bf)
        for h in range(heads):
            at = slice(2 * HD * h, 2 * HD * (h + 1))
            wk_scr[:, at] = jnp.concatenate([w_scr[:, local + HD * h : local + HD * (h + 1)], zero], axis=1)
            wv_scr[:, at] = jnp.concatenate([w_scr[:, 2 * local + HD * h : 2 * local + HD * (h + 1)], zero], axis=1)

    n, _ = normalize(x_ref[...].astype(f32))
    a = (n * norm_ref[0:1, :] + norm_ref[2:3, :]).astype(bf)
    a_ref[...] = a
    token = (step ^ c_ref[0]) * rows + lax.broadcasted_iota(jnp.int32, (rows, 2 * local), 0)
    lane = lax.broadcasted_iota(jnp.int32, (rows, 2 * local), 1) % (2 * HD)
    ones = jnp.where((lane > HD) & (lane < HD + 4), 1.0, 0.0)
    bias = jnp.where((lane == HD) & (token >= c_ref[2]), NEGATIVE, ones)
    kp_ref[...] = (dot(a, wk_scr[...]) + bias).astype(bf)
    vp_ref[...] = (dot(a, wv_scr[...]) + ones).astype(bf)
    both = dot(wt_scr[...], a, NT)
    qt_ref[...] = (both[0:local] * 0.125).astype(bf)
    kt_ref[...] = both[local : 2 * local].astype(bf)
    vt_ref[...] = both[2 * local : 3 * local].astype(bf)


def project(scalars, x, w, norms, local):
    count, width = x.shape
    heads = local // HD
    rows = count // 4
    block = lambda i, c: (i ^ c[0], 0)
    turned = lambda i, c: (0, i ^ c[0])
    extra = [] if norms is None else [norms]
    spec = pltpu.PrefetchScalarGridSpec(
        num_scalar_prefetch=1,
        grid=(4,),
        in_specs=[pl.BlockSpec((rows, width), block)] + [ANY] * (len(w) + len(extra)),
        out_specs=[
            pl.BlockSpec((rows, width), lambda i, c: (i, 0)),
            pl.BlockSpec((rows, 2 * local), block),
            pl.BlockSpec((rows, 2 * local), block),
            pl.BlockSpec((local, rows), turned),
            pl.BlockSpec((local, rows), turned),
            pl.BlockSpec((local, rows), turned),
            whole((8, width)),
        ],
        scratch_shapes=[
            pltpu.VMEM((width, 3 * local), bf),
            pltpu.VMEM((8 if len(w) == 2 else 1, 16, 3 * local), bf),
            pltpu.VMEM((3 * local, width), bf),
            pltpu.VMEM((width, 2 * local), bf),
            pltpu.VMEM((width, 2 * local), bf),
            pltpu.SemaphoreType.DMA((2,)),
        ],
    )
    return pl.pallas_call(
        functools.partial(project_kernel, heads, len(w)),
        grid_spec=spec,
        out_shape=[SDS((count, width), bf), SDS((count, 2 * local), bf), SDS((count, 2 * local), bf)]
        + [SDS((local, count), bf)] * 3
        + [SDS((8, width), f32)],
        compiler_params=params(),
        cost_estimate=cost(14 * count * width * local, 24 << 20),
        name="project",
    )(scalars, x, *w, *extra)


def attend_kernel(chunk, c_ref, kp_ref, vt_ref, qt_ref, o_ref, lse_ref, s_scr):
    q = qt_ref.shape[1]
    keys = kp_ref.shape[0]
    queries = with_tail(qt_ref[...], [jnp.ones((1, q), f32)])
    top = None
    for i in range(keys // chunk):
        at = slice(i * chunk, (i + 1) * chunk)
        s = dot(kp_ref[at, :], queries)
        s_scr[at, :] = s
        here = jnp.max(s, axis=0, keepdims=True)
        top = here if top is None else jnp.maximum(top, here)
    total = None
    out = None
    for i in range(keys // chunk):
        at = slice(i * chunk, (i + 1) * chunk)
        p = jnp.exp2((s_scr[at, :] - top) * LOG2E)
        here = jnp.sum(p, axis=0, keepdims=True)
        part = dot(vt_ref[:, at], p.astype(bf))
        total = here if total is None else total + here
        out = part if out is None else out + part
    o_ref[0] = (out / total).astype(bf)
    lse_ref[0, 0] = jnp.broadcast_to(top + jnp.log(total), (8, q))


def attend(scalars, kp, vt, qt, part):
    count = kp.shape[0]
    heads = qt.shape[0] // HD
    q = count // 4
    spec = pltpu.PrefetchScalarGridSpec(
        num_scalar_prefetch=1,
        grid=(heads, 2),
        in_specs=[
            pl.BlockSpec((count, 2 * HD), lambda h, i, c: (0, h)),
            pl.BlockSpec((HD, count), lambda h, i, c: (h, 0)),
            pl.BlockSpec((HD, q), lambda h, i, c: (h, (2 * part + i) ^ c[0])),
        ],
        out_specs=[
            pl.BlockSpec((1, HD, q), lambda h, i, c: (i, h, 0)),
            pl.BlockSpec((1, 1, 8, q), lambda h, i, c: (h, i, 0, 0)),
        ],
        scratch_shapes=[pltpu.VMEM((count, q), f32)],
    )
    return pl.pallas_call(
        functools.partial(attend_kernel, min(512, count)),
        grid_spec=spec,
        out_shape=[SDS((2, heads * HD, q), bf), SDS((heads, 2, 8, q), f32)],
        compiler_params=params(),
        cost_estimate=cost(heads * 2 * count * count * 256, heads * count * 512, heads * count * count // 2),
        name=f"attend{part}",
    )(scalars, kp, vt, qt)


def out_kernel(pieces, c_ref, o_ref, other_ref, *refs):
    mine, theirs, (part_ref, w_scr, sem) = refs[:pieces], refs[pieces : 2 * pieces], refs[2 * pieces :]
    width = part_ref.shape[0]
    for k, group in enumerate((mine, theirs)):
        for copy in row_copies(group, c_ref[1], width, w_scr.at[k], slice(0, 256), sem.at[k]):
            copy.start()
    local = o_ref.shape[1]
    wait_for(w_scr.at[0], sem.at[0])
    part = dot(w_scr[0, :, 0:local], o_ref[0])
    wait_for(w_scr.at[1], sem.at[1])
    part_ref[...] = (part + dot(w_scr[1, :, 0:local], other_ref[...])).astype(bf)


def out_product(scalars, o, other, mine, theirs, width):
    local, q = other.shape
    spec = pltpu.PrefetchScalarGridSpec(
        num_scalar_prefetch=1,
        grid=(1,),
        in_specs=[whole(o.shape), whole(other.shape)] + [ANY] * (2 * len(mine)),
        out_specs=whole((width, q)),
        scratch_shapes=[pltpu.VMEM((2, width, 256), bf), pltpu.SemaphoreType.DMA((2,))],
    )
    return pl.pallas_call(
        functools.partial(out_kernel, len(mine)),
        grid_spec=spec,
        out_shape=SDS((width, q), bf),
        compiler_params=params(),
        cost_estimate=cost(4 * local * width * q, 2 << 20),
        name="out_product",
    )(scalars, o, other, *mine, *theirs)


def ffn_kernel(part, pieces, c_ref, x_ref, g_ref, own_ref, recv_ref, norm_ref, *refs):
    groups = [refs[i * pieces : (i + 1) * pieces] for i in range(4)]
    h_ref, c_out, gb_ref, e_ref, du_ref, ffn_ref, dc_ref, w_scr, sem = refs[4 * pieces :]
    rows, width = x_ref.shape
    units = e_ref.shape[2]
    for j, group in enumerate(groups):
        for copy in row_copies(group, c_ref[1], width, w_scr.at[j], slice(0, units), sem.at[j]):
            copy.start()
    h = x_ref[...].astype(f32) + (own_ref[...].astype(f32) + recv_ref[...].astype(f32)).T
    h_ref[...] = h
    n2, _ = normalize(h)
    c = (n2 * norm_ref[1:2, :] + norm_ref[3:4, :]).astype(bf)
    c_out[...] = c
    token = ((2 * part) ^ c_ref[0]) * rows + lax.broadcasted_iota(jnp.int32, (rows, 1), 0)
    gb = jnp.where(token < c_ref[3], g_ref[...].astype(f32), 0.0).astype(bf)
    gb_ref[...] = gb
    ffn = dc = None
    for k in range(2):
        wait_for(w_scr.at[2 * k], sem.at[2 * k])
        u = dot(c, w_scr[2 * k])
        wait_for(w_scr.at[2 * k + 1], sem.at[2 * k + 1])
        de = dot(gb, w_scr[2 * k + 1])
        phi = 0.5 * (1.0 + lax.erf(u * math.sqrt(0.5)))
        e = (u * phi).astype(bf)
        e_ref[k] = e
        du = (de * (phi + u * jnp.exp(-0.5 * u * u) * (1.0 / math.sqrt(2.0 * math.pi)))).astype(bf)
        du_ref[k] = du
        one, two = dot(du, w_scr[2 * k], NT), dot(e, w_scr[2 * k + 1], NT)
        dc = one if dc is None else dc + one
        ffn = two if ffn is None else ffn + two
    dc_ref[...] = dc.astype(bf)
    ffn_ref[...] = ffn.astype(bf)


def ffn(part, scalars, x, g, own, recv, norms, up, down, up_other, down_other, units):
    width, rows = own.shape
    token_block = pl.BlockSpec((rows, width), lambda i, c: ((2 * part) ^ c[0], 0))
    weights = [*up, *down, *up_other, *down_other]
    spec = pltpu.PrefetchScalarGridSpec(
        num_scalar_prefetch=1,
        grid=(1,),
        in_specs=[token_block, token_block, whole(own.shape), whole(own.shape), whole(norms.shape)] + [ANY] * len(weights),
        out_specs=[whole((rows, width))] * 3 + [whole((2, rows, units))] * 2 + [whole((rows, width))] * 2,
        scratch_shapes=[pltpu.VMEM((4, width, units), bf), pltpu.SemaphoreType.DMA((4,))],
    )
    return pl.pallas_call(
        functools.partial(ffn_kernel, part, len(up)),
        grid_spec=spec,
        out_shape=[SDS((rows, width), f32), SDS((rows, width), bf), SDS((rows, width), bf)]
        + [SDS((2, rows, units), bf)] * 2
        + [SDS((rows, width), bf)] * 2,
        compiler_params=params(),
        cost_estimate=cost(16 * rows * width * units, 16 << 20, 4 * rows * units),
        name=f"ffn{part}",
    )(scalars, x, g, own, recv, norms, *weights)


def middle_kernel(part, pieces, c_ref, h_ref, own_ref, recv_ref, g_ref, norm_ref, *refs):
    mine, theirs = refs[:pieces], refs[pieces : 2 * pieces]
    dh_ref, dhb_ref, do_ref, sum_ref, w_scr, sem = refs[2 * pieces :]
    rows, width = h_ref.shape
    local = do_ref.shape[1]
    for k, group in enumerate((mine, theirs)):
        for copy in row_copies(group, c_ref[1], width, w_scr.at[k], slice(0, 256), sem.at[k]):
            copy.start()
    n2, r2 = normalize(h_ref[...])
    dc = own_ref[...].astype(f32) + recv_ref[...].astype(f32)
    token = ((2 * part) ^ c_ref[0]) * rows + lax.broadcasted_iota(jnp.int32, (rows, 1), 0)
    g = jnp.where(token < c_ref[3], g_ref[...].astype(f32), 0.0)
    dh = g + norm_back(dc, n2, r2, norm_ref[1:2, :])
    dh_ref[...] = dh
    dhb = dh.astype(bf)
    dhb_ref[...] = dhb
    sum_ref[0:1, :] = jnp.sum(dc * n2, axis=0, keepdims=True)
    sum_ref[1:2, :] = jnp.sum(dc, axis=0, keepdims=True)
    sum_ref[2:8, :] = jnp.zeros((6, width), f32)
    for k in range(2):
        wait_for(w_scr.at[k], sem.at[k])
        do_ref[k] = dot(dhb, w_scr[k]).T[0:local].astype(bf)


def middle(part, scalars, h, own, recv, g, norms, mine, theirs, local):
    rows, width = h.shape
    spec = pltpu.PrefetchScalarGridSpec(
        num_scalar_prefetch=1,
        grid=(1,),
        in_specs=[whole(h.shape)] * 3 + [pl.BlockSpec((rows, width), lambda i, c: ((2 * part) ^ c[0], 0)), whole(norms.shape)] + [ANY] * (2 * len(mine)),
        out_specs=[whole(h.shape), whole(h.shape), whole((2, local, rows)), whole((8, width))],
        scratch_shapes=[pltpu.VMEM((2, width, 256), bf), pltpu.SemaphoreType.DMA((2,))],
    )
    return pl.pallas_call(
        functools.partial(middle_kernel, part, len(mine)),
        grid_spec=spec,
        out_shape=[SDS(h.shape, f32), SDS(h.shape, bf), SDS((2, local, rows), bf), SDS((8, width), f32)],
        compiler_params=params(),
        cost_estimate=cost(4 * rows * width * 256, 8 << 20),
        name=f"middle{part}",
    )(scalars, h, own, recv, g, norms, *mine, *theirs)


def relative_rows(scr, d, index, count, relative):
    r = count // 8
    y, s = index // 4, index % 4
    at = pl.multiple_of((d ^ (2 * s + y)) * r, r) if relative else index * r
    return scr[pl.ds(at, r), :]


def weight_grad_kernel(first, relative, k, c_ref, *refs):
    if first:
        src, (e1, e2, du1, du2, o1, o2, grad_ref, turned_ref, scr, w_scr) = refs[:6], refs[6:]
        rows, width = src[0].shape
        for j in range(3):
            for i in range(2):
                scr[:, i * rows : (i + 1) * rows] = src[2 * j + i][...].T
            for b in range(8):
                r = width // 8
                turned_ref[j, b * r : (b + 1) * r, :] = relative_rows(scr, c_ref[1], b, width, relative)
    else:
        turned_ref, e1, e2, du1, du2, o1, o2, recv_ref, grad_ref = refs
        width = turned_ref.shape[1]
        rows = turned_ref.shape[2] // 2
    units = du1.shape[2]
    local = o1.shape[-2]
    a, b = slice(0, rows), slice(rows, 2 * rows)
    o_at = (0,) if len(o1.shape) == 3 else ()
    up = dot(turned_ref[0, :, a], du1[k]) + dot(turned_ref[0, :, b], du2[k])
    down = dot(turned_ref[1, :, a], e1[k]) + dot(turned_ref[1, :, b], e2[k])
    out = dot(turned_ref[2, :, a], o1[o_at + (Ellipsis,)], NT) + dot(turned_ref[2, :, b], o2[o_at + (Ellipsis,)], NT)
    out = jnp.concatenate([out, jnp.zeros((width, 256 - local), f32)], axis=1)
    for at, value in ((slice(0, units), up), (slice(units, 2 * units), down), (slice(2 * units, 2 * units + 256), out)):
        if not first:
            value = value + recv_ref[:, at].astype(f32)
        grad_ref[:, at] = value.astype(bf)


def weight_grad_first(scalars, relative, cs, gbs, dhbs, es, dus, others):
    rows, width = cs[0].shape
    units = es[0].shape[2]
    ins = [*cs, *gbs, *dhbs, *es, *dus, *others]
    spec = pltpu.PrefetchScalarGridSpec(
        num_scalar_prefetch=1,
        grid=(1,),
        in_specs=[whole(v.shape) for v in ins],
        out_specs=[whole((width, 2 * units + 256)), whole((3, width, 2 * rows))],
        scratch_shapes=[pltpu.VMEM((width, 2 * rows), bf), pltpu.VMEM((8, 128), f32)],
    )
    return pl.pallas_call(
        functools.partial(weight_grad_kernel, True, relative, 1),
        grid_spec=spec,
        out_shape=[SDS((width, 2 * units + 256), bf), SDS((3, width, 2 * rows), bf)],
        compiler_params=params(),
        cost_estimate=cost(10 * rows * width * units, 18 << 20),
        name="weight_grad_first",
    )(scalars, *ins)


def weight_grad_second(scalars, turned, es, dus, os, recv):
    _, width, tokens = turned.shape
    units = es[0].shape[2]
    ins = [turned, *es, *dus, *os, recv]
    spec = pltpu.PrefetchScalarGridSpec(
        num_scalar_prefetch=1,
        grid=(1,),
        in_specs=[whole(v.shape) for v in ins],
        out_specs=whole((width, 2 * units + 256)),
    )
    return pl.pallas_call(
        functools.partial(weight_grad_kernel, False, False, 0),
        grid_spec=spec,
        out_shape=SDS((width, 2 * units + 256), bf),
        compiler_params=params(),
        cost_estimate=cost(5 * tokens * width * units, 18 << 20),
        name="weight_grad_second",
    )(scalars, *ins)


def attend_back_kernel(part, chunk, c_ref, kp_ref, vp_ref, kt_ref, qt_ref, o_ref, lse_ref, do_ref, *refs):
    if part == 0:
        dq_ref, dk_ref, dv_ref = refs
    else:
        dk_in, dv_in, dq_ref, out_ref, dk_ref, dv_ref = refs
    q = qt_ref.shape[1]
    keys = kp_ref.shape[0]
    step = pl.program_id(1)

    @pl.when(step == 0)
    def _():
        if part == 0:
            dk_ref[...] = jnp.zeros_like(dk_ref)
            dv_ref[...] = jnp.zeros_like(dv_ref)
        else:
            dk_ref[...] = dk_in[...]
            dv_ref[...] = dv_in[...]

    qt = qt_ref[...]
    do = do_ref[0]
    delta = jnp.sum(do.astype(f32) * o_ref[0].astype(f32), axis=0, keepdims=True)
    one = jnp.ones((1, q), f32)
    queries = with_tail(qt, [one] + [-v for v in split3(lse_ref[0, 0, 0:1])])
    grads = with_tail(do, [0.0 * one] + [-v for v in split3(delta)])
    dq = None
    for i in range(keys // chunk):
        at = slice(i * chunk, (i + 1) * chunk)
        p = jnp.exp2(dot(kp_ref[at, :], queries) * LOG2E)
        dp = dot(vp_ref[at, :], grads)
        ds = (p * dp).astype(bf)
        dv_ref[0, at, :] += dot(p.astype(bf), do, NT)
        dk_ref[0, at, :] += dot(ds, qt, NT)
        here = dot(kt_ref[:, at], ds)
        dq = here if dq is None else dq + here
    dq_ref[0] = (dq * 0.125).astype(bf)
    if part == 1:

        @pl.when(step == 1)
        def _():
            for m in range(4):
                at = pl.ds(pl.multiple_of((m ^ c_ref[0]) * q, q), q)
                out_ref[m % 2, m // 2, 0] = dk_ref[0, at, :].T.astype(bf)
                out_ref[m % 2, m // 2, 1] = dv_ref[0, at, :].T.astype(bf)


def attend_back(part, scalars, kp, vp, kt, qt, o, lse, do, sums=()):
    count = kp.shape[0]
    heads = qt.shape[0] // HD
    q = count // 4
    keyed = pl.BlockSpec((count, 2 * HD), lambda h, i, c: (0, h))
    block = pl.BlockSpec((1, HD, q), lambda h, i, c: (i, h, 0))
    total = pl.BlockSpec((1, count, HD), lambda h, i, c: (h, 0, 0))
    total_shape = SDS((heads, count, HD), f32)
    dq_shape = SDS((2, heads * HD, q), bf)
    if part == 0:
        out_specs, out_shape, scratch = [block, total, total], [dq_shape, total_shape, total_shape], []
    else:
        out_specs = [block, pl.BlockSpec((2, 2, 2, HD, q), lambda h, i, c: (0, 0, 0, h, 0))]
        out_shape = [dq_shape, SDS((2, 2, 2, heads * HD, q), bf)]
        scratch = [pltpu.VMEM((1, count, HD), f32)] * 2
    spec = pltpu.PrefetchScalarGridSpec(
        num_scalar_prefetch=1,
        grid=(heads, 2),
        in_specs=[
            keyed,
            keyed,
            pl.BlockSpec((HD, count), lambda h, i, c: (h, 0)),
            pl.BlockSpec((HD, q), lambda h, i, c: (h, (2 * part + i) ^ c[0])),
            block,
            pl.BlockSpec((1, 1, 8, q), lambda h, i, c: (h, i, 0, 0)),
            block,
        ]
        + [total] * len(sums),
        out_specs=out_specs,
        scratch_shapes=scratch,
    )
    return pl.pallas_call(
        functools.partial(attend_back_kernel, part, min(512, count)),
        grid_spec=spec,
        out_shape=out_shape,
        compiler_params=params(),
        cost_estimate=cost(heads * 5 * count * count * 256, heads * count * 2048, heads * count * count // 2),
        name=f"attend_back{part}",
    )(scalars, kp, vp, kt, qt, o, lse, do, *sums)


def da_kernel(pieces, c_ref, dq1, dq2, dkv, rq1, rq2, rkv, *refs):
    mine, theirs = refs[:pieces], refs[pieces : 2 * pieces]
    one_ref, two_ref, w_scr, d_scr, sem = refs[2 * pieces :]
    width = one_ref.shape[0]
    local = rq1.shape[0]
    for k, group in enumerate((mine, theirs)):
        for copy in row_copies(group, c_ref[1], width, w_scr.at[k], slice(0, 3 * local), sem.at[k]):
            copy.start()
    for i, out_ref in enumerate((one_ref, two_ref)):
        own, other = (dq1, dq2)[i], (rq1, rq2)[i]
        d_scr[i, 0, 0:local, :] = own[0]
        d_scr[i, 1, 0:local, :] = other[...]
        for j in range(2):
            at = slice((j + 1) * local, (j + 2) * local)
            d_scr[i, 0, at, :] = dkv[0, i, j]
            d_scr[i, 1, at, :] = rkv[i, j]
    for k in range(2):
        wait_for(w_scr.at[k], sem.at[k])
    for i, out_ref in enumerate((one_ref, two_ref)):
        out_ref[...] = (dot(w_scr[0], d_scr[i, 0]) + dot(w_scr[1], d_scr[i, 1])).astype(bf)


def da_product(scalars, dq1, dq2, dkv, rq1, rq2, rkv, mine, theirs, width):
    local, q = rq1.shape
    ins = [dq1, dq2, dkv, rq1, rq2, rkv]
    spec = pltpu.PrefetchScalarGridSpec(
        num_scalar_prefetch=1,
        grid=(1,),
        in_specs=[whole(v.shape) for v in ins] + [ANY] * (2 * len(mine)),
        out_specs=[whole((width, q))] * 2,
        scratch_shapes=[pltpu.VMEM((2, width, 3 * local), bf), pltpu.VMEM((2, 2, 3 * local, q), bf), pltpu.SemaphoreType.DMA((2,))],
    )
    return pl.pallas_call(
        functools.partial(da_kernel, len(mine)),
        grid_spec=spec,
        out_shape=[SDS((width, q), bf)] * 2,
        compiler_params=params(),
        cost_estimate=cost(24 * local * width * q, 8 << 20),
        name="da_product",
    )(scalars, *ins, *mine, *theirs)


def dx_kernel(c_ref, own_ref, recv_ref, x_ref, dh_ref, norm_ref, dx_ref, sum_ref):
    width = norm_ref.shape[1]
    da = (own_ref[...].astype(f32) + recv_ref[...].astype(f32)).T
    n1, r1 = normalize(x_ref[...].astype(f32))
    dx_ref[...] = (dh_ref[...] + norm_back(da, n1, r1, norm_ref[0:1, :])).astype(bf)
    sum_ref[0:1, :] = jnp.sum(da * n1, axis=0, keepdims=True)
    sum_ref[1:2, :] = jnp.sum(da, axis=0, keepdims=True)
    sum_ref[2:8, :] = jnp.zeros((6, width), f32)


def dx_block(part, scalars, own, recv, x, dh, norms):
    width, rows = own.shape
    spec = pltpu.PrefetchScalarGridSpec(
        num_scalar_prefetch=1,
        grid=(1,),
        in_specs=[whole(own.shape)] * 2
        + [pl.BlockSpec((rows, width), lambda i, c: ((2 * part) ^ c[0], 0)), whole(dh.shape), whole(norms.shape)],
        out_specs=[whole((rows, width)), whole((8, width))],
    )
    return pl.pallas_call(
        dx_kernel,
        grid_spec=spec,
        out_shape=[SDS((rows, width), bf), SDS((8, width), f32)],
        compiler_params=params(),
        cost_estimate=cost(20 * rows * width, 6 << 20),
        name=f"dx{part}",
    )(scalars, own, recv, x, dh, norms)


def qkv_grad_kernel(relative, c_ref, a_ref, dq1, dq2, dkv, grad_ref, g_scr):
    local, q = dq1.shape[1:]
    width = a_ref.shape[1]
    total = [None] * 3
    for m in range(4):
        a = a_ref[m * q : (m + 1) * q, :]
        parts = [(dq1, dq2)[m // 2][m % 2], dkv[m % 2, m // 2, 0], dkv[m % 2, m // 2, 1]]
        for j in range(3):
            here = dot(parts[j], a)
            total[j] = here if total[j] is None else total[j] + here
    for j in range(3):
        g_scr[:, j * local : (j + 1) * local] = total[j].T.astype(bf)
    r = width // 8
    for b in range(8):
        grad_ref[b * r : (b + 1) * r, :] = relative_rows(g_scr, c_ref[1], b, width, relative)


def qkv_grad(scalars, relative, normed, dq1, dq2, dkv):
    width = normed.shape[1]
    local = dq1.shape[1]
    ins = [normed, dq1, dq2, dkv]
    spec = pltpu.PrefetchScalarGridSpec(
        num_scalar_prefetch=1,
        grid=(1,),
        in_specs=[whole(v.shape) for v in ins],
        out_specs=whole((width, 3 * local)),
        scratch_shapes=[pltpu.VMEM((width, 3 * local), bf)],
    )
    return pl.pallas_call(
        functools.partial(qkv_grad_kernel, relative),
        grid_spec=spec,
        out_shape=SDS((width, 3 * local), bf),
        compiler_params=params(),
        cost_estimate=cost(6 * normed.shape[0] * width * local, 8 << 20),
        name="qkv_grad",
    )(scalars, *ins)


def gather_z(piece, n):
    return jnp.stack([piece] + [swap(piece, "dp", 2 * s, n) for s in (1, 2, 3)])


def scatter_rows(value, n):
    if n != 8:
        return lax.psum_scatter(value, "dp", scatter_dimension=0, tiled=True).astype(f32)
    r = value.shape[0] // 8
    keep, send = value[: 4 * r], value[4 * r :]
    half = (keep.astype(f32) + swap(send, "dp", 1, n).astype(f32)).astype(bf)
    total = half[0:r].astype(f32)
    for s in (1, 2, 3):
        total = total + swap(half[s * r : (s + 1) * r], "dp", 2 * s, n).astype(f32)
    return total


def sum_everywhere(value, n):
    value = value + core_swap(value)
    if n != 8:
        return lax.psum(value, "dp")
    value = value + swap(value, "dp", 1, n)
    return value + swap(value, "dp", 2, n) + swap(value, "dp", 4, n) + swap(value, "dp", 6, n)


def in_order(c, first, first_other, second, second_other):
    one = jnp.where(c == 0, jnp.concatenate([first, first_other]), jnp.concatenate([first_other, first]))
    two = jnp.where(c == 0, jnp.concatenate([second, second_other]), jnp.concatenate([second_other, second]))
    return jnp.concatenate([one, two])


def body(n, embeddings, cotangent, species, gene_ids, w_qkv, w_out, w_up, w_down, norm_gains, norm_shifts):
    c = lax.axis_index("tensor") % 2
    d = lax.axis_index("dp")
    relative = n == 8
    count, width = embeddings.shape
    r = width // n
    local = w_qkv.shape[2]
    units = w_up.shape[1]
    length = jnp.sum((gene_ids != 0).astype(jnp.int32))
    alive = jnp.where(species[0] == 2, 0, length)
    scalars = jnp.stack([c, d, length, alive]).astype(jnp.int32)

    qkv_own = jnp.concatenate([w_qkv[j].astype(bf) for j in range(3)], axis=1)
    norms_own = jnp.concatenate([norm_gains, norm_shifts]).astype(bf)
    out_own = jnp.pad(w_out.astype(bf).T, ((0, 0), (0, 256 - local)))
    up_own = w_up.astype(bf)
    down_own = w_down.astype(bf).T
    if relative:
        spread = lax.dynamic_update_slice(jnp.zeros((4, width), bf), norms_own, (0, d * r))
        spread = spread.reshape(4, 2, width // 2).transpose(1, 0, 2).reshape(8, width // 2)
        spread = jnp.pad(spread, ((0, 8), (0, 3 * local - width // 2)))
        first_z = gather_z(jnp.concatenate([qkv_own, spread]), n)
        w_first = [first_z, swap(first_z, "dp", 1, n)]
        norms = None
        out_own = after(out_own, first_z)
        out_z = gather_z(out_own, n)
        w_o = [out_z, swap(out_z, "dp", 1, n)]
        up_z = gather_z(after(up_own, first_z), n)
        w_u = [up_z, swap(up_z, "dp", 1, n)]
        down_z = gather_z(after(down_own, out_z), n)
        w_d = [down_z, swap(down_z, "dp", 1, n)]
    else:
        rows = lambda v: [lax.all_gather(v, "dp", axis=0, tiled=True)]
        w_first, w_o, w_u, w_d = rows(qkv_own), rows(out_own), rows(up_own), rows(down_own)
        norms = lax.all_gather(norms_own, "dp", axis=1, tiled=True)
        norms = norms.reshape(4, 2, width // 2).transpose(1, 0, 2).reshape(8, width // 2)
        norms = jnp.pad(norms, ((0, 8), (0, 3 * local - width // 2)))
    others = lambda group: [core_swap(v) for v in group]

    normed, kp, vp, kt, vt, qt, norm_rows = project(scalars, embeddings, w_first, norms, local)
    w_o2, w_u2, w_d2 = others(w_o), others(w_u), others(w_d)
    o, lse, o_other, h, cs, gbs, es, dus, ffns, dcs = ([None] * 2 for _ in range(10))
    sent = [None] * 2
    for i in range(2):
        o[i], lse[i] = attend(scalars, kp, vt, qt, i)
        o_other[i] = core_swap(o[i][1])
        sent[i] = out_product(scalars, o[i], o_other[i], w_o, w_o2, width)
    for i in range(2):
        recv = x_swap(sent[i])
        h[i], cs[i], gbs[i], es[i], dus[i], ffns[i], dcs[i] = ffn(
            i, scalars, embeddings, cotangent, sent[i], recv, norm_rows, w_u, w_d, w_u2, w_d2, units
        )
    dh, dhb, do, sums = ([None] * 2 for _ in range(4))
    for i in range(2):
        recv = x_swap(dcs[i])
        dh[i], dhb[i], do[i], sums[i] = middle(i, scalars, h[i], dcs[i], recv, cotangent, norm_rows, w_o, w_o2, local)
        do[i] = jnp.stack([do[i][0], core_swap(do[i][1])])
    dq1, dk, dv = attend_back(0, scalars, kp, vp, kt, qt, o[0], lse[0], do[0])
    grad_theirs, turned = weight_grad_first(scalars, relative, cs, gbs, dhb, es, dus, o_other)
    grad_ours = weight_grad_second(scalars, turned, es, dus, o, core_swap(grad_theirs))
    s_rest = scatter_rows(grad_ours, n)
    dq2, dkv = attend_back(1, scalars, kp, vp, kt, qt, o[1], lse[1], do[1], (dk, dv))

    ffns = [after(v, dcs[1]) for v in ffns]
    mixed = [(h[i] + (ffns[i].astype(f32) + x_swap(ffns[i]).astype(f32))).astype(bf) for i in range(2)]
    mixed = in_order(c, mixed[0], core_swap(mixed[0]), mixed[1], core_swap(mixed[1]))

    rq1, rq2, rkv = core_swap(dq1[1]), core_swap(dq2[1]), core_swap(dkv[1])
    w_first2 = others(w_first)
    da = da_product(scalars, dq1, dq2, dkv, rq1, rq2, rkv, w_first, w_first2, width)
    grad_first = qkv_grad(scalars, relative, normed, dq1, dq2, dkv)
    s_first = scatter_rows(grad_first, n)
    dx, sums1 = [None] * 2, [None] * 2
    for i in range(2):
        dx[i], sums1[i] = dx_block(i, scalars, da[i], x_swap(da[i]), embeddings, dh[i], norm_rows)
    grad_input = in_order(c, dx[0], core_swap(dx[0]), dx[1], core_swap(dx[1]))
    both = jnp.concatenate([(sums1[0] + sums1[1])[0:2], (sums[0] + sums[1])[0:2]])
    both = lax.dynamic_slice(sum_everywhere(both, n), (0, d * r), (4, r))
    s_qkv = s_first.reshape(r, 3, local).transpose(1, 0, 2)
    s_up, s_down, s_out = s_rest[:, :units], s_rest[:, units : 2 * units].T, s_rest[:, 2 * units : 2 * units + local].T
    gains = jnp.stack([both[0], both[2]])
    shifts = jnp.stack([both[1], both[3]])
    return (mixed, grad_input, s_qkv, s_out, s_up, s_down, gains, shifts, both[3])


def solution(mesh):
    return jax.shard_map(
        functools.partial(body, mesh.shape["dp"]),
        mesh=mesh,
        in_specs=(
            P("dp", None),
            P("dp", None),
            P("dp"),
            P("dp", None),
            P(None, "dp", "tensor"),
            P("tensor", "dp"),
            P("dp", "tensor"),
            P("tensor", "dp"),
            P(None, "dp"),
            P(None, "dp"),
        ),
        out_specs=(
            P("dp", None),
            P("dp", None),
            P(None, "dp", "tensor"),
            P("tensor", "dp"),
            P("dp", "tensor"),
            P("tensor", "dp"),
            P(None, "dp"),
            P(None, "dp"),
            P("dp"),
        ),
        check_vma=False,
    )
```

```python
import functools
import math

import jax
import jax.numpy as jnp
from jax import lax
from jax.experimental import pallas as pl
from jax.experimental.pallas import tpu as pltpu
from jax.sharding import PartitionSpec as P

HD = 64
EPSILON = 1e-05
NEGATIVE = -1e30
LOG2E = math.log2(math.e)
bf = jnp.bfloat16
f32 = jnp.float32
NN = ((1,), (0,))
NT = ((1,), (1,))
ANY = pl.BlockSpec(memory_space=pl.ANY)
SDS = jax.ShapeDtypeStruct


def dot(a, b, dims=NN):
    return lax.dot_general(a, b, (dims, ((), ())), preferred_element_type=f32)


def swap(value, axis, mask, size):
    return lax.ppermute(value, axis, [(i, i ^ mask) for i in range(size)])


def core_swap(value):
    return swap(value, "tensor", 1, 4)


def x_swap(value):
    return swap(value, "tensor", 2, 4)


def after(value, *others):
    return lax.optimization_barrier((value,) + others)[0]


def params(mib=48):
    return pltpu.CompilerParams(vmem_limit_bytes=mib << 20)


def cost(flops, moved, exps=0):
    return pl.CostEstimate(flops=int(flops), bytes_accessed=int(moved), transcendentals=int(exps))


def whole(shape):
    return pl.BlockSpec(shape, lambda *_: (0,) * len(shape))


def row_copies(refs, d, count, dst, columns, sem):
    copies = []
    if len(refs) == 1:
        copies.append(pltpu.make_async_copy(refs[0].at[:, columns], dst, sem))
        return copies
    r = count // 8
    for y, ref in enumerate(refs):
        for s in range(4):
            at = pl.multiple_of((d ^ (2 * s + y)) * r, r)
            copies.append(pltpu.make_async_copy(ref.at[s, 0:r, columns], dst.at[pl.ds(at, r), :], sem))
    return copies


def wait_for(dst, sem):
    pltpu.make_async_copy(dst, dst, sem).wait()


def split3(v):
    a = v.astype(bf)
    rest = v - a.astype(f32)
    b = rest.astype(bf)
    c = (rest - b.astype(f32)).astype(bf)
    return [a.astype(f32), b.astype(f32), c.astype(f32)]


def with_tail(block, rows):
    q = block.shape[1]
    index = lax.broadcasted_iota(jnp.int32, (HD, q), 0)
    tail = jnp.zeros((HD, q), f32)
    for i, row in enumerate(rows):
        tail = jnp.where(index == i, row, tail)
    return jnp.concatenate([block, tail.astype(bf)], axis=0)


def normalize(v):
    center = v - jnp.mean(v, axis=-1, keepdims=True)
    variance = jnp.mean(center * center, axis=-1, keepdims=True)
    r = lax.rsqrt(variance + EPSILON)
    return center * r, r


def norm_back(dn, n, r, gain):
    scaled = dn * gain
    return r * (scaled - jnp.mean(scaled, axis=-1, keepdims=True) - n * jnp.mean(scaled * n, axis=-1, keepdims=True))


def project_kernel(heads, pieces, c_ref, x_ref, *refs):
    w_refs = refs[:pieces]
    a_ref, kp_ref, vp_ref, kt_ref, vt_ref, qt_ref, norm_ref, w_scr, wt_scr, wk_scr, wv_scr, sem = refs[pieces:]
    step = pl.program_id(0)
    rows, width = x_ref.shape
    local = HD * heads

    @pl.when(step == 0)
    def _():
        for copy in row_copies(w_refs, c_ref[1], width, w_scr, slice(0, w_scr.shape[1]), sem):
            copy.start()
        wait_for(w_scr, sem)
        wt_scr[...] = w_scr[...].T
        norm_ref[...] = wt_scr[3 * local : 3 * local + 16, :].astype(f32)[0:8]
        zero = jnp.zeros((width, HD), bf)
        for h in range(heads):
            at = slice(2 * HD * h, 2 * HD * (h + 1))
            wk_scr[:, at] = jnp.concatenate([w_scr[:, local + HD * h : local + HD * (h + 1)], zero], axis=1)
            wv_scr[:, at] = jnp.concatenate([w_scr[:, 2 * local + HD * h : 2 * local + HD * (h + 1)], zero], axis=1)

    n, _ = normalize(x_ref[...].astype(f32))
    a = (n * norm_ref[0:1, :] + norm_ref[2:3, :]).astype(bf)
    a_ref[...] = a
    token = (step ^ c_ref[0]) * rows + lax.broadcasted_iota(jnp.int32, (rows, 2 * local), 0)
    lane = lax.broadcasted_iota(jnp.int32, (rows, 2 * local), 1) % (2 * HD)
    ones = jnp.where((lane > HD) & (lane < HD + 4), 1.0, 0.0)
    bias = jnp.where((lane == HD) & (token >= c_ref[2]), NEGATIVE, ones)
    kp_ref[...] = (dot(a, wk_scr[...]) + bias).astype(bf)
    vp_ref[...] = (dot(a, wv_scr[...]) + ones).astype(bf)
    both = dot(wt_scr[0 : 3 * local, :], a, NT)
    qt_ref[...] = (both[0:local] * 0.125).astype(bf)
    kt_ref[...] = both[local : 2 * local].astype(bf)
    vt_ref[...] = both[2 * local : 3 * local].astype(bf)


def project(scalars, x, w, local):
    count, width = x.shape
    heads = local // HD
    rows = count // 4
    packed = w[0].shape[-1]
    block = lambda i, c: (i ^ c[0], 0)
    turned = lambda i, c: (0, i ^ c[0])
    spec = pltpu.PrefetchScalarGridSpec(
        num_scalar_prefetch=1,
        grid=(4,),
        in_specs=[pl.BlockSpec((rows, width), block)] + [ANY] * len(w),
        out_specs=[
            pl.BlockSpec((rows, width), lambda i, c: (i, 0)),
            pl.BlockSpec((rows, 2 * local), block),
            pl.BlockSpec((rows, 2 * local), block),
            pl.BlockSpec((local, rows), turned),
            pl.BlockSpec((local, rows), turned),
            pl.BlockSpec((local, rows), turned),
            whole((8, width)),
        ],
        scratch_shapes=[
            pltpu.VMEM((width, packed), bf),
            pltpu.VMEM((packed, width), bf),
            pltpu.VMEM((width, 2 * local), bf),
            pltpu.VMEM((width, 2 * local), bf),
            pltpu.SemaphoreType.DMA,
        ],
    )
    return pl.pallas_call(
        functools.partial(project_kernel, heads, len(w)),
        grid_spec=spec,
        out_shape=[SDS((count, width), bf), SDS((count, 2 * local), bf), SDS((count, 2 * local), bf)]
        + [SDS((local, count), bf)] * 3
        + [SDS((8, width), f32)],
        compiler_params=params(),
        cost_estimate=cost(14 * count * width * local, 24 << 20),
        name="project",
    )(scalars, x, *w)


def attend_kernel(chunk, c_ref, kp_ref, vt_ref, qt_ref, o_ref, lse_ref, s_scr):
    q = qt_ref.shape[1]
    keys = kp_ref.shape[0]
    queries = with_tail(qt_ref[...], [jnp.ones((1, q), f32)])
    top = None
    for i in range(keys // chunk):
        at = slice(i * chunk, (i + 1) * chunk)
        s = dot(kp_ref[at, :], queries)
        s_scr[at, :] = s
        here = jnp.max(s, axis=0, keepdims=True)
        top = here if top is None else jnp.maximum(top, here)
    total = None
    out = None
    for i in range(keys // chunk):
        at = slice(i * chunk, (i + 1) * chunk)
        p = jnp.exp2((s_scr[at, :] - top) * LOG2E)
        here = jnp.sum(p, axis=0, keepdims=True)
        part = dot(vt_ref[:, at], p.astype(bf))
        total = here if total is None else total + here
        out = part if out is None else out + part
    o_ref[0] = (out / total).astype(bf)
    lse_ref[0, 0] = jnp.broadcast_to(top + jnp.log(total), (8, q))


def attend(scalars, kp, vt, qt, part):
    count = kp.shape[0]
    heads = qt.shape[0] // HD
    q = count // 4
    spec = pltpu.PrefetchScalarGridSpec(
        num_scalar_prefetch=1,
        grid=(heads, 2),
        in_specs=[
            pl.BlockSpec((count, 2 * HD), lambda h, i, c: (0, h)),
            pl.BlockSpec((HD, count), lambda h, i, c: (h, 0)),
            pl.BlockSpec((HD, q), lambda h, i, c: (h, (2 * part + i) ^ c[0])),
        ],
        out_specs=[
            pl.BlockSpec((1, HD, q), lambda h, i, c: (i, h, 0)),
            pl.BlockSpec((1, 1, 8, q), lambda h, i, c: (h, i, 0, 0)),
        ],
        scratch_shapes=[pltpu.VMEM((count, q), f32)],
    )
    return pl.pallas_call(
        functools.partial(attend_kernel, min(512, count)),
        grid_spec=spec,
        out_shape=[SDS((2, heads * HD, q), bf), SDS((heads, 2, 8, q), f32)],
        compiler_params=params(),
        cost_estimate=cost(heads * 2 * count * count * 256, heads * count * 512, heads * count * count // 2),
        name=f"attend{part}",
    )(scalars, kp, vt, qt)


def out_kernel(pieces, c_ref, o_ref, other_ref, *refs):
    mine, theirs, (part_ref, w_scr, sem) = refs[:pieces], refs[pieces : 2 * pieces], refs[2 * pieces :]
    width = part_ref.shape[0]
    for k, group in enumerate((mine, theirs)):
        for copy in row_copies(group, c_ref[1], width, w_scr.at[k], slice(0, 256), sem.at[k]):
            copy.start()
    local = o_ref.shape[1]
    wait_for(w_scr.at[0], sem.at[0])
    part = dot(w_scr[0, :, 0:local], o_ref[0])
    wait_for(w_scr.at[1], sem.at[1])
    part_ref[...] = (part + dot(w_scr[1, :, 0:local], other_ref[...])).astype(bf)


def out_product(scalars, o, other, mine, theirs, width):
    local, q = other.shape
    spec = pltpu.PrefetchScalarGridSpec(
        num_scalar_prefetch=1,
        grid=(1,),
        in_specs=[whole(o.shape), whole(other.shape)] + [ANY] * (2 * len(mine)),
        out_specs=whole((width, q)),
        scratch_shapes=[pltpu.VMEM((2, width, 256), bf), pltpu.SemaphoreType.DMA((2,))],
    )
    return pl.pallas_call(
        functools.partial(out_kernel, len(mine)),
        grid_spec=spec,
        out_shape=SDS((width, q), bf),
        compiler_params=params(),
        cost_estimate=cost(4 * local * width * q, 2 << 20),
        name="out_product",
    )(scalars, o, other, *mine, *theirs)


def ffn_kernel(part, pieces, c_ref, x_ref, g_ref, own_ref, recv_ref, norm_ref, *refs):
    groups = [refs[i * pieces : (i + 1) * pieces] for i in range(4)]
    h_ref, c_out, gb_ref, e_ref, du_ref, ffn_ref, dc_ref, w_scr, sem = refs[4 * pieces :]
    rows, width = x_ref.shape
    units = e_ref.shape[2]
    for j, group in enumerate(groups):
        for copy in row_copies(group, c_ref[1], width, w_scr.at[j], slice(0, units), sem.at[j]):
            copy.start()
    h = x_ref[...].astype(f32) + (own_ref[...].astype(f32) + recv_ref[...].astype(f32)).T
    h_ref[...] = h
    n2, _ = normalize(h)
    c = (n2 * norm_ref[1:2, :] + norm_ref[3:4, :]).astype(bf)
    c_out[...] = c
    token = ((2 * part) ^ c_ref[0]) * rows + lax.broadcasted_iota(jnp.int32, (rows, 1), 0)
    gb = jnp.where(token < c_ref[3], g_ref[...].astype(f32), 0.0).astype(bf)
    gb_ref[...] = gb
    ffn = dc = None
    for k in range(2):
        wait_for(w_scr.at[2 * k], sem.at[2 * k])
        u = dot(c, w_scr[2 * k])
        wait_for(w_scr.at[2 * k + 1], sem.at[2 * k + 1])
        de = dot(gb, w_scr[2 * k + 1])
        phi = 0.5 * (1.0 + lax.erf(u * math.sqrt(0.5)))
        e = (u * phi).astype(bf)
        e_ref[k] = e
        du = (de * (phi + u * jnp.exp(-0.5 * u * u) * (1.0 / math.sqrt(2.0 * math.pi)))).astype(bf)
        du_ref[k] = du
        one, two = dot(du, w_scr[2 * k], NT), dot(e, w_scr[2 * k + 1], NT)
        dc = one if dc is None else dc + one
        ffn = two if ffn is None else ffn + two
    dc_ref[...] = dc.astype(bf)
    ffn_ref[...] = ffn.astype(bf)


def ffn(part, scalars, x, g, own, recv, norms, up, down, up_other, down_other, units):
    width, rows = own.shape
    token_block = pl.BlockSpec((rows, width), lambda i, c: ((2 * part) ^ c[0], 0))
    weights = [*up, *down, *up_other, *down_other]
    spec = pltpu.PrefetchScalarGridSpec(
        num_scalar_prefetch=1,
        grid=(1,),
        in_specs=[token_block, token_block, whole(own.shape), whole(own.shape), whole(norms.shape)] + [ANY] * len(weights),
        out_specs=[whole((rows, width))] * 3 + [whole((2, rows, units))] * 2 + [whole((rows, width))] * 2,
        scratch_shapes=[pltpu.VMEM((4, width, units), bf), pltpu.SemaphoreType.DMA((4,))],
    )
    return pl.pallas_call(
        functools.partial(ffn_kernel, part, len(up)),
        grid_spec=spec,
        out_shape=[SDS((rows, width), f32), SDS((rows, width), bf), SDS((rows, width), bf)]
        + [SDS((2, rows, units), bf)] * 2
        + [SDS((rows, width), bf)] * 2,
        compiler_params=params(),
        cost_estimate=cost(16 * rows * width * units, 16 << 20, 4 * rows * units),
        name=f"ffn{part}",
    )(scalars, x, g, own, recv, norms, *weights)


def middle_kernel(part, pieces, c_ref, h_ref, own_ref, recv_ref, g_ref, norm_ref, *refs):
    mine, theirs = refs[:pieces], refs[pieces : 2 * pieces]
    dh_ref, dhb_ref, do_ref, sum_ref, w_scr, sem = refs[2 * pieces :]
    rows, width = h_ref.shape
    local = do_ref.shape[1]
    for k, group in enumerate((mine, theirs)):
        for copy in row_copies(group, c_ref[1], width, w_scr.at[k], slice(0, 256), sem.at[k]):
            copy.start()
    n2, r2 = normalize(h_ref[...])
    dc = own_ref[...].astype(f32) + recv_ref[...].astype(f32)
    token = ((2 * part) ^ c_ref[0]) * rows + lax.broadcasted_iota(jnp.int32, (rows, 1), 0)
    g = jnp.where(token < c_ref[3], g_ref[...].astype(f32), 0.0)
    dh = g + norm_back(dc, n2, r2, norm_ref[1:2, :])
    dh_ref[...] = dh
    dhb = dh.astype(bf)
    dhb_ref[...] = dhb
    sum_ref[...] = jnp.zeros((8, width), f32)
    sum_ref[2:3, :] = jnp.sum(dc * n2, axis=0, keepdims=True)
    sum_ref[3:4, :] = jnp.sum(dc, axis=0, keepdims=True)
    for k in range(2):
        wait_for(w_scr.at[k], sem.at[k])
        do_ref[k] = dot(dhb, w_scr[k]).T[0:local].astype(bf)


def middle(part, scalars, h, own, recv, g, norms, mine, theirs, local):
    rows, width = h.shape
    spec = pltpu.PrefetchScalarGridSpec(
        num_scalar_prefetch=1,
        grid=(1,),
        in_specs=[whole(h.shape)] * 3 + [pl.BlockSpec((rows, width), lambda i, c: ((2 * part) ^ c[0], 0)), whole(norms.shape)] + [ANY] * (2 * len(mine)),
        out_specs=[whole(h.shape), whole(h.shape), whole((2, local, rows)), whole((8, width))],
        scratch_shapes=[pltpu.VMEM((2, width, 256), bf), pltpu.SemaphoreType.DMA((2,))],
    )
    return pl.pallas_call(
        functools.partial(middle_kernel, part, len(mine)),
        grid_spec=spec,
        out_shape=[SDS(h.shape, f32), SDS(h.shape, bf), SDS((2, local, rows), bf), SDS((8, width), f32)],
        compiler_params=params(),
        cost_estimate=cost(4 * rows * width * 256, 8 << 20),
        name=f"middle{part}",
    )(scalars, h, own, recv, g, norms, *mine, *theirs)


def relative_rows(scr, d, index, count, relative):
    r = count // 8
    y, s = index // 4, index % 4
    at = pl.multiple_of((d ^ (2 * s + y)) * r, r) if relative else index * r
    return scr[pl.ds(at, r), :]


def turn(values, c_ref, scr, turned_ref, j, relative):
    rows, width = values[0].shape
    r = width // 8
    for i in range(2):
        scr[:, i * rows : (i + 1) * rows] = values[i][...].T
    for b in range(8):
        turned_ref[j, b * r : (b + 1) * r, :] = relative_rows(scr, c_ref[1], b, width, relative)


def weight_grad_kernel(first, relative, k, c_ref, *refs):
    if first:
        c1, c2, gb1, gb2, e1, e2, du1, du2, grad_ref, turned_ref, scr = refs
        turn((c1, c2), c_ref, scr, turned_ref, 0, relative)
        turn((gb1, gb2), c_ref, scr, turned_ref, 1, relative)
    else:
        turned_ref, e1, e2, du1, du2, recv_ref, grad_ref = refs
    rows, units = du1.shape[1:]
    a, b = slice(0, rows), slice(rows, 2 * rows)
    up = dot(turned_ref[0, :, a], du1[k]) + dot(turned_ref[0, :, b], du2[k])
    down = dot(turned_ref[1, :, a], e1[k]) + dot(turned_ref[1, :, b], e2[k])
    if not first:
        up = up + recv_ref[:, 0:units].astype(f32)
        down = down + recv_ref[:, units:].astype(f32)
    grad_ref[:, 0:units] = up.astype(bf)
    grad_ref[:, units:] = down.astype(bf)


def weight_grad_first(scalars, relative, cs, gbs, es, dus):
    rows, width = cs[0].shape
    units = es[0].shape[2]
    ins = [*cs, *gbs, *es, *dus]
    spec = pltpu.PrefetchScalarGridSpec(
        num_scalar_prefetch=1,
        grid=(1,),
        in_specs=[whole(v.shape) for v in ins],
        out_specs=[whole((width, 2 * units)), whole((2, width, 2 * rows))],
        scratch_shapes=[pltpu.VMEM((width, 2 * rows), bf)],
    )
    return pl.pallas_call(
        functools.partial(weight_grad_kernel, True, relative, 1),
        grid_spec=spec,
        out_shape=[SDS((width, 2 * units), bf), SDS((2, width, 2 * rows), bf)],
        compiler_params=params(),
        cost_estimate=cost(10 * rows * width * units, 18 << 20),
        name="weight_grad_first",
    )(scalars, *ins)


def weight_grad_second(scalars, turned, es, dus, recv):
    _, width, tokens = turned.shape
    units = es[0].shape[2]
    ins = [turned, *es, *dus, recv]
    spec = pltpu.PrefetchScalarGridSpec(
        num_scalar_prefetch=1,
        grid=(1,),
        in_specs=[whole(v.shape) for v in ins],
        out_specs=whole((width, 2 * units)),
    )
    return pl.pallas_call(
        functools.partial(weight_grad_kernel, False, False, 0),
        grid_spec=spec,
        out_shape=SDS((width, 2 * units), bf),
        compiler_params=params(),
        cost_estimate=cost(5 * tokens * width * units, 18 << 20),
        name="weight_grad_second",
    )(scalars, *ins)


def out_grad_kernel(relative, c_ref, dhb1, dhb2, o1, o2, other1, other2, ours_ref, theirs_ref, scr, turned):
    rows = dhb1.shape[0]
    turn((dhb1, dhb2), c_ref, scr, turned, 0, relative)
    a, b = turned[0, :, 0:rows], turned[0, :, rows : 2 * rows]
    theirs_ref[...] = (dot(a, other1[...], NT) + dot(b, other2[...], NT)).astype(bf)
    ours_ref[...] = (dot(a, o1[0], NT) + dot(b, o2[0], NT)).astype(bf)


def out_grad(scalars, relative, dhbs, os, others):
    rows, width = dhbs[0].shape
    local = others[0].shape[0]
    ins = [*dhbs, *os, *others]
    spec = pltpu.PrefetchScalarGridSpec(
        num_scalar_prefetch=1,
        grid=(1,),
        in_specs=[whole(v.shape) for v in ins],
        out_specs=[whole((width, local))] * 2,
        scratch_shapes=[pltpu.VMEM((width, 2 * rows), bf), pltpu.VMEM((1, width, 2 * rows), bf)],
    )
    return pl.pallas_call(
        functools.partial(out_grad_kernel, relative),
        grid_spec=spec,
        out_shape=[SDS((width, local), bf)] * 2,
        compiler_params=params(),
        cost_estimate=cost(8 * rows * width * local, 5 << 20),
        name="out_grad",
    )(scalars, *ins)


def attend_back_kernel(part, chunk, c_ref, kp_ref, vp_ref, kt_ref, qt_ref, o_ref, lse_ref, do_ref, *refs):
    if part == 0:
        dq_ref, dk_ref, dv_ref = refs
    else:
        dk_in, dv_in, dq_ref, out_ref, dk_ref, dv_ref = refs
    q = qt_ref.shape[1]
    keys = kp_ref.shape[0]
    step = pl.program_id(1)

    @pl.when(step == 0)
    def _():
        if part == 0:
            dk_ref[...] = jnp.zeros_like(dk_ref)
            dv_ref[...] = jnp.zeros_like(dv_ref)
        else:
            dk_ref[...] = dk_in[...]
            dv_ref[...] = dv_in[...]

    qt = qt_ref[...]
    do = do_ref[0]
    delta = jnp.sum(do.astype(f32) * o_ref[0].astype(f32), axis=0, keepdims=True)
    one = jnp.ones((1, q), f32)
    queries = with_tail(qt, [one] + [-v for v in split3(lse_ref[0, 0, 0:1])])
    grads = with_tail(do, [0.0 * one] + [-v for v in split3(delta)])
    dq = None
    for i in range(keys // chunk):
        at = slice(i * chunk, (i + 1) * chunk)
        p = jnp.exp2(dot(kp_ref[at, :], queries) * LOG2E)
        dp = dot(vp_ref[at, :], grads)
        ds = (p * dp).astype(bf)
        dv_ref[0, at, :] += dot(p.astype(bf), do, NT)
        dk_ref[0, at, :] += dot(ds, qt, NT)
        here = dot(kt_ref[:, at], ds)
        dq = here if dq is None else dq + here
    dq_ref[0] = (dq * 0.125).astype(bf)
    if part == 1:

        @pl.when(step == 1)
        def _():
            for m in range(4):
                at = pl.ds(pl.multiple_of((m ^ c_ref[0]) * q, q), q)
                out_ref[m % 2, m // 2, 0] = dk_ref[0, at, :].T.astype(bf)
                out_ref[m % 2, m // 2, 1] = dv_ref[0, at, :].T.astype(bf)


def attend_back(part, scalars, kp, vp, kt, qt, o, lse, do, sums=()):
    count = kp.shape[0]
    heads = qt.shape[0] // HD
    q = count // 4
    keyed = pl.BlockSpec((count, 2 * HD), lambda h, i, c: (0, h))
    block = pl.BlockSpec((1, HD, q), lambda h, i, c: (i, h, 0))
    total = pl.BlockSpec((1, count, HD), lambda h, i, c: (h, 0, 0))
    total_shape = SDS((heads, count, HD), f32)
    dq_shape = SDS((2, heads * HD, q), bf)
    if part == 0:
        out_specs, out_shape, scratch = [block, total, total], [dq_shape, total_shape, total_shape], []
    else:
        out_specs = [block, pl.BlockSpec((2, 2, 2, HD, q), lambda h, i, c: (0, 0, 0, h, 0))]
        out_shape = [dq_shape, SDS((2, 2, 2, heads * HD, q), bf)]
        scratch = [pltpu.VMEM((1, count, HD), f32)] * 2
    spec = pltpu.PrefetchScalarGridSpec(
        num_scalar_prefetch=1,
        grid=(heads, 2),
        in_specs=[
            keyed,
            keyed,
            pl.BlockSpec((HD, count), lambda h, i, c: (h, 0)),
            pl.BlockSpec((HD, q), lambda h, i, c: (h, (2 * part + i) ^ c[0])),
            block,
            pl.BlockSpec((1, 1, 8, q), lambda h, i, c: (h, i, 0, 0)),
            block,
        ]
        + [total] * len(sums),
        out_specs=out_specs,
        scratch_shapes=scratch,
    )
    return pl.pallas_call(
        functools.partial(attend_back_kernel, part, min(512, count)),
        grid_spec=spec,
        out_shape=out_shape,
        compiler_params=params(),
        cost_estimate=cost(heads * 5 * count * count * 256, heads * count * 2048, heads * count * count // 2),
        name=f"attend_back{part}",
    )(scalars, kp, vp, kt, qt, o, lse, do, *sums)


def da_kernel(pieces, c_ref, dq1, dq2, dkv, rq1, rq2, rkv, x1_ref, x2_ref, *refs):
    mine, theirs = refs[:pieces], refs[pieces : 2 * pieces]
    one_ref, two_ref, sum_ref, w_scr, d_scr, sem = refs[2 * pieces :]
    width = one_ref.shape[0]
    local = rq1.shape[0]
    for k, group in enumerate((mine, theirs)):
        for copy in row_copies(group, c_ref[1], width, w_scr.at[k], slice(0, w_scr.shape[2]), sem.at[k]):
            copy.start()
    for i in range(2):
        own, other = (dq1, dq2)[i], (rq1, rq2)[i]
        d_scr[i, 0, 0:local, :] = own[0]
        d_scr[i, 1, 0:local, :] = other[...]
        for j in range(2):
            at = slice((j + 1) * local, (j + 2) * local)
            d_scr[i, 0, at, :] = dkv[0, i, j]
            d_scr[i, 1, at, :] = rkv[i, j]
    for k in range(2):
        wait_for(w_scr.at[k], sem.at[k])
    sums = [jnp.zeros((1, width), f32)] * 2
    at = slice(0, 3 * local)
    for i, (da_ref, x_ref) in enumerate(((one_ref, x1_ref), (two_ref, x2_ref))):
        da = (dot(w_scr[0, :, at], d_scr[i, 0]) + dot(w_scr[1, :, at], d_scr[i, 1])).astype(bf)
        da_ref[...] = da
        n1, _ = normalize(x_ref[...].astype(f32))
        da = da.astype(f32).T
        sums = [sums[0] + jnp.sum(da * n1, axis=0, keepdims=True), sums[1] + jnp.sum(da, axis=0, keepdims=True)]
    sum_ref[0:1, :], sum_ref[1:2, :] = sums
    sum_ref[2:8, :] = jnp.zeros((6, width), f32)


def da_product(scalars, dq1, dq2, dkv, rq1, rq2, rkv, x, mine, theirs):
    local, q = rq1.shape
    width = x.shape[1]
    packed = mine[0].shape[-1]
    ins = [dq1, dq2, dkv, rq1, rq2, rkv]
    spec = pltpu.PrefetchScalarGridSpec(
        num_scalar_prefetch=1,
        grid=(1,),
        in_specs=[whole(v.shape) for v in ins]
        + [pl.BlockSpec((q, width), lambda i, c: (c[0], 0)), pl.BlockSpec((q, width), lambda i, c: (2 ^ c[0], 0))]
        + [ANY] * (2 * len(mine)),
        out_specs=[whole((width, q))] * 2 + [whole((8, width))],
        scratch_shapes=[pltpu.VMEM((2, width, packed), bf), pltpu.VMEM((2, 2, 3 * local, q), bf), pltpu.SemaphoreType.DMA((2,))],
    )
    return pl.pallas_call(
        functools.partial(da_kernel, len(mine)),
        grid_spec=spec,
        out_shape=[SDS((width, q), bf)] * 2 + [SDS((8, width), f32)],
        compiler_params=params(),
        cost_estimate=cost(24 * local * width * q, 8 << 20),
        name="da_product",
    )(scalars, *ins, x, x, *mine, *theirs)


def dx_kernel(c_ref, own_ref, recv_ref, x_ref, dh_ref, norm_ref, dx_ref):
    da = (own_ref[...].astype(f32) + recv_ref[...].astype(f32)).T
    n1, r1 = normalize(x_ref[...].astype(f32))
    dx_ref[...] = (dh_ref[...] + norm_back(da, n1, r1, norm_ref[0:1, :])).astype(bf)


def dx_block(part, scalars, own, recv, x, dh, norms):
    width, rows = own.shape
    spec = pltpu.PrefetchScalarGridSpec(
        num_scalar_prefetch=1,
        grid=(1,),
        in_specs=[whole(own.shape)] * 2
        + [pl.BlockSpec((rows, width), lambda i, c: ((2 * part) ^ c[0], 0)), whole(dh.shape), whole(norms.shape)],
        out_specs=whole((rows, width)),
    )
    return pl.pallas_call(
        dx_kernel,
        grid_spec=spec,
        out_shape=SDS((rows, width), bf),
        compiler_params=params(),
        cost_estimate=cost(20 * rows * width, 6 << 20),
        name=f"dx{part}",
    )(scalars, own, recv, x, dh, norms)


def qkv_grad_kernel(relative, c_ref, a_ref, dq1, dq2, dkv, out1, out2, sum_ref, grad_ref, g_scr):
    local, q = dq1.shape[1:]
    width = a_ref.shape[1]
    total = [None] * 3
    for m in range(4):
        a = a_ref[m * q : (m + 1) * q, :]
        parts = [(dq1, dq2)[m // 2][m % 2], dkv[m % 2, m // 2, 0], dkv[m % 2, m // 2, 1]]
        for j in range(3):
            here = dot(parts[j], a)
            total[j] = here if total[j] is None else total[j] + here
    for j in range(3):
        g_scr[:, j * local : (j + 1) * local] = total[j].T.astype(bf)
    tall = jnp.concatenate([sum_ref[...], jnp.zeros((120, width), f32)], axis=0)
    g_scr[:, 4 * local : 4 * local + 128] = tall.T.astype(bf)
    r = width // 8
    for b in range(8):
        rows = relative_rows(g_scr, c_ref[1], b, width, relative)
        grad_ref[b * r : (b + 1) * r, local : 4 * local] = rows[:, 0 : 3 * local]
        grad_ref[b * r : (b + 1) * r, 4 * local :] = rows[:, 4 * local :]
    grad_ref[:, 0:local] = (out1[...].astype(f32) + out2[...].astype(f32)).astype(bf)


def qkv_grad(scalars, relative, normed, dq1, dq2, dkv, out1, out2, sums):
    width = normed.shape[1]
    local = dq1.shape[1]
    ins = [normed, dq1, dq2, dkv, out1, out2, sums]
    spec = pltpu.PrefetchScalarGridSpec(
        num_scalar_prefetch=1,
        grid=(1,),
        in_specs=[whole(v.shape) for v in ins],
        out_specs=whole((width, 4 * local + 128)),
        scratch_shapes=[pltpu.VMEM((width, 4 * local + 128), bf)],
    )
    return pl.pallas_call(
        functools.partial(qkv_grad_kernel, relative),
        grid_spec=spec,
        out_shape=SDS((width, 4 * local + 128), bf),
        compiler_params=params(),
        cost_estimate=cost(6 * normed.shape[0] * width * local, 8 << 20),
        name="qkv_grad",
    )(scalars, *ins)


def gather_z(piece, n):
    return [piece] + [swap(piece, "dp", 2 * s, n) for s in (1, 2, 3)]


def gather_y(pieces, n):
    along_z = jnp.stack(pieces)
    return [along_z, swap(along_z, "dp", 1, n)]


def scatter_y(value, n):
    if n != 8:
        return value
    half = value.shape[0] // 2
    return (value[:half].astype(f32) + swap(value[half:], "dp", 1, n).astype(f32)).astype(bf)


def scatter_z(half, n):
    if n != 8:
        return lax.psum_scatter(half, "dp", scatter_dimension=0, tiled=True).astype(f32)
    r = half.shape[0] // 4
    total = half[0:r].astype(f32)
    for s in (1, 2, 3):
        total = total + swap(half[s * r : (s + 1) * r], "dp", 2 * s, n).astype(f32)
    return total


def in_order(c, first, first_other, second, second_other):
    one = jnp.where(c == 0, jnp.concatenate([first, first_other]), jnp.concatenate([first_other, first]))
    two = jnp.where(c == 0, jnp.concatenate([second, second_other]), jnp.concatenate([second_other, second]))
    return jnp.concatenate([one, two])


def body(n, embeddings, cotangent, species, gene_ids, w_qkv, w_out, w_up, w_down, norm_gains, norm_shifts):
    c = lax.axis_index("tensor") % 2
    d = lax.axis_index("dp")
    relative = n == 8
    count, width = embeddings.shape
    r = width // n
    local = w_qkv.shape[2]
    units = w_up.shape[1]
    length = jnp.sum((gene_ids != 0).astype(jnp.int32))
    alive = jnp.where(species[0] == 2, 0, length)
    scalars = jnp.stack([c, d, length, alive]).astype(jnp.int32)

    norms_own = jnp.concatenate([norm_gains, norm_shifts]).T
    packed = jnp.concatenate([w_qkv[0], w_qkv[1], w_qkv[2], jnp.pad(norms_own, ((0, 0), (0, 60)))], axis=1).astype(bf)
    pad = ((0, 0), (0, 256 - local))
    if relative:
        w_first = gather_y(gather_z(packed, n), n)
        w_out, w_up = after((w_out, w_up), w_first[0])
        out_up_z = gather_z(jnp.concatenate([jnp.pad(w_out.T, pad), w_up], axis=1).astype(bf), n)
        down_z = gather_z(after(w_down, w_first[1]).astype(bf).T, n)
    else:
        rows = lambda v: [lax.all_gather(v.astype(bf), "dp", axis=0, tiled=True)]
        w_first, w_o, w_u, w_d = rows(packed), rows(jnp.pad(w_out.T, pad)), rows(w_up), rows(w_down.T)
    others = lambda group: [core_swap(v) for v in group]

    normed, kp, vp, kt, vt, qt, norm_rows = project(scalars, embeddings, w_first, local)
    if relative:
        out_up_z = after(out_up_z, norm_rows)
        w_o = gather_y([v[:, :256] for v in out_up_z], n)
        w_u = gather_y([v[:, 256:] for v in out_up_z], n)
    o, lse, o_other, h, cs, gbs, es, dus, ffns, dcs = ([None] * 2 for _ in range(10))
    sent = [None] * 2
    o[0], lse[0] = attend(scalars, kp, vt, qt, 0)
    o_other[0] = core_swap(o[0][1])
    w_o2 = others(after(w_o, lse[0]))
    sent[0] = out_product(scalars, o[0], o_other[0], w_o, w_o2, width)
    if relative:
        w_d = gather_y(after(down_z, sent[0]), n)
    o[1], lse[1] = attend(after(scalars, sent[0]), kp, vt, qt, 1)
    o_other[1] = core_swap(o[1][1])
    w_u, w_d = after((w_u, w_d), lse[1])
    w_u2, w_d2 = others(w_u), others(w_d)
    sent[1] = out_product(scalars, o[1], o_other[1], w_o, w_o2, width)
    last = after(scalars, sent[1])
    for i in range(2):
        recv = x_swap(sent[i])
        h[i], cs[i], gbs[i], es[i], dus[i], ffns[i], dcs[i] = ffn(
            i, last, embeddings, cotangent, sent[i], recv, norm_rows, w_u, w_d, w_u2, w_d2, units
        )
        last = after(scalars, dcs[i])
    dh, dhb, do, sums = ([None] * 2 for _ in range(4))
    i = 0
    dh[i], dhb[i], do[i], sums[i] = middle(i, last, h[i], dcs[i], x_swap(dcs[i]), cotangent, norm_rows, w_o, w_o2, local)
    recv_ffn = [x_swap(v) for v in after(ffns, do[0])]
    do[i] = jnp.stack([do[i][0], core_swap(do[i][1])])
    last = after(scalars, dhb[0])
    grad_theirs, turned = weight_grad_first(last, relative, cs, gbs, es, dus)
    last = after(scalars, turned)
    dq1, dk, dv = attend_back(0, last, kp, vp, kt, qt, o[0], lse[0], do[0])
    last = after(scalars, dq1)
    grad_ours = weight_grad_second(last, turned, es, dus, core_swap(grad_theirs))
    last = after(scalars, grad_ours, recv_ffn[0])
    i = 1
    dh[i], dhb[i], do[i], sums[i] = middle(i, last, h[i], dcs[i], x_swap(dcs[i]), cotangent, norm_rows, w_o, w_o2, local)
    do[i] = jnp.stack([do[i][0], core_swap(do[i][1])])
    last = after(scalars, dhb[1])
    out_ours, out_theirs = out_grad(last, relative, dhb, o, o_other)
    last = after(scalars, out_ours)
    dq2, dkv = attend_back(1, last, kp, vp, kt, qt, o[1], lse[1], do[1], (dk, dv))
    half_ours = scatter_y(grad_ours, n)

    rq1, rq2, rkv = core_swap(dq1[1]), core_swap(dq2[1]), core_swap(dkv[1])
    w_first2 = others(w_first)
    last = after(scalars, half_ours, recv_ffn[1])
    s_rest = scatter_z(half_ours, n)
    da0, da1, sums1 = da_product(last, dq1, dq2, dkv, rq1, rq2, rkv, embeddings, w_first, w_first2)
    recv_da = [x_swap(da0), x_swap(da1)]
    both = sums1 + 0.5 * (sums[0] + sums[1])
    both = both + core_swap(both)
    both = both + x_swap(both)
    grad_first = qkv_grad(scalars, relative, normed, dq1, dq2, dkv, out_ours, core_swap(out_theirs), both)
    half_first = scatter_y(grad_first, n)
    last = after(scalars, grad_first)
    dx0 = dx_block(0, last, da0, recv_da[0], embeddings, dh[0], norm_rows)

    ffns, recv_ffn = after((ffns, recv_ffn), dx0)
    mixed = [(h[i] + (ffns[i].astype(f32) + recv_ffn[i].astype(f32))).astype(bf) for i in range(2)]
    mixed = in_order(c, mixed[0], core_swap(mixed[0]), mixed[1], core_swap(mixed[1]))
    last = after(scalars, s_rest, half_first)
    s_first = scatter_z(half_first, n)
    dx1 = dx_block(1, last, da1, recv_da[1], embeddings, dh[1], norm_rows)
    grad_input = in_order(c, dx0, core_swap(dx0), dx1, core_swap(dx1))
    s_up, s_down = s_rest[:, :units], s_rest[:, units:].T
    s_out = s_first[:, :local].T
    s_qkv = s_first[:, local : 4 * local].reshape(r, 3, local).transpose(1, 0, 2)
    both = s_first[:, 4 * local : 4 * local + 4].T
    gains = jnp.stack([both[0], both[2]])
    shifts = jnp.stack([both[1], both[3]])
    return (mixed, grad_input, s_qkv, s_out, s_up, s_down, gains, shifts, both[3])


def solution(mesh):
    return jax.shard_map(
        functools.partial(body, mesh.shape["dp"]),
        mesh=mesh,
        in_specs=(
            P("dp", None),
            P("dp", None),
            P("dp"),
            P("dp", None),
            P(None, "dp", "tensor"),
            P("tensor", "dp"),
            P("dp", "tensor"),
            P("tensor", "dp"),
            P(None, "dp"),
            P(None, "dp"),
        ),
        out_specs=(
            P("dp", None),
            P("dp", None),
            P(None, "dp", "tensor"),
            P("tensor", "dp"),
            P("dp", "tensor"),
            P("tensor", "dp"),
            P(None, "dp"),
            P(None, "dp"),
            P("dp"),
        ),
        check_vma=False,
    )
```

```python
import functools
import math

import jax
import jax.numpy as jnp
from jax import lax
from jax.experimental import pallas as pl
from jax.experimental.pallas import tpu as pltpu
from jax.sharding import PartitionSpec as P

HD = 64
EPSILON = 1e-05
NEGATIVE = -1e30
LOG2E = math.log2(math.e)
bf = jnp.bfloat16
f32 = jnp.float32
NN = ((1,), (0,))
NT = ((1,), (1,))
ANY = pl.BlockSpec(memory_space=pltpu.HBM)
SDS = jax.ShapeDtypeStruct


def dot(a, b, dims=NN):
    return lax.dot_general(a, b, (dims, ((), ())), preferred_element_type=f32)


def swap(value, axis, mask, size):
    return lax.ppermute(value, axis, [(i, i ^ mask) for i in range(size)])


def core_swap(value):
    return swap(value, "tensor", 1, 4)


def x_swap(value):
    return swap(value, "tensor", 2, 4)


def in_hbm(value):
    return pltpu.with_memory_space_constraint(value, pltpu.HBM)


def after(value, *others):
    return lax.optimization_barrier((value,) + others)[0]


def params(mib=32):
    return pltpu.CompilerParams(vmem_limit_bytes=mib << 20)


SCALE = 0.1


def cost(us):
    return pl.CostEstimate(flops=int(us * SCALE * 1.15e9), bytes_accessed=int(us * SCALE * 1e6), transcendentals=0)


def whole(shape):
    return pl.BlockSpec(shape, lambda *_: (0,) * len(shape))


def row_copies(refs, d, count, dst, columns, sem):
    copies = []
    if len(refs) == 1:
        copies.append(pltpu.make_async_copy(refs[0].at[:, columns], dst, sem))
        return copies
    r = count // 8
    for y, ref in enumerate(refs):
        for s in range(4):
            at = pl.multiple_of((d ^ (2 * s + y)) * r, r)
            copies.append(pltpu.make_async_copy(ref.at[s, 0:r, columns], dst.at[pl.ds(at, r), :], sem))
    return copies


def wait_for(dst, sem):
    pltpu.make_async_copy(dst, dst, sem).wait()


def split3(v):
    a = v.astype(bf)
    rest = v - a.astype(f32)
    b = rest.astype(bf)
    c = (rest - b.astype(f32)).astype(bf)
    return [a.astype(f32), b.astype(f32), c.astype(f32)]


def with_tail(block, rows):
    q = block.shape[1]
    index = lax.broadcasted_iota(jnp.int32, (HD, q), 0)
    tail = jnp.zeros((HD, q), f32)
    for i, row in enumerate(rows):
        tail = jnp.where(index == i, row, tail)
    return jnp.concatenate([block, tail.astype(bf)], axis=0)


def normalize(v):
    center = v - jnp.mean(v, axis=-1, keepdims=True)
    variance = jnp.mean(center * center, axis=-1, keepdims=True)
    r = lax.rsqrt(variance + EPSILON)
    return center * r, r


def norm_back(dn, n, r, gain):
    scaled = dn * gain
    return r * (scaled - jnp.mean(scaled, axis=-1, keepdims=True) - n * jnp.mean(scaled * n, axis=-1, keepdims=True))


def project_kernel(heads, pieces, c_ref, x_ref, *refs):
    w_refs = refs[:pieces]
    a_ref, kp_ref, vp_ref, kt_ref, vt_ref, qt_ref, norm_ref, w_scr, wt_scr, wk_scr, wv_scr, sem = refs[pieces:]
    step = pl.program_id(0)
    rows, width = x_ref.shape
    local = HD * heads

    @pl.when(step == 0)
    def _():
        for copy in row_copies(w_refs, c_ref[1], width, w_scr, slice(0, w_scr.shape[1]), sem):
            copy.start()
        wait_for(w_scr, sem)
        wt_scr[...] = w_scr[...].T
        norm_ref[...] = wt_scr[3 * local : 3 * local + 16, :].astype(f32)[0:8]
        zero = jnp.zeros((width, HD), bf)
        for h in range(heads):
            at = slice(2 * HD * h, 2 * HD * (h + 1))
            wk_scr[:, at] = jnp.concatenate([w_scr[:, local + HD * h : local + HD * (h + 1)], zero], axis=1)
            wv_scr[:, at] = jnp.concatenate([w_scr[:, 2 * local + HD * h : 2 * local + HD * (h + 1)], zero], axis=1)

    n, _ = normalize(x_ref[...].astype(f32))
    a = (n * norm_ref[0:1, :] + norm_ref[2:3, :]).astype(bf)
    a_ref[...] = a
    token = (step ^ c_ref[0]) * rows + lax.broadcasted_iota(jnp.int32, (rows, 2 * local), 0)
    lane = lax.broadcasted_iota(jnp.int32, (rows, 2 * local), 1) % (2 * HD)
    ones = jnp.where((lane > HD) & (lane < HD + 4), 1.0, 0.0)
    bias = jnp.where((lane == HD) & (token >= c_ref[2]), NEGATIVE, ones)
    kp_ref[...] = (dot(a, wk_scr[...]) + bias).astype(bf)
    vp_ref[...] = (dot(a, wv_scr[...]) + ones).astype(bf)
    both = dot(wt_scr[0 : 3 * local, :], a, NT)
    qt_ref[...] = (both[0:local] * 0.125).astype(bf)
    kt_ref[...] = both[local : 2 * local].astype(bf)
    vt_ref[...] = both[2 * local : 3 * local].astype(bf)


def project(scalars, x, w, local):
    count, width = x.shape
    heads = local // HD
    rows = count // 4
    packed = w[0].shape[-1]
    block = lambda i, c: (i ^ c[0], 0)
    turned = lambda i, c: (0, i ^ c[0])
    spec = pltpu.PrefetchScalarGridSpec(
        num_scalar_prefetch=1,
        grid=(4,),
        in_specs=[pl.BlockSpec((rows, width), block)] + [ANY] * len(w),
        out_specs=[
            pl.BlockSpec((rows, width), lambda i, c: (i, 0)),
            pl.BlockSpec((rows, 2 * local), block),
            pl.BlockSpec((rows, 2 * local), block),
            pl.BlockSpec((local, rows), turned),
            pl.BlockSpec((local, rows), turned),
            pl.BlockSpec((local, rows), turned),
            whole((8, width)),
        ],
        scratch_shapes=[
            pltpu.VMEM((width, packed), bf),
            pltpu.VMEM((packed, width), bf),
            pltpu.VMEM((width, 2 * local), bf),
            pltpu.VMEM((width, 2 * local), bf),
            pltpu.SemaphoreType.DMA,
        ],
    )
    return pl.pallas_call(
        functools.partial(project_kernel, heads, len(w)),
        grid_spec=spec,
        out_shape=[SDS((count, width), bf), SDS((count, 2 * local), bf), SDS((count, 2 * local), bf)]
        + [SDS((local, count), bf)] * 3
        + [SDS((8, width), f32)],
        compiler_params=params(),
        cost_estimate=cost(10),
        name="project",
    )(scalars, x, *w)


def attend_kernel(chunk, c_ref, kp_ref, kp_next, vt_ref, q1_ref, q2_ref, q1_next, o_ref, lse_ref, a_scr, b_scr, top_scr):
    keys = kp_ref.shape[0]
    q = q1_ref.shape[1]
    spans = [slice(i * chunk, (i + 1) * chunk) for i in range(keys // chunk)]
    one = [jnp.ones((1, q), f32)]

    def scores(k_ref, queries, at, scr, top):
        s = dot(k_ref[at, :], queries)
        scr[at, :] = s
        here = jnp.max(s, axis=0, keepdims=True)
        return here if top is None else jnp.maximum(top, here)

    @pl.when(pl.program_id(0) == 0)
    def _():
        queries = with_tail(q1_ref[...], one)
        top = None
        for at in spans:
            top = scores(kp_ref, queries, at, a_scr, top)
        top_scr[...] = jnp.broadcast_to(top, (8, q))

    before = top_scr[0:1, :]
    turns = ((0, a_scr, b_scr, kp_ref, q2_ref), (1, b_scr, a_scr, kp_next, q1_next))
    for i, ready, filling, k_ref, q_ref in turns:
        queries = with_tail(q_ref[...], one)
        top = total = out = None
        for at in spans:
            top = scores(k_ref, queries, at, filling, top)
            p = jnp.exp2((ready[at, :] - before) * LOG2E)
            here = jnp.sum(p, axis=0, keepdims=True)
            part = dot(vt_ref[:, at], p.astype(bf))
            total = here if total is None else total + here
            out = part if out is None else out + part
        o_ref[i] = (out / total).astype(bf)
        lse_ref[0, i] = jnp.broadcast_to(before + jnp.log(total), (8, q))
        before = top
    top_scr[...] = jnp.broadcast_to(before, (8, q))


def attend(scalars, kp, vt, qt, part):
    count = kp.shape[0]
    heads = qt.shape[0] // HD
    q = count // 4
    follow = lambda h: jnp.minimum(h + 1, heads - 1)
    spec = pltpu.PrefetchScalarGridSpec(
        num_scalar_prefetch=1,
        grid=(heads,),
        in_specs=[
            pl.BlockSpec((count, 2 * HD), lambda h, c: (0, h)),
            pl.BlockSpec((count, 2 * HD), lambda h, c: (0, follow(h))),
            pl.BlockSpec((HD, count), lambda h, c: (h, 0)),
            pl.BlockSpec((HD, q), lambda h, c: (h, (2 * part) ^ c[0])),
            pl.BlockSpec((HD, q), lambda h, c: (h, (2 * part + 1) ^ c[0])),
            pl.BlockSpec((HD, q), lambda h, c: (follow(h), (2 * part) ^ c[0])),
        ],
        out_specs=[
            pl.BlockSpec((2, HD, q), lambda h, c: (0, h, 0)),
            pl.BlockSpec((1, 2, 8, q), lambda h, c: (h, 0, 0, 0)),
        ],
        scratch_shapes=[pltpu.VMEM((count, q), f32), pltpu.VMEM((count, q), f32), pltpu.VMEM((8, q), f32)],
    )
    return pl.pallas_call(
        functools.partial(attend_kernel, min(512, count)),
        grid_spec=spec,
        out_shape=[SDS((2, heads * HD, q), bf), SDS((heads, 2, 8, q), f32)],
        compiler_params=params(),
        cost_estimate=cost(10),
        name=f"attend{part}",
    )(scalars, kp, kp, vt, qt, qt, qt)


def out_kernel(pieces, c_ref, o_ref, other_ref, *refs):
    mine, theirs, (part_ref, w_scr, sem) = refs[:pieces], refs[pieces : 2 * pieces], refs[2 * pieces :]
    width = part_ref.shape[0]
    for k, group in enumerate((mine, theirs)):
        for copy in row_copies(group, c_ref[1], width, w_scr.at[k], slice(0, 256), sem.at[k]):
            copy.start()
    local = o_ref.shape[1]
    wait_for(w_scr.at[0], sem.at[0])
    part = dot(w_scr[0, :, 0:local], o_ref[0])
    wait_for(w_scr.at[1], sem.at[1])
    part_ref[...] = (part + dot(w_scr[1, :, 0:local], other_ref[...])).astype(bf)


def out_product(scalars, o, other, mine, theirs, width):
    local, q = other.shape
    spec = pltpu.PrefetchScalarGridSpec(
        num_scalar_prefetch=1,
        grid=(1,),
        in_specs=[whole(o.shape), whole(other.shape)] + [ANY] * (2 * len(mine)),
        out_specs=whole((width, q)),
        scratch_shapes=[pltpu.VMEM((2, width, 256), bf), pltpu.SemaphoreType.DMA((2,))],
    )
    return pl.pallas_call(
        functools.partial(out_kernel, len(mine)),
        grid_spec=spec,
        out_shape=SDS((width, q), bf),
        compiler_params=params(),
        cost_estimate=cost(2.2),
        name="out_product",
    )(scalars, o, other, *mine, *theirs)


def ffn_kernel(part, pieces, steps, c_ref, x_ref, g_ref, own_ref, recv_ref, norm_ref, *refs):
    groups = [refs[i * pieces : (i + 1) * pieces] for i in range(4)]
    h_ref, c_out, gb_ref, e_ref, du_ref, ffn_ref, dc_ref, w_scr, sem = refs[4 * pieces :]
    step = pl.program_id(0)
    rows, width = x_ref.shape
    units = e_ref.shape[2]

    @pl.when(step == 0)
    def _():
        for j, group in enumerate(groups):
            for copy in row_copies(group, c_ref[1], width, w_scr.at[j], slice(0, units), sem.at[j]):
                copy.start()

    h = x_ref[...].astype(f32) + (own_ref[...].astype(f32) + recv_ref[...].astype(f32)).T
    h_ref[...] = h
    n2, _ = normalize(h)
    c = (n2 * norm_ref[1:2, :] + norm_ref[3:4, :]).astype(bf)
    c_out[...] = c
    token = (((2 * part) ^ c_ref[0]) * steps + step) * rows + lax.broadcasted_iota(jnp.int32, (rows, 1), 0)
    gb = jnp.where(token < c_ref[3], g_ref[...].astype(f32), 0.0).astype(bf)
    gb_ref[...] = gb

    @pl.when(step == 0)
    def _():
        for j in range(4):
            wait_for(w_scr.at[j], sem.at[j])

    u = [dot(c, w_scr[2 * k]) for k in range(2)]
    de = [dot(gb, w_scr[2 * k + 1]) for k in range(2)]
    ffn = dc = None
    for k in range(2):
        phi = 0.5 * (1.0 + lax.erf(u[k] * math.sqrt(0.5)))
        e = (u[k] * phi).astype(bf)
        e_ref[k] = e
        du = (de[k] * (phi + u[k] * jnp.exp(-0.5 * u[k] * u[k]) * (1.0 / math.sqrt(2.0 * math.pi)))).astype(bf)
        du_ref[k] = du
        one, two = dot(du, w_scr[2 * k], NT), dot(e, w_scr[2 * k + 1], NT)
        dc = one if dc is None else dc + one
        ffn = two if ffn is None else ffn + two
    dc_ref[...] = dc.astype(bf)
    ffn_ref[...] = ffn.astype(bf)


def ffn(part, scalars, x, g, own, recv, norms, up, down, up_other, down_other, units, steps=2):
    width, count = own.shape
    rows = count // steps
    token_block = pl.BlockSpec((rows, width), lambda i, c: (((2 * part) ^ c[0]) * steps + i, 0))
    turned = pl.BlockSpec((width, rows), lambda i, c: (0, i))
    block = pl.BlockSpec((rows, width), lambda i, c: (i, 0))
    unit_block = pl.BlockSpec((2, rows, units), lambda i, c: (0, i, 0))
    weights = [*up, *down, *up_other, *down_other]
    spec = pltpu.PrefetchScalarGridSpec(
        num_scalar_prefetch=1,
        grid=(steps,),
        in_specs=[token_block, token_block, turned, turned, whole(norms.shape)] + [ANY] * len(weights),
        out_specs=[block, block, block, unit_block, unit_block, block, block],
        scratch_shapes=[pltpu.VMEM((4, width, units), bf), pltpu.SemaphoreType.DMA((4,))],
    )
    return pl.pallas_call(
        functools.partial(ffn_kernel, part, len(up), steps),
        grid_spec=spec,
        out_shape=[SDS((count, width), f32), SDS((count, width), bf), SDS((count, width), bf)]
        + [SDS((2, count, units), bf)] * 2
        + [SDS((count, width), bf)] * 2,
        compiler_params=params(),
        cost_estimate=cost(10),
        name=f"ffn{part}",
    )(scalars, x, g, own, recv, norms, *weights)


def middle_kernel(part, pieces, steps, c_ref, h_ref, own_ref, recv_ref, g_ref, norm_ref, *refs):
    mine, theirs = refs[:pieces], refs[pieces : 2 * pieces]
    dh_ref, dhb_ref, do_ref, sum_ref, w_scr, sem = refs[2 * pieces :]
    step = pl.program_id(0)
    rows, width = h_ref.shape
    local = do_ref.shape[1]

    @pl.when(step == 0)
    def _():
        sum_ref[...] = jnp.zeros((8, width), f32)
        for k, group in enumerate((mine, theirs)):
            for copy in row_copies(group, c_ref[1], width, w_scr.at[k], slice(0, 256), sem.at[k]):
                copy.start()

    n2, r2 = normalize(h_ref[...])
    dc = own_ref[...].astype(f32) + recv_ref[...].astype(f32)
    token = (((2 * part) ^ c_ref[0]) * steps + step) * rows + lax.broadcasted_iota(jnp.int32, (rows, 1), 0)
    g = jnp.where(token < c_ref[3], g_ref[...].astype(f32), 0.0)
    dh = g + norm_back(dc, n2, r2, norm_ref[1:2, :])
    dh_ref[...] = dh
    dhb = dh.astype(bf)
    dhb_ref[...] = dhb
    sum_ref[2:3, :] += jnp.sum(dc * n2, axis=0, keepdims=True)
    sum_ref[3:4, :] += jnp.sum(dc, axis=0, keepdims=True)

    @pl.when(step == 0)
    def _():
        for k in range(2):
            wait_for(w_scr.at[k], sem.at[k])

    for k in range(2):
        do_ref[k] = dot(dhb, w_scr[k]).T[0:local].astype(bf)


def middle(part, scalars, h, own, recv, g, norms, mine, theirs, local, steps=2):
    count, width = h.shape
    rows = count // steps
    block = pl.BlockSpec((rows, width), lambda i, c: (i, 0))
    spec = pltpu.PrefetchScalarGridSpec(
        num_scalar_prefetch=1,
        grid=(steps,),
        in_specs=[block] * 3 + [pl.BlockSpec((rows, width), lambda i, c: (((2 * part) ^ c[0]) * steps + i, 0)), whole(norms.shape)] + [ANY] * (2 * len(mine)),
        out_specs=[block, block, pl.BlockSpec((2, local, rows), lambda i, c: (0, 0, i)), whole((8, width))],
        scratch_shapes=[pltpu.VMEM((2, width, 256), bf), pltpu.SemaphoreType.DMA((2,))],
    )
    return pl.pallas_call(
        functools.partial(middle_kernel, part, len(mine), steps),
        grid_spec=spec,
        out_shape=[SDS(h.shape, f32), SDS(h.shape, bf), SDS((2, local, count), bf), SDS((8, width), f32)],
        compiler_params=params(),
        cost_estimate=cost(3.5),
        name=f"middle{part}",
    )(scalars, h, own, recv, g, norms, *mine, *theirs)


def relative_rows(scr, d, index, count, relative):
    r = count // 8
    y, s = index // 4, index % 4
    at = pl.multiple_of((d ^ (2 * s + y)) * r, r) if relative else index * r
    return scr[pl.ds(at, r), :]


def turn(values, c_ref, scr, turned_ref, j, relative):
    rows, width = values[0].shape
    r = width // 8
    for i in range(2):
        scr[:, i * rows : (i + 1) * rows] = values[i][...].T
    for b in range(8):
        turned_ref[j, b * r : (b + 1) * r, :] = relative_rows(scr, c_ref[1], b, width, relative)


def weight_grad_kernel(first, relative, c_ref, *refs):
    if first:
        c1, c2, gb1, gb2, e1, e2, du1, du2, grad_ref, turned_ref, scr = refs
        turn((c1, c2), c_ref, scr, turned_ref, 0, relative)
        turn((gb1, gb2), c_ref, scr, turned_ref, 1, relative)
    else:
        turned_ref, e1, e2, du1, du2, recv_ref, grad_ref = refs
    rows, units = du1.shape[1:]
    a, b = slice(0, rows), slice(rows, 2 * rows)
    up = dot(turned_ref[0, :, a], du1[0]) + dot(turned_ref[0, :, b], du2[0])
    down = dot(turned_ref[1, :, a], e1[0]) + dot(turned_ref[1, :, b], e2[0])
    if not first:
        up = up + recv_ref[:, 0:units].astype(f32)
        down = down + recv_ref[:, units:].astype(f32)
    grad_ref[:, 0:units] = up.astype(bf)
    grad_ref[:, units:] = down.astype(bf)


def weight_grad_first(scalars, relative, cs, gbs, es, dus):
    rows, width = cs[0].shape
    units = es[0].shape[2]
    ins = [*cs, *gbs, *es, *dus]
    spec = pltpu.PrefetchScalarGridSpec(
        num_scalar_prefetch=1,
        grid=(1,),
        in_specs=[whole((rows, width))] * 4 + [pl.BlockSpec((1, rows, units), lambda i, c: (1, 0, 0))] * 4,
        out_specs=[whole((width, 2 * units)), whole((2, width, 2 * rows))],
        scratch_shapes=[pltpu.VMEM((width, 2 * rows), bf)],
    )
    return pl.pallas_call(
        functools.partial(weight_grad_kernel, True, relative),
        grid_spec=spec,
        out_shape=[SDS((width, 2 * units), bf), SDS((2, width, 2 * rows), bf)],
        compiler_params=params(),
        cost_estimate=cost(5.5),
        name="weight_grad_first",
    )(scalars, *ins)


def weight_grad_second(scalars, turned, es, dus, recv):
    _, width, tokens = turned.shape
    units = es[0].shape[2]
    ins = [turned, *es, *dus, recv]
    spec = pltpu.PrefetchScalarGridSpec(
        num_scalar_prefetch=1,
        grid=(1,),
        in_specs=[whole(turned.shape)] + [pl.BlockSpec((1, tokens // 2, units), lambda i, c: (0, 0, 0))] * 4 + [whole(recv.shape)],
        out_specs=whole((width, 2 * units)),
    )
    return pl.pallas_call(
        functools.partial(weight_grad_kernel, False, False),
        grid_spec=spec,
        out_shape=SDS((width, 2 * units), bf),
        compiler_params=params(),
        cost_estimate=cost(3.2),
        name="weight_grad_second",
    )(scalars, *ins)


def out_grad_kernel(relative, c_ref, dhb1, dhb2, o1, o2, other1, other2, ours_ref, theirs_ref, scr, turned):
    rows = dhb1.shape[0]
    turn((dhb1, dhb2), c_ref, scr, turned, 0, relative)
    a, b = turned[0, :, 0:rows], turned[0, :, rows : 2 * rows]
    theirs_ref[...] = (dot(a, other1[...], NT) + dot(b, other2[...], NT)).astype(bf)
    ours_ref[...] = (dot(a, o1[0], NT) + dot(b, o2[0], NT)).astype(bf)


def out_grad(scalars, relative, dhbs, os, others):
    rows, width = dhbs[0].shape
    local = others[0].shape[0]
    ins = [*dhbs, *os, *others]
    spec = pltpu.PrefetchScalarGridSpec(
        num_scalar_prefetch=1,
        grid=(1,),
        in_specs=[whole(v.shape) for v in ins],
        out_specs=[whole((width, local))] * 2,
        scratch_shapes=[pltpu.VMEM((width, 2 * rows), bf), pltpu.VMEM((1, width, 2 * rows), bf)],
    )
    return pl.pallas_call(
        functools.partial(out_grad_kernel, relative),
        grid_spec=spec,
        out_shape=[SDS((width, local), bf)] * 2,
        compiler_params=params(),
        cost_estimate=cost(2.6),
        name="out_grad",
    )(scalars, *ins)


def attend_back_kernel(part, c_ref, kp_ref, vp_ref, kt_ref, q1_ref, q2_ref, o_ref, lse_ref, do1_ref, do2_ref, *refs):
    if part == 0:
        dq_ref, kv_ref = refs
    else:
        kv_in, dq_ref, out_ref = refs
    q = q1_ref.shape[1]
    one = jnp.ones((1, q), f32)
    zero = jnp.zeros((HD, q), bf)
    blocks = []
    for i, (q_ref, do) in enumerate(((q1_ref, do1_ref[0]), (q2_ref, do2_ref[...]))):
        delta = jnp.sum(do.astype(f32) * o_ref[i].astype(f32), axis=0, keepdims=True)
        queries = with_tail(q_ref[...], [one] + [-v for v in split3(lse_ref[0, i, 0:1])])
        grads = with_tail(do, [0.0 * one] + [-v for v in split3(delta)])
        blocks.append((queries, grads, jnp.concatenate([do, zero], axis=0), jnp.concatenate([zero, q_ref[...]], axis=0)))
    dq = [None] * 2
    for b in range(4):
        at = slice(b * q, (b + 1) * q)
        kv = None if part == 0 else kv_in[0, at, :]
        for i, (queries, grads, do_low, q_high) in enumerate(blocks):
            p = jnp.exp2(dot(kp_ref[at, :], queries) * LOG2E)
            ds = (p * dot(vp_ref[at, :], grads)).astype(bf)
            here = dot(p.astype(bf), do_low, NT) + dot(ds, q_high, NT)
            kv = here if kv is None else kv + here
            here = dot(kt_ref[:, at], ds)
            dq[i] = here if dq[i] is None else dq[i] + here
        if part == 0:
            kv_ref[0, at, :] = kv
        else:
            turned = kv.T.astype(bf)
            other = (b % 2) ^ c_ref[0]
            out_ref[other, b // 2, 0] = turned[HD:]
            out_ref[other, b // 2, 1] = turned[:HD]
    for i in range(2):
        dq_ref[i] = (dq[i] * 0.125).astype(bf)


def attend_back(part, scalars, kp, vp, kt, qt, o, lse, do, do_other, sums=()):
    count = kp.shape[0]
    heads = qt.shape[0] // HD
    q = count // 4
    keyed = pl.BlockSpec((count, 2 * HD), lambda h, c: (0, h))
    pair = pl.BlockSpec((2, HD, q), lambda h, c: (0, h, 0))
    total = pl.BlockSpec((1, count, 2 * HD), lambda h, c: (h, 0, 0))
    dq_shape = SDS((2, heads * HD, q), bf)
    if part == 0:
        out_specs, out_shape = [pair, total], [dq_shape, SDS((heads, count, 2 * HD), f32)]
    else:
        out_specs = [pair, pl.BlockSpec((2, 2, 2, HD, q), lambda h, c: (0, 0, 0, h, 0))]
        out_shape = [dq_shape, SDS((2, 2, 2, heads * HD, q), bf)]
    spec = pltpu.PrefetchScalarGridSpec(
        num_scalar_prefetch=1,
        grid=(heads,),
        in_specs=[
            keyed,
            keyed,
            pl.BlockSpec((HD, count), lambda h, c: (h, 0)),
            pl.BlockSpec((HD, q), lambda h, c: (h, (2 * part) ^ c[0])),
            pl.BlockSpec((HD, q), lambda h, c: (h, (2 * part + 1) ^ c[0])),
            pair,
            pl.BlockSpec((1, 2, 8, q), lambda h, c: (h, 0, 0, 0)),
            pl.BlockSpec((1, HD, q), lambda h, c: (0, h, 0)),
            pl.BlockSpec((HD, q), lambda h, c: (h, 0)),
        ]
        + [total] * len(sums),
        out_specs=out_specs,
    )
    return pl.pallas_call(
        functools.partial(attend_back_kernel, part),
        grid_spec=spec,
        out_shape=out_shape,
        compiler_params=params(),
        cost_estimate=cost(18),
        name=f"attend_back{part}",
    )(scalars, kp, vp, kt, qt, qt, o, lse, do, do_other, *sums)


def da_kernel(pieces, c_ref, dq1, dq2, dkv, rq1, rq2, rkv, x1_ref, x2_ref, *refs):
    mine, theirs = refs[:pieces], refs[pieces : 2 * pieces]
    one_ref, two_ref, sum_ref, w_scr, d_scr, sem = refs[2 * pieces :]
    width = one_ref.shape[0]
    local = rq1.shape[0]
    for k, group in enumerate((mine, theirs)):
        for copy in row_copies(group, c_ref[1], width, w_scr.at[k], slice(0, w_scr.shape[2]), sem.at[k]):
            copy.start()
    for i in range(2):
        own, other = (dq1, dq2)[i], (rq1, rq2)[i]
        d_scr[i, 0, 0:local, :] = own[0]
        d_scr[i, 1, 0:local, :] = other[...]
        for j in range(2):
            at = slice((j + 1) * local, (j + 2) * local)
            d_scr[i, 0, at, :] = dkv[0, i, j]
            d_scr[i, 1, at, :] = rkv[i, j]
    for k in range(2):
        wait_for(w_scr.at[k], sem.at[k])
    sums = [jnp.zeros((1, width), f32)] * 2
    at = slice(0, 3 * local)
    for i, (da_ref, x_ref) in enumerate(((one_ref, x1_ref), (two_ref, x2_ref))):
        da = (dot(w_scr[0, :, at], d_scr[i, 0]) + dot(w_scr[1, :, at], d_scr[i, 1])).astype(bf)
        da_ref[...] = da
        n1, _ = normalize(x_ref[...].astype(f32))
        da = da.astype(f32).T
        sums = [sums[0] + jnp.sum(da * n1, axis=0, keepdims=True), sums[1] + jnp.sum(da, axis=0, keepdims=True)]
    sum_ref[0:1, :], sum_ref[1:2, :] = sums
    sum_ref[2:8, :] = jnp.zeros((6, width), f32)


def da_product(scalars, dq1, dq2, dkv, rq1, rq2, rkv, x, mine, theirs):
    local, q = rq1.shape
    width = x.shape[1]
    packed = mine[0].shape[-1]
    ins = [dq1, dq2, dkv, rq1, rq2, rkv]
    spec = pltpu.PrefetchScalarGridSpec(
        num_scalar_prefetch=1,
        grid=(1,),
        in_specs=[whole(v.shape) for v in ins]
        + [pl.BlockSpec((q, width), lambda i, c: (c[0], 0)), pl.BlockSpec((q, width), lambda i, c: (2 ^ c[0], 0))]
        + [ANY] * (2 * len(mine)),
        out_specs=[whole((width, q))] * 2 + [whole((8, width))],
        scratch_shapes=[pltpu.VMEM((2, width, packed), bf), pltpu.VMEM((2, 2, 3 * local, q), bf), pltpu.SemaphoreType.DMA((2,))],
    )
    return pl.pallas_call(
        functools.partial(da_kernel, len(mine)),
        grid_spec=spec,
        out_shape=[SDS((width, q), bf)] * 2 + [SDS((8, width), f32)],
        compiler_params=params(),
        cost_estimate=cost(5.4),
        name="da_product",
    )(scalars, *ins, x, x, *mine, *theirs)


def dx_kernel(c_ref, own_ref, recv_ref, x_ref, dh_ref, norm_ref, dx_ref):
    da = (own_ref[...].astype(f32) + recv_ref[...].astype(f32)).T
    n1, r1 = normalize(x_ref[...].astype(f32))
    dx_ref[...] = (dh_ref[...] + norm_back(da, n1, r1, norm_ref[0:1, :])).astype(bf)


def dx_block(part, scalars, own, recv, x, dh, norms):
    width, rows = own.shape
    spec = pltpu.PrefetchScalarGridSpec(
        num_scalar_prefetch=1,
        grid=(1,),
        in_specs=[whole(own.shape)] * 2
        + [pl.BlockSpec((rows, width), lambda i, c: ((2 * part) ^ c[0], 0)), whole(dh.shape), whole(norms.shape)],
        out_specs=whole((rows, width)),
    )
    return pl.pallas_call(
        dx_kernel,
        grid_spec=spec,
        out_shape=SDS((rows, width), bf),
        compiler_params=params(),
        cost_estimate=cost(2.8),
        name=f"dx{part}",
    )(scalars, own, recv, x, dh, norms)


def qkv_grad_kernel(relative, c_ref, a_ref, dq1, dq2, dkv, out1, out2, sum_ref, grad_ref, g_scr):
    local, q = dq1.shape[1:]
    width = a_ref.shape[1]
    total = [None] * 3
    for m in range(4):
        a = a_ref[m * q : (m + 1) * q, :]
        parts = [(dq1, dq2)[m // 2][m % 2], dkv[m % 2, m // 2, 0], dkv[m % 2, m // 2, 1]]
        for j in range(3):
            here = dot(parts[j], a)
            total[j] = here if total[j] is None else total[j] + here
    for j in range(3):
        g_scr[:, j * local : (j + 1) * local] = total[j].T.astype(bf)
    tall = jnp.concatenate([sum_ref[...], jnp.zeros((120, width), f32)], axis=0)
    g_scr[:, 4 * local : 4 * local + 128] = tall.T.astype(bf)
    r = width // 8
    for b in range(8):
        rows = relative_rows(g_scr, c_ref[1], b, width, relative)
        grad_ref[b * r : (b + 1) * r, local : 4 * local] = rows[:, 0 : 3 * local]
        grad_ref[b * r : (b + 1) * r, 4 * local :] = rows[:, 4 * local :]
    grad_ref[:, 0:local] = (out1[...].astype(f32) + out2[...].astype(f32)).astype(bf)


def qkv_grad(scalars, relative, normed, dq1, dq2, dkv, out1, out2, sums):
    width = normed.shape[1]
    local = dq1.shape[1]
    ins = [normed, dq1, dq2, dkv, out1, out2, sums]
    spec = pltpu.PrefetchScalarGridSpec(
        num_scalar_prefetch=1,
        grid=(1,),
        in_specs=[whole(v.shape) for v in ins],
        out_specs=whole((width, 4 * local + 128)),
        scratch_shapes=[pltpu.VMEM((width, 4 * local + 128), bf)],
    )
    return pl.pallas_call(
        functools.partial(qkv_grad_kernel, relative),
        grid_spec=spec,
        out_shape=SDS((width, 4 * local + 128), bf),
        compiler_params=params(),
        cost_estimate=cost(4.2),
        name="qkv_grad",
    )(scalars, *ins)


def gather_z(piece, n):
    return [piece] + [swap(piece, "dp", 2 * s, n) for s in (1, 2, 3)]


def gather_y(pieces, n):
    along_z = jnp.stack(pieces)
    return [in_hbm(along_z), in_hbm(swap(along_z, "dp", 1, n))]


def scatter_y(value, n):
    if n != 8:
        return value
    half = value.shape[0] // 2
    return (value[:half].astype(f32) + swap(value[half:], "dp", 1, n).astype(f32)).astype(bf)


def scatter_z(half, n):
    if n != 8:
        return lax.psum_scatter(half, "dp", scatter_dimension=0, tiled=True).astype(f32)
    r = half.shape[0] // 4
    total = half[0:r].astype(f32)
    for s in (1, 2, 3):
        total = total + swap(half[s * r : (s + 1) * r], "dp", 2 * s, n).astype(f32)
    return total


def assemble_kernel(c_ref, *refs):
    blocks, (out_ref, sem) = refs[:4], refs[4:]
    rows = blocks[0].shape[0]
    copies = []
    for m, block in enumerate(blocks):
        at = pl.multiple_of((m ^ c_ref[0]) * rows, rows)
        copies.append(pltpu.make_async_copy(block, out_ref.at[pl.ds(at, rows), :], sem.at[m]))
    for copy in copies:
        copy.start()
    for copy in copies:
        copy.wait()


def assemble(scalars, *blocks):
    rows, width = blocks[0].shape
    spec = pltpu.PrefetchScalarGridSpec(
        num_scalar_prefetch=1,
        grid=(1,),
        in_specs=[pl.BlockSpec(memory_space=pltpu.VMEM)] * 4,
        out_specs=pl.BlockSpec(memory_space=pl.ANY),
        scratch_shapes=[pltpu.SemaphoreType.DMA((4,))],
    )
    return pl.pallas_call(
        assemble_kernel,
        grid_spec=spec,
        out_shape=SDS((4 * rows, width), bf),
        compiler_params=params(),
        cost_estimate=cost(2.2),
        name="assemble",
    )(scalars, *blocks)


def body(n, embeddings, cotangent, species, gene_ids, w_qkv, w_out, w_up, w_down, norm_gains, norm_shifts):
    c = lax.axis_index("tensor") % 2
    d = lax.axis_index("dp")
    relative = n == 8
    count, width = embeddings.shape
    r = width // n
    local = w_qkv.shape[2]
    units = w_up.shape[1]
    length = jnp.sum((gene_ids != 0).astype(jnp.int32))
    alive = jnp.where(species[0] == 2, 0, length)
    scalars = jnp.stack([c, d, length, alive]).astype(jnp.int32)

    norms_own = jnp.concatenate([norm_gains, norm_shifts]).T
    packed = jnp.concatenate([w_qkv[0], w_qkv[1], w_qkv[2], jnp.pad(norms_own, ((0, 0), (0, 60)))], axis=1).astype(bf)
    pad = ((0, 0), (0, 256 - local))
    if relative:
        w_first = gather_y(gather_z(packed, n), n)
        w_out, w_up = after((w_out, w_up), w_first[0])
        out_up_z = gather_z(jnp.concatenate([jnp.pad(w_out.T, pad), w_up], axis=1).astype(bf), n)
    else:
        rows = lambda v: [lax.all_gather(v.astype(bf), "dp", axis=0, tiled=True)]
        w_first, w_o, w_u, w_d = rows(packed), rows(jnp.pad(w_out.T, pad)), rows(w_up), rows(w_down.T)
    others = lambda group: [in_hbm(core_swap(v)) for v in group]

    normed, kp, vp, kt, vt, qt, norm_rows = project(scalars, embeddings, w_first, local)
    if relative:
        out_up_z, w_down = after((out_up_z, w_down), norm_rows)
        w_o = gather_y([v[:, :256] for v in out_up_z], n)
        w_u = gather_y([v[:, 256:] for v in out_up_z], n)
        down_z = gather_z(w_down.astype(bf).T, n)
    o, lse, o_other, h, cs, gbs, es, dus, ffns, dcs = ([None] * 2 for _ in range(10))
    sent = [None] * 2
    o[0], lse[0] = attend(scalars, kp, vt, qt, 0)
    o_other[0] = core_swap(o[0][1])
    w_o2 = others(after(w_o, lse[0]))
    w_u = after(w_u, lse[0])
    w_u2 = others(w_u)
    sent[0] = out_product(after(scalars, w_u, down_z) if relative else scalars, o[0], o_other[0], w_o, w_o2, width)
    if relative:
        w_d = gather_y(after(down_z, sent[0]), n)
    o[1], lse[1] = attend(after(scalars, sent[0]), kp, vt, qt, 1)
    o_other[1] = core_swap(o[1][1])
    recv0 = x_swap(sent[0])
    sent[1] = out_product(after(scalars, recv0), o[1], o_other[1], w_o, w_o2, width)
    w_d2 = others(after(w_d, sent[1]))
    last = after(scalars, sent[1])
    for i in range(2):
        recv = x_swap(sent[1]) if i else recv0
        h[i], cs[i], gbs[i], es[i], dus[i], ffns[i], dcs[i] = ffn(
            i, last, embeddings, cotangent, sent[i], recv, norm_rows, w_u, w_d, w_u2, w_d2, units
        )
        last = after(scalars, dcs[i])
    dh, dhb, do, do_other, sums = ([None] * 2 for _ in range(5))
    i = 0
    dh[i], dhb[i], do[i], sums[i] = middle(i, last, h[i], dcs[i], x_swap(dcs[i]), cotangent, norm_rows, w_o, w_o2, local)
    recv_ffn = [x_swap(v) for v in after(ffns, do[0])]
    do_other[i] = core_swap(do[i][1])
    last = after(scalars, dhb[0])
    grad_theirs, turned = weight_grad_first(last, relative, cs, gbs, es, dus)
    grad_ours = weight_grad_second(after(scalars,turned), turned, es, dus, core_swap(grad_theirs))
    last = after(scalars, grad_ours)
    dq1, dkv1 = attend_back(0, last, kp, vp, kt, qt, o[0], lse[0], do[0], do_other[0])
    last = after(scalars, dq1)
    i = 1
    dh[i], dhb[i], do[i], sums[i] = middle(i, last, h[i], dcs[i], x_swap(dcs[i]), cotangent, norm_rows, w_o, w_o2, local)
    do_other[i] = core_swap(do[i][1])
    last = after(scalars, dhb[1])
    out_ours, out_theirs = out_grad(last, relative, dhb, o, o_other)
    last = after(scalars, out_ours, recv_ffn[0])
    dq2, dkv = attend_back(1, last, kp, vp, kt, qt, o[1], lse[1], do[1], do_other[1], (dkv1,))
    half_ours = scatter_y(grad_ours, n)

    rq1, rq2, rkv = core_swap(dq1[1]), core_swap(dq2[1]), core_swap(dkv[1])
    w_first2 = others(w_first)
    da0, da1, sums1 = da_product(after(scalars, half_ours), dq1, dq2, dkv, rq1, rq2, rkv, embeddings, w_first, w_first2)
    recv_da = [x_swap(da0), x_swap(da1)]
    last = after(scalars, da0)
    s_rest = scatter_z(half_ours, n)
    grad_first = qkv_grad(last, relative, normed, dq1, dq2, dkv, out_ours, core_swap(out_theirs), sums1 + 0.5 * (sums[0] + sums[1]))
    half_first = scatter_y(grad_first, n)

    ffns, recv_ffn = after((ffns, recv_ffn), grad_first)
    mixed = [(h[i] + (ffns[i].astype(f32) + recv_ffn[i].astype(f32))).astype(bf) for i in range(2)]
    mixed = assemble(scalars, mixed[0], core_swap(mixed[0]), mixed[1], core_swap(mixed[1]))
    last = after(scalars, mixed)
    dx0 = dx_block(0, last, da0, recv_da[0], embeddings, dh[0], norm_rows)
    last = after(scalars, dx0, half_first)
    s_first = scatter_z(half_first, n)
    dx1 = dx_block(1, last, da1, recv_da[1], embeddings, dh[1], norm_rows)
    grad_input = assemble(scalars, dx0, core_swap(dx0), dx1, core_swap(dx1))
    s_up, s_down = s_rest[:, :units], s_rest[:, units:].T
    s_out = s_first[:, :local].T
    s_qkv = s_first[:, local : 4 * local].reshape(r, 3, local).transpose(1, 0, 2)
    both = s_first[:, 4 * local : 4 * local + 4]
    both = both + core_swap(both)
    both = (both + x_swap(both)).T
    gains = jnp.stack([both[0], both[2]])
    shifts = jnp.stack([both[1], both[3]])
    return (mixed, grad_input, s_qkv, s_out, s_up, s_down, gains, shifts, both[3])


def solution(mesh):
    return jax.shard_map(
        functools.partial(body, mesh.shape["dp"]),
        mesh=mesh,
        in_specs=(
            P("dp", None),
            P("dp", None),
            P("dp"),
            P("dp", None),
            P(None, "dp", "tensor"),
            P("tensor", "dp"),
            P("dp", "tensor"),
            P("tensor", "dp"),
            P(None, "dp"),
            P(None, "dp"),
        ),
        out_specs=(
            P("dp", None),
            P("dp", None),
            P(None, "dp", "tensor"),
            P("tensor", "dp"),
            P("dp", "tensor"),
            P("tensor", "dp"),
            P(None, "dp"),
            P(None, "dp"),
            P("dp"),
        ),
        check_vma=False,
    )
```

```python
import functools
import math

import jax
import jax.numpy as jnp
from jax import lax
from jax.experimental import pallas as pl
from jax.experimental.pallas import tpu as pltpu
from jax.sharding import PartitionSpec as P

HD = 64
EPSILON = 1e-05
NEGATIVE = -1e30
LOG2E = math.log2(math.e)
bf = jnp.bfloat16
f32 = jnp.float32
NN = ((1,), (0,))
NT = ((1,), (1,))
ANY = pl.BlockSpec(memory_space=pltpu.HBM)
SDS = jax.ShapeDtypeStruct


def dot(a, b, dims=NN):
    return lax.dot_general(a, b, (dims, ((), ())), preferred_element_type=f32)


def swap(value, axis, mask, size):
    return lax.ppermute(value, axis, [(i, i ^ mask) for i in range(size)])


def core_swap(value):
    return swap(value, "tensor", 1, 4)


def x_swap(value):
    return swap(value, "tensor", 2, 4)


def in_hbm(value):
    return pltpu.with_memory_space_constraint(value, pltpu.HBM)


def after(value, *others):
    return lax.optimization_barrier((value,) + others)[0]


def params(mib=32):
    return pltpu.CompilerParams(vmem_limit_bytes=mib << 20)


SCALE = 0.001


def cost(us):
    return pl.CostEstimate(flops=int(us * SCALE * 1.15e9), bytes_accessed=int(us * SCALE * 1e6), transcendentals=0)


def whole(shape):
    return pl.BlockSpec(shape, lambda *_: (0,) * len(shape))


def row_copies(refs, d, count, dst, columns, sem):
    copies = []
    if len(refs) == 1:
        copies.append(pltpu.make_async_copy(refs[0].at[:, columns], dst, sem))
        return copies
    r = count // 8
    for y, ref in enumerate(refs):
        for s in range(4):
            at = pl.multiple_of((d ^ (2 * s + y)) * r, r)
            copies.append(pltpu.make_async_copy(ref.at[s, 0:r, columns], dst.at[pl.ds(at, r), :], sem))
    return copies


def wait_for(dst, sem):
    pltpu.make_async_copy(dst, dst, sem).wait()


def split3(v):
    a = v.astype(bf)
    rest = v - a.astype(f32)
    b = rest.astype(bf)
    c = (rest - b.astype(f32)).astype(bf)
    return [a.astype(f32), b.astype(f32), c.astype(f32)]


def with_tail(block, rows):
    q = block.shape[1]
    index = lax.broadcasted_iota(jnp.int32, (HD, q), 0)
    tail = jnp.zeros((HD, q), f32)
    for i, row in enumerate(rows):
        tail = jnp.where(index == i, row, tail)
    return jnp.concatenate([block, tail.astype(bf)], axis=0)


def normalize(v):
    center = v - jnp.mean(v, axis=-1, keepdims=True)
    variance = jnp.mean(center * center, axis=-1, keepdims=True)
    r = lax.rsqrt(variance + EPSILON)
    return center * r, r


def norm_back(dn, n, r, gain):
    scaled = dn * gain
    return r * (scaled - jnp.mean(scaled, axis=-1, keepdims=True) - n * jnp.mean(scaled * n, axis=-1, keepdims=True))


def project_kernel(heads, pieces, c_ref, x_ref, *refs):
    w_refs = refs[:pieces]
    a_ref, kp_ref, vp_ref, kt_ref, vt_ref, qt_ref, norm_ref, w_scr, wt_scr, wk_scr, wv_scr, sem = refs[pieces:]
    step = pl.program_id(0)
    rows, width = x_ref.shape
    local = HD * heads

    @pl.when(step == 0)
    def _():
        for copy in row_copies(w_refs, c_ref[1], width, w_scr, slice(0, w_scr.shape[1]), sem):
            copy.start()
        wait_for(w_scr, sem)
        wt_scr[...] = w_scr[...].T
        norm_ref[...] = wt_scr[3 * local : 3 * local + 16, :].astype(f32)[0:8]
        zero = jnp.zeros((width, HD), bf)
        for h in range(heads):
            at = slice(2 * HD * h, 2 * HD * (h + 1))
            wk_scr[:, at] = jnp.concatenate([w_scr[:, local + HD * h : local + HD * (h + 1)], zero], axis=1)
            wv_scr[:, at] = jnp.concatenate([w_scr[:, 2 * local + HD * h : 2 * local + HD * (h + 1)], zero], axis=1)

    n, _ = normalize(x_ref[...].astype(f32))
    a = (n * norm_ref[0:1, :] + norm_ref[2:3, :]).astype(bf)
    a_ref[...] = a
    token = (step ^ c_ref[0]) * rows + lax.broadcasted_iota(jnp.int32, (rows, 2 * local), 0)
    lane = lax.broadcasted_iota(jnp.int32, (rows, 2 * local), 1) % (2 * HD)
    ones = jnp.where((lane > HD) & (lane < HD + 4), 1.0, 0.0)
    bias = jnp.where((lane == HD) & (token >= c_ref[2]), NEGATIVE, ones)
    kp_ref[...] = (dot(a, wk_scr[...]) + bias).astype(bf)
    vp_ref[...] = (dot(a, wv_scr[...]) + ones).astype(bf)
    both = dot(wt_scr[0 : 3 * local, :], a, NT)
    qt_ref[...] = (both[0:local] * 0.125).astype(bf)
    kt_ref[...] = both[local : 2 * local].astype(bf)
    vt_ref[...] = both[2 * local : 3 * local].astype(bf)


def project(scalars, x, w, local):
    count, width = x.shape
    heads = local // HD
    rows = count // 4
    packed = w[0].shape[-1]
    block = lambda i, c: (i ^ c[0], 0)
    turned = lambda i, c: (0, i ^ c[0])
    spec = pltpu.PrefetchScalarGridSpec(
        num_scalar_prefetch=1,
        grid=(4,),
        in_specs=[pl.BlockSpec((rows, width), block)] + [ANY] * len(w),
        out_specs=[
            pl.BlockSpec((rows, width), lambda i, c: (i, 0)),
            pl.BlockSpec((rows, 2 * local), block),
            pl.BlockSpec((rows, 2 * local), block),
            pl.BlockSpec((local, rows), turned),
            pl.BlockSpec((local, rows), turned),
            pl.BlockSpec((local, rows), turned),
            whole((8, width)),
        ],
        scratch_shapes=[
            pltpu.VMEM((width, packed), bf),
            pltpu.VMEM((packed, width), bf),
            pltpu.VMEM((width, 2 * local), bf),
            pltpu.VMEM((width, 2 * local), bf),
            pltpu.SemaphoreType.DMA,
        ],
    )
    return pl.pallas_call(
        functools.partial(project_kernel, heads, len(w)),
        grid_spec=spec,
        out_shape=[SDS((count, width), bf), SDS((count, 2 * local), bf), SDS((count, 2 * local), bf)]
        + [SDS((local, count), bf)] * 3
        + [SDS((8, width), f32)],
        compiler_params=params(),
        cost_estimate=cost(10),
        name="project",
    )(scalars, x, *w)


def attend_kernel(chunk, c_ref, kp_ref, kp_next, vt_ref, q1_ref, q2_ref, q1_next, o_ref, lse_ref, a_scr, b_scr, top_scr):
    keys = kp_ref.shape[0]
    q = q1_ref.shape[1]
    spans = [slice(i * chunk, (i + 1) * chunk) for i in range(keys // chunk)]
    one = [jnp.ones((1, q), f32)]

    def scores(k_ref, queries, at, scr, top):
        s = dot(k_ref[at, :], queries)
        scr[at, :] = s
        here = jnp.max(s, axis=0, keepdims=True)
        return here if top is None else jnp.maximum(top, here)

    @pl.when(pl.program_id(0) == 0)
    def _():
        queries = with_tail(q1_ref[...], one)
        top = None
        for at in spans:
            top = scores(kp_ref, queries, at, a_scr, top)
        top_scr[...] = jnp.broadcast_to(top, (8, q))

    before = top_scr[0:1, :]
    turns = ((0, a_scr, b_scr, kp_ref, q2_ref), (1, b_scr, a_scr, kp_next, q1_next))
    for i, ready, filling, k_ref, q_ref in turns:
        queries = with_tail(q_ref[...], one)
        top = total = out = None
        for at in spans:
            top = scores(k_ref, queries, at, filling, top)
            p = jnp.exp2((ready[at, :] - before) * LOG2E)
            here = jnp.sum(p, axis=0, keepdims=True)
            part = dot(vt_ref[:, at], p.astype(bf))
            total = here if total is None else total + here
            out = part if out is None else out + part
        o_ref[i] = (out / total).astype(bf)
        lse_ref[0, i] = jnp.broadcast_to(before + jnp.log(total), (8, q))
        before = top
    top_scr[...] = jnp.broadcast_to(before, (8, q))


def attend(scalars, kp, vt, qt, part):
    count = kp.shape[0]
    heads = qt.shape[0] // HD
    q = count // 4
    follow = lambda h: jnp.minimum(h + 1, heads - 1)
    spec = pltpu.PrefetchScalarGridSpec(
        num_scalar_prefetch=1,
        grid=(heads,),
        in_specs=[
            pl.BlockSpec((count, 2 * HD), lambda h, c: (0, h)),
            pl.BlockSpec((count, 2 * HD), lambda h, c: (0, follow(h))),
            pl.BlockSpec((HD, count), lambda h, c: (h, 0)),
            pl.BlockSpec((HD, q), lambda h, c: (h, (2 * part) ^ c[0])),
            pl.BlockSpec((HD, q), lambda h, c: (h, (2 * part + 1) ^ c[0])),
            pl.BlockSpec((HD, q), lambda h, c: (follow(h), (2 * part) ^ c[0])),
        ],
        out_specs=[
            pl.BlockSpec((2, HD, q), lambda h, c: (0, h, 0)),
            pl.BlockSpec((1, 2, 8, q), lambda h, c: (h, 0, 0, 0)),
        ],
        scratch_shapes=[pltpu.VMEM((count, q), f32), pltpu.VMEM((count, q), f32), pltpu.VMEM((8, q), f32)],
    )
    return pl.pallas_call(
        functools.partial(attend_kernel, min(512, count)),
        grid_spec=spec,
        out_shape=[SDS((2, heads * HD, q), bf), SDS((heads, 2, 8, q), f32)],
        compiler_params=params(),
        cost_estimate=cost(10),
        name=f"attend{part}",
    )(scalars, kp, kp, vt, qt, qt, qt)


def out_kernel(pieces, c_ref, o_ref, other_ref, *refs):
    mine, theirs, (part_ref, w_scr, sem) = refs[:pieces], refs[pieces : 2 * pieces], refs[2 * pieces :]
    width = part_ref.shape[0]
    for k, group in enumerate((mine, theirs)):
        for copy in row_copies(group, c_ref[1], width, w_scr.at[k], slice(0, 256), sem.at[k]):
            copy.start()
    local = o_ref.shape[1]
    wait_for(w_scr.at[0], sem.at[0])
    part = dot(w_scr[0, :, 0:local], o_ref[0])
    wait_for(w_scr.at[1], sem.at[1])
    part_ref[...] = (part + dot(w_scr[1, :, 0:local], other_ref[...])).astype(bf)


def out_product(scalars, o, other, mine, theirs, width):
    local, q = other.shape
    spec = pltpu.PrefetchScalarGridSpec(
        num_scalar_prefetch=1,
        grid=(1,),
        in_specs=[whole(o.shape), whole(other.shape)] + [ANY] * (2 * len(mine)),
        out_specs=whole((width, q)),
        scratch_shapes=[pltpu.VMEM((2, width, 256), bf), pltpu.SemaphoreType.DMA((2,))],
    )
    return pl.pallas_call(
        functools.partial(out_kernel, len(mine)),
        grid_spec=spec,
        out_shape=SDS((width, q), bf),
        compiler_params=params(),
        cost_estimate=cost(2.2),
        name="out_product",
    )(scalars, o, other, *mine, *theirs)


def ffn_kernel(part, pieces, steps, c_ref, x_ref, g_ref, own_ref, recv_ref, norm_ref, *refs):
    groups = [refs[i * pieces : (i + 1) * pieces] for i in range(4)]
    h_ref, c_out, gb_ref, e_ref, du_ref, dc_ref, ffn_ref, w_scr, sem = refs[4 * pieces + part :]
    step = pl.program_id(0)
    rows, width = x_ref.shape
    units = e_ref.shape[2]

    @pl.when(step == 0)
    def _():
        for j, group in enumerate(groups):
            for copy in row_copies(group, c_ref[1], width, w_scr.at[j], slice(0, units), sem.at[j]):
                copy.start()

    h = x_ref[...].astype(f32) + (own_ref[...].astype(f32) + recv_ref[...].astype(f32)).T
    h_ref[...] = h
    n2, _ = normalize(h)
    c = (n2 * norm_ref[1:2, :] + norm_ref[3:4, :]).astype(bf)
    c_out[...] = c
    token = (((2 * part) ^ c_ref[0]) * steps + step) * rows + lax.broadcasted_iota(jnp.int32, (rows, 1), 0)
    gb = jnp.where(token < c_ref[3], g_ref[...].astype(f32), 0.0).astype(bf)
    gb_ref[...] = gb

    @pl.when(step == 0)
    def _():
        for j in range(4):
            wait_for(w_scr.at[j], sem.at[j])

    u = [dot(c, w_scr[2 * k]) for k in range(2)]
    de = [dot(gb, w_scr[2 * k + 1]) for k in range(2)]
    ffn = dc = None
    for k in range(2):
        phi = 0.5 * (1.0 + lax.erf(u[k] * math.sqrt(0.5)))
        e = (u[k] * phi).astype(bf)
        e_ref[k] = e
        du = (de[k] * (phi + u[k] * jnp.exp(-0.5 * u[k] * u[k]) * (1.0 / math.sqrt(2.0 * math.pi)))).astype(bf)
        du_ref[k] = du
        one, two = dot(du, w_scr[2 * k], NT), dot(e, w_scr[2 * k + 1], NT)
        dc = one if dc is None else dc + one
        ffn = two if ffn is None else ffn + two
    dc_ref[...] = dc.astype(bf)
    ffn_ref[0] = ffn.astype(bf)


def ffn(part, scalars, x, g, own, recv, norms, up, down, up_other, down_other, units, before=(), steps=2):
    width, count = own.shape
    rows = count // steps
    token_block = pl.BlockSpec((rows, width), lambda i, c: (((2 * part) ^ c[0]) * steps + i, 0))
    turned = pl.BlockSpec((width, rows), lambda i, c: (0, i))
    block = pl.BlockSpec((rows, width), lambda i, c: (i, 0))
    unit_block = pl.BlockSpec((2, rows, units), lambda i, c: (0, i, 0))
    weights = [*up, *down, *up_other, *down_other]
    spec = pltpu.PrefetchScalarGridSpec(
        num_scalar_prefetch=1,
        grid=(steps,),
        in_specs=[token_block, token_block, turned, turned, whole(norms.shape)] + [ANY] * len(weights) + [pl.BlockSpec(memory_space=pl.ANY)] * part,
        out_specs=[block, block, block, unit_block, unit_block, block, pl.BlockSpec((1, rows, width), lambda i, c: (part, i, 0))],
        scratch_shapes=[pltpu.VMEM((4, width, units), bf), pltpu.SemaphoreType.DMA((4,))],
    )
    return pl.pallas_call(
        functools.partial(ffn_kernel, part, len(up), steps),
        grid_spec=spec,
        out_shape=[SDS((count, width), f32), SDS((count, width), bf), SDS((count, width), bf)]
        + [SDS((2, count, units), bf)] * 2
        + [SDS((count, width), bf), SDS((2, count, width), bf)],
        input_output_aliases={6 + len(weights): 6} if part else {},
        compiler_params=params(),
        cost_estimate=cost(10),
        name=f"ffn{part}",
    )(scalars, x, g, own, recv, norms, *weights, *before)


def middle_kernel(part, pieces, steps, c_ref, h_ref, own_ref, recv_ref, g_ref, norm_ref, *refs):
    mine, theirs = refs[:pieces], refs[pieces : 2 * pieces]
    dh_ref, dhb_ref, do_ref, sum_ref, w_scr, sem = refs[2 * pieces :]
    step = pl.program_id(0)
    rows, width = h_ref.shape
    local = do_ref.shape[1]

    @pl.when(step == 0)
    def _():
        sum_ref[...] = jnp.zeros((8, width), f32)
        for k, group in enumerate((mine, theirs)):
            for copy in row_copies(group, c_ref[1], width, w_scr.at[k], slice(0, 256), sem.at[k]):
                copy.start()

    n2, r2 = normalize(h_ref[...])
    dc = own_ref[...].astype(f32) + recv_ref[...].astype(f32)
    token = (((2 * part) ^ c_ref[0]) * steps + step) * rows + lax.broadcasted_iota(jnp.int32, (rows, 1), 0)
    g = jnp.where(token < c_ref[3], g_ref[...].astype(f32), 0.0)
    dh = g + norm_back(dc, n2, r2, norm_ref[1:2, :])
    dh_ref[...] = dh
    dhb = dh.astype(bf)
    dhb_ref[...] = dhb
    sum_ref[2:3, :] += jnp.sum(dc * n2, axis=0, keepdims=True)
    sum_ref[3:4, :] += jnp.sum(dc, axis=0, keepdims=True)

    @pl.when(step == 0)
    def _():
        for k in range(2):
            wait_for(w_scr.at[k], sem.at[k])

    for k in range(2):
        do_ref[k] = dot(dhb, w_scr[k]).T[0:local].astype(bf)


def middle(part, scalars, h, own, recv, g, norms, mine, theirs, local, steps=2):
    count, width = h.shape
    rows = count // steps
    block = pl.BlockSpec((rows, width), lambda i, c: (i, 0))
    spec = pltpu.PrefetchScalarGridSpec(
        num_scalar_prefetch=1,
        grid=(steps,),
        in_specs=[block] * 3 + [pl.BlockSpec((rows, width), lambda i, c: (((2 * part) ^ c[0]) * steps + i, 0)), whole(norms.shape)] + [ANY] * (2 * len(mine)),
        out_specs=[block, block, pl.BlockSpec((2, local, rows), lambda i, c: (0, 0, i)), whole((8, width))],
        scratch_shapes=[pltpu.VMEM((2, width, 256), bf), pltpu.SemaphoreType.DMA((2,))],
    )
    return pl.pallas_call(
        functools.partial(middle_kernel, part, len(mine), steps),
        grid_spec=spec,
        out_shape=[SDS(h.shape, f32), SDS(h.shape, bf), SDS((2, local, count), bf), SDS((8, width), f32)],
        compiler_params=params(),
        cost_estimate=cost(3.5),
        name=f"middle{part}",
    )(scalars, h, own, recv, g, norms, *mine, *theirs)


def relative_rows(scr, d, index, count, relative):
    r = count // 8
    y, s = index // 4, index % 4
    at = pl.multiple_of((d ^ (2 * s + y)) * r, r) if relative else index * r
    return scr[pl.ds(at, r), :]


def turn(values, c_ref, scr, turned_ref, j, relative):
    rows, width = values[0].shape
    r = width // 8
    for i in range(2):
        scr[:, i * rows : (i + 1) * rows] = values[i][...].T
    for b in range(8):
        turned_ref[j, b * r : (b + 1) * r, :] = relative_rows(scr, c_ref[1], b, width, relative)


def weight_grad_kernel(first, relative, c_ref, *refs):
    if first:
        c1, c2, gb1, gb2, e1, e2, du1, du2, grad_ref, turned_ref, scr = refs
        turn((c1, c2), c_ref, scr, turned_ref, 0, relative)
        turn((gb1, gb2), c_ref, scr, turned_ref, 1, relative)
    else:
        turned_ref, e1, e2, du1, du2, recv_ref, grad_ref = refs
    rows, units = du1.shape[1:]
    a, b = slice(0, rows), slice(rows, 2 * rows)
    up = dot(turned_ref[0, :, a], du1[0]) + dot(turned_ref[0, :, b], du2[0])
    down = dot(turned_ref[1, :, a], e1[0]) + dot(turned_ref[1, :, b], e2[0])
    if not first:
        up = up + recv_ref[:, 0:units].astype(f32)
        down = down + recv_ref[:, units:].astype(f32)
    grad_ref[:, 0:units] = up.astype(bf)
    grad_ref[:, units:] = down.astype(bf)


def weight_grad_first(scalars, relative, cs, gbs, es, dus):
    rows, width = cs[0].shape
    units = es[0].shape[2]
    ins = [*cs, *gbs, *es, *dus]
    spec = pltpu.PrefetchScalarGridSpec(
        num_scalar_prefetch=1,
        grid=(1,),
        in_specs=[whole((rows, width))] * 4 + [pl.BlockSpec((1, rows, units), lambda i, c: (1, 0, 0))] * 4,
        out_specs=[whole((width, 2 * units)), whole((2, width, 2 * rows))],
        scratch_shapes=[pltpu.VMEM((width, 2 * rows), bf)],
    )
    return pl.pallas_call(
        functools.partial(weight_grad_kernel, True, relative),
        grid_spec=spec,
        out_shape=[SDS((width, 2 * units), bf), SDS((2, width, 2 * rows), bf)],
        compiler_params=params(),
        cost_estimate=cost(5.5),
        name="weight_grad_first",
    )(scalars, *ins)


def weight_grad_second(scalars, turned, es, dus, recv):
    _, width, tokens = turned.shape
    units = es[0].shape[2]
    ins = [turned, *es, *dus, recv]
    spec = pltpu.PrefetchScalarGridSpec(
        num_scalar_prefetch=1,
        grid=(1,),
        in_specs=[whole(turned.shape)] + [pl.BlockSpec((1, tokens // 2, units), lambda i, c: (0, 0, 0))] * 4 + [whole(recv.shape)],
        out_specs=whole((width, 2 * units)),
    )
    return pl.pallas_call(
        functools.partial(weight_grad_kernel, False, False),
        grid_spec=spec,
        out_shape=SDS((width, 2 * units), bf),
        compiler_params=params(),
        cost_estimate=cost(3.2),
        name="weight_grad_second",
    )(scalars, *ins)


def out_grad_kernel(relative, c_ref, dhb1, dhb2, o1, o2, other1, other2, ours_ref, theirs_ref, scr, turned):
    rows = dhb1.shape[0]
    turn((dhb1, dhb2), c_ref, scr, turned, 0, relative)
    a, b = turned[0, :, 0:rows], turned[0, :, rows : 2 * rows]
    theirs_ref[...] = (dot(a, other1[...], NT) + dot(b, other2[...], NT)).astype(bf)
    ours_ref[...] = (dot(a, o1[0], NT) + dot(b, o2[0], NT)).astype(bf)


def out_grad(scalars, relative, dhbs, os, others):
    rows, width = dhbs[0].shape
    local = others[0].shape[0]
    ins = [*dhbs, *os, *others]
    spec = pltpu.PrefetchScalarGridSpec(
        num_scalar_prefetch=1,
        grid=(1,),
        in_specs=[whole(v.shape) for v in ins],
        out_specs=[whole((width, local))] * 2,
        scratch_shapes=[pltpu.VMEM((width, 2 * rows), bf), pltpu.VMEM((1, width, 2 * rows), bf)],
    )
    return pl.pallas_call(
        functools.partial(out_grad_kernel, relative),
        grid_spec=spec,
        out_shape=[SDS((width, local), bf)] * 2,
        compiler_params=params(),
        cost_estimate=cost(2.6),
        name="out_grad",
    )(scalars, *ins)


def attend_back_kernel(part, c_ref, kp_ref, vp_ref, kt_ref, q1_ref, q2_ref, o_ref, lse_ref, do1_ref, do2_ref, *refs):
    if part == 0:
        dq_ref, kv_ref = refs
    else:
        kv_in, dq_ref, out_ref = refs
    q = q1_ref.shape[1]
    one = jnp.ones((1, q), f32)
    zero = jnp.zeros((HD, q), bf)
    blocks = []
    for i, (q_ref, do) in enumerate(((q1_ref, do1_ref[0]), (q2_ref, do2_ref[...]))):
        delta = jnp.sum(do.astype(f32) * o_ref[i].astype(f32), axis=0, keepdims=True)
        queries = with_tail(q_ref[...], [one] + [-v for v in split3(lse_ref[0, i, 0:1])])
        grads = with_tail(do, [0.0 * one] + [-v for v in split3(delta)])
        blocks.append((queries, grads, jnp.concatenate([do, zero], axis=0), jnp.concatenate([zero, q_ref[...]], axis=0)))
    dq = [None] * 2
    for b in range(4):
        at = slice(b * q, (b + 1) * q)
        kv = None if part == 0 else kv_in[0, at, :]
        for i, (queries, grads, do_low, q_high) in enumerate(blocks):
            p = jnp.exp2(dot(kp_ref[at, :], queries) * LOG2E)
            ds = (p * dot(vp_ref[at, :], grads)).astype(bf)
            here = dot(p.astype(bf), do_low, NT) + dot(ds, q_high, NT)
            kv = here if kv is None else kv + here
            here = dot(kt_ref[:, at], ds)
            dq[i] = here if dq[i] is None else dq[i] + here
        if part == 0:
            kv_ref[0, at, :] = kv
        else:
            turned = kv.T.astype(bf)
            other = (b % 2) ^ c_ref[0]
            out_ref[other, b // 2, 0] = turned[HD:]
            out_ref[other, b // 2, 1] = turned[:HD]
    for i in range(2):
        dq_ref[i] = (dq[i] * 0.125).astype(bf)


def attend_back(part, scalars, kp, vp, kt, qt, o, lse, do, do_other, sums=()):
    count = kp.shape[0]
    heads = qt.shape[0] // HD
    q = count // 4
    keyed = pl.BlockSpec((count, 2 * HD), lambda h, c: (0, h))
    pair = pl.BlockSpec((2, HD, q), lambda h, c: (0, h, 0))
    total = pl.BlockSpec((1, count, 2 * HD), lambda h, c: (h, 0, 0))
    dq_shape = SDS((2, heads * HD, q), bf)
    if part == 0:
        out_specs, out_shape = [pair, total], [dq_shape, SDS((heads, count, 2 * HD), f32)]
    else:
        out_specs = [pair, pl.BlockSpec((2, 2, 2, HD, q), lambda h, c: (0, 0, 0, h, 0))]
        out_shape = [dq_shape, SDS((2, 2, 2, heads * HD, q), bf)]
    spec = pltpu.PrefetchScalarGridSpec(
        num_scalar_prefetch=1,
        grid=(heads,),
        in_specs=[
            keyed,
            keyed,
            pl.BlockSpec((HD, count), lambda h, c: (h, 0)),
            pl.BlockSpec((HD, q), lambda h, c: (h, (2 * part) ^ c[0])),
            pl.BlockSpec((HD, q), lambda h, c: (h, (2 * part + 1) ^ c[0])),
            pair,
            pl.BlockSpec((1, 2, 8, q), lambda h, c: (h, 0, 0, 0)),
            pl.BlockSpec((1, HD, q), lambda h, c: (0, h, 0)),
            pl.BlockSpec((HD, q), lambda h, c: (h, 0)),
        ]
        + [total] * len(sums),
        out_specs=out_specs,
    )
    return pl.pallas_call(
        functools.partial(attend_back_kernel, part),
        grid_spec=spec,
        out_shape=out_shape,
        compiler_params=params(),
        cost_estimate=cost(18),
        name=f"attend_back{part}",
    )(scalars, kp, vp, kt, qt, qt, o, lse, do, do_other, *sums)


def da_kernel(pieces, c_ref, dq1, dq2, dkv, rq1, rq2, rkv, x1_ref, x2_ref, *refs):
    mine, theirs = refs[:pieces], refs[pieces : 2 * pieces]
    one_ref, two_ref, sum_ref, w_scr, d_scr, sem = refs[2 * pieces :]
    width = one_ref.shape[0]
    local = rq1.shape[0]
    for k, group in enumerate((mine, theirs)):
        for copy in row_copies(group, c_ref[1], width, w_scr.at[k], slice(0, w_scr.shape[2]), sem.at[k]):
            copy.start()
    for i in range(2):
        own, other = (dq1, dq2)[i], (rq1, rq2)[i]
        d_scr[i, 0, 0:local, :] = own[0]
        d_scr[i, 1, 0:local, :] = other[...]
        for j in range(2):
            at = slice((j + 1) * local, (j + 2) * local)
            d_scr[i, 0, at, :] = dkv[0, i, j]
            d_scr[i, 1, at, :] = rkv[i, j]
    for k in range(2):
        wait_for(w_scr.at[k], sem.at[k])
    sums = [jnp.zeros((1, width), f32)] * 2
    at = slice(0, 3 * local)
    for i, (da_ref, x_ref) in enumerate(((one_ref, x1_ref), (two_ref, x2_ref))):
        da = (dot(w_scr[0, :, at], d_scr[i, 0]) + dot(w_scr[1, :, at], d_scr[i, 1])).astype(bf)
        da_ref[...] = da
        n1, _ = normalize(x_ref[...].astype(f32))
        da = da.astype(f32).T
        sums = [sums[0] + jnp.sum(da * n1, axis=0, keepdims=True), sums[1] + jnp.sum(da, axis=0, keepdims=True)]
    sum_ref[0:1, :], sum_ref[1:2, :] = sums
    sum_ref[2:8, :] = jnp.zeros((6, width), f32)


def da_product(scalars, dq1, dq2, dkv, rq1, rq2, rkv, x, mine, theirs):
    local, q = rq1.shape
    width = x.shape[1]
    packed = mine[0].shape[-1]
    ins = [dq1, dq2, dkv, rq1, rq2, rkv]
    spec = pltpu.PrefetchScalarGridSpec(
        num_scalar_prefetch=1,
        grid=(1,),
        in_specs=[whole(v.shape) for v in ins]
        + [pl.BlockSpec((q, width), lambda i, c: (c[0], 0)), pl.BlockSpec((q, width), lambda i, c: (2 ^ c[0], 0))]
        + [ANY] * (2 * len(mine)),
        out_specs=[whole((width, q))] * 2 + [whole((8, width))],
        scratch_shapes=[pltpu.VMEM((2, width, packed), bf), pltpu.VMEM((2, 2, 3 * local, q), bf), pltpu.SemaphoreType.DMA((2,))],
    )
    return pl.pallas_call(
        functools.partial(da_kernel, len(mine)),
        grid_spec=spec,
        out_shape=[SDS((width, q), bf)] * 2 + [SDS((8, width), f32)],
        compiler_params=params(),
        cost_estimate=cost(5.4),
        name="da_product",
    )(scalars, *ins, x, x, *mine, *theirs)


def dx_kernel(c_ref, own_ref, recv_ref, x_ref, dh_ref, norm_ref, dx_ref):
    da = (own_ref[...].astype(f32) + recv_ref[...].astype(f32)).T
    n1, r1 = normalize(x_ref[...].astype(f32))
    dx_ref[...] = (dh_ref[...] + norm_back(da, n1, r1, norm_ref[0:1, :])).astype(bf)


def dx_block(part, scalars, own, recv, x, dh, norms):
    width, rows = own.shape
    spec = pltpu.PrefetchScalarGridSpec(
        num_scalar_prefetch=1,
        grid=(1,),
        in_specs=[whole(own.shape)] * 2
        + [pl.BlockSpec((rows, width), lambda i, c: ((2 * part) ^ c[0], 0)), whole(dh.shape), whole(norms.shape)],
        out_specs=whole((rows, width)),
    )
    return pl.pallas_call(
        dx_kernel,
        grid_spec=spec,
        out_shape=SDS((rows, width), bf),
        compiler_params=params(),
        cost_estimate=cost(2),
        name=f"dx{part}",
    )(scalars, own, recv, x, dh, norms)


def qkv_grad_kernel(relative, c_ref, a_ref, dq1, dq2, dkv, out1, out2, sum_ref, grad_ref, g_scr):
    local, q = dq1.shape[1:]
    width = a_ref.shape[1]
    total = [None] * 3
    for m in range(4):
        a = a_ref[m * q : (m + 1) * q, :]
        parts = [(dq1, dq2)[m // 2][m % 2], dkv[m % 2, m // 2, 0], dkv[m % 2, m // 2, 1]]
        for j in range(3):
            here = dot(parts[j], a)
            total[j] = here if total[j] is None else total[j] + here
    for j in range(3):
        g_scr[:, j * local : (j + 1) * local] = total[j].T.astype(bf)
    tall = jnp.concatenate([sum_ref[...], jnp.zeros((120, width), f32)], axis=0)
    g_scr[:, 4 * local : 4 * local + 128] = tall.T.astype(bf)
    r = width // 8
    for b in range(8):
        rows = relative_rows(g_scr, c_ref[1], b, width, relative)
        grad_ref[b * r : (b + 1) * r, local : 4 * local] = rows[:, 0 : 3 * local]
        grad_ref[b * r : (b + 1) * r, 4 * local :] = rows[:, 4 * local :]
    grad_ref[:, 0:local] = (out1[...].astype(f32) + out2[...].astype(f32)).astype(bf)


def qkv_grad(scalars, relative, normed, dq1, dq2, dkv, out1, out2, sums):
    width = normed.shape[1]
    local = dq1.shape[1]
    ins = [normed, dq1, dq2, dkv, out1, out2, sums]
    spec = pltpu.PrefetchScalarGridSpec(
        num_scalar_prefetch=1,
        grid=(1,),
        in_specs=[whole(v.shape) for v in ins],
        out_specs=whole((width, 4 * local + 128)),
        scratch_shapes=[pltpu.VMEM((width, 4 * local + 128), bf)],
    )
    return pl.pallas_call(
        functools.partial(qkv_grad_kernel, relative),
        grid_spec=spec,
        out_shape=SDS((width, 4 * local + 128), bf),
        compiler_params=params(),
        cost_estimate=cost(4.2),
        name="qkv_grad",
    )(scalars, *ins)


def gather_z(piece, n):
    return [piece] + [swap(piece, "dp", 2 * s, n) for s in (1, 2, 3)]


def gather_y(pieces, n):
    along_z = jnp.stack(pieces)
    return [in_hbm(along_z), in_hbm(swap(along_z, "dp", 1, n))]


def scatter_y(value, n):
    if n != 8:
        return value
    half = value.shape[0] // 2
    return (value[:half].astype(f32) + swap(value[half:], "dp", 1, n).astype(f32)).astype(bf)


def scatter_far(half, n):
    if n != 8:
        return half
    half, send = jnp.split(half, 2)
    return (half.astype(f32) + swap(send, "dp", 4, n).astype(f32)).astype(bf)


def scatter_near(part, n):
    if n != 8:
        return [lax.psum_scatter(part, "dp", scatter_dimension=0, tiled=True)]
    return [part, swap(part[part.shape[0] // 2 :], "dp", 2, n)]


def scatter_z(half, n):
    if n != 8:
        return [lax.psum_scatter(half, "dp", scatter_dimension=0, tiled=True)]
    r = half.shape[0] // 4
    return [half] + [swap(half[s * r : (s + 1) * r], "dp", 2 * s, n) for s in (1, 2, 3)]


def finish_kernel(pieces, local, *refs):
    outs = refs[pieces:]
    total = refs[0][...].astype(f32)
    for piece in refs[1:pieces]:
        total = total + piece[...].astype(f32)
    if len(outs) == 2:
        units = outs[0].shape[1]
        outs[0][...] = total[:, 0:units]
        outs[1][...] = total[:, units:].T
    else:
        outs[0][...] = total[:, 0 : 2 * local].T[0:local]
        for j in range(3):
            outs[1][j] = total[:, (j + 1) * local : (j + 2) * local]
        outs[2][...] = total[:, 4 * local :]


def finish(name, pieces, shapes, local):
    block = whole((shapes[0][0] if len(shapes) == 2 else shapes[2][0], pieces[0].shape[1]))
    return pl.pallas_call(
        functools.partial(finish_kernel, len(pieces), local),
        grid=(1,),
        in_specs=[block] * len(pieces),
        out_specs=[whole(v) for v in shapes],
        out_shape=[SDS(v, f32) for v in shapes],
        compiler_params=params(),
        cost_estimate=cost(1.5),
        name=name,
    )(*pieces)


def assemble_kernel(c_ref, *refs):
    arrays, (out_ref, sem) = refs[:-2], refs[-2:]
    rows = arrays[0].shape[-2]
    copies = []
    for m in range(4):
        at = pl.multiple_of((m ^ c_ref[0]) * rows, rows)
        block = arrays[m % 2].at[m // 2] if len(arrays) == 2 else arrays[m]
        copies.append(pltpu.make_async_copy(block, out_ref.at[pl.ds(at, rows), :], sem.at[m]))
    for copy in copies:
        copy.start()
    for copy in copies:
        copy.wait()


def assemble(scalars, *arrays):
    rows, width = arrays[0].shape[-2:]
    spec = pltpu.PrefetchScalarGridSpec(
        num_scalar_prefetch=1,
        grid=(1,),
        in_specs=[pl.BlockSpec(memory_space=pltpu.VMEM)] * len(arrays),
        out_specs=pl.BlockSpec(memory_space=pl.ANY),
        scratch_shapes=[pltpu.SemaphoreType.DMA((4,))],
    )
    return pl.pallas_call(
        assemble_kernel,
        grid_spec=spec,
        out_shape=SDS((4 * rows, width), bf),
        compiler_params=params(),
        cost_estimate=cost(2.2),
        name="assemble",
    )(scalars, *arrays)


def mix_kernel(c_ref, h1_ref, h2_ref, own_ref, recv_ref, out_ref):
    for i, h_ref in enumerate((h1_ref, h2_ref)):
        out_ref[i] = (h_ref[...] + (own_ref[i].astype(f32) + recv_ref[i].astype(f32))).astype(bf)


def mix(scalars, h, own, recv):
    spec = pltpu.PrefetchScalarGridSpec(
        num_scalar_prefetch=1,
        grid=(1,),
        in_specs=[whole(h[0].shape)] * 2 + [whole(own.shape)] * 2,
        out_specs=whole(own.shape),
    )
    return pl.pallas_call(
        mix_kernel,
        grid_spec=spec,
        out_shape=SDS(own.shape, bf),
        compiler_params=params(),
        cost_estimate=cost(2),
        name="mix",
    )(scalars, *h, own, recv)


def body(n, embeddings, cotangent, species, gene_ids, w_qkv, w_out, w_up, w_down, norm_gains, norm_shifts):
    c = lax.axis_index("tensor") % 2
    d = lax.axis_index("dp")
    relative = n == 8
    count, width = embeddings.shape
    r = width // n
    local = w_qkv.shape[2]
    units = w_up.shape[1]
    length = jnp.sum((gene_ids != 0).astype(jnp.int32))
    alive = jnp.where(species[0] == 2, 0, length)
    scalars = jnp.stack([c, d, length, alive]).astype(jnp.int32)

    norms_own = jnp.concatenate([norm_gains, norm_shifts]).T
    packed = jnp.concatenate([w_qkv[0], w_qkv[1], w_qkv[2], jnp.pad(norms_own, ((0, 0), (0, 60)))], axis=1).astype(bf)
    pad = ((0, 0), (0, 256 - local))
    if relative:
        w_first = gather_y(gather_z(packed, n), n)
        w_out, w_up = after((w_out, w_up), w_first[0])
        out_up_z = gather_z(jnp.concatenate([jnp.pad(w_out.T, pad), w_up], axis=1).astype(bf), n)
    else:
        rows = lambda v: [lax.all_gather(v.astype(bf), "dp", axis=0, tiled=True)]
        w_first, w_o, w_u, w_d = rows(packed), rows(jnp.pad(w_out.T, pad)), rows(w_up), rows(w_down.T)
    others = lambda group: [in_hbm(core_swap(v)) for v in group]

    normed, kp, vp, kt, vt, qt, norm_rows = project(scalars, embeddings, w_first, local)
    if relative:
        out_up_z, w_down = after((out_up_z, w_down), norm_rows)
        w_o = gather_y([v[:, :256] for v in out_up_z], n)
        w_u = gather_y([v[:, 256:] for v in out_up_z], n)
        down_z = gather_z(w_down.astype(bf).T, n)
    o, lse, o_other, h, cs, gbs, es, dus, ffns, dcs = ([None] * 2 for _ in range(10))
    sent = [None] * 2
    o[0], lse[0] = attend(scalars, kp, vt, qt, 0)
    o_other[0] = core_swap(o[0][1])
    w_o2 = others(after(w_o, lse[0]))
    w_u = after(w_u, lse[0])
    w_u2 = others(w_u)
    sent[0] = out_product(after(scalars, w_u, down_z) if relative else scalars, o[0], o_other[0], w_o, w_o2, width)
    if relative:
        w_d = gather_y(after(down_z, sent[0]), n)
    o[1], lse[1] = attend(after(scalars, sent[0]), kp, vt, qt, 1)
    o_other[1] = core_swap(o[1][1])
    recv0 = x_swap(sent[0])
    sent[1] = out_product(after(scalars, recv0), o[1], o_other[1], w_o, w_o2, width)
    w_d2 = others(after(w_d, sent[1]))
    last = after(scalars, sent[1])
    for i in range(2):
        recv = x_swap(sent[1]) if i else recv0
        before = (ffns,) if i else ()
        h[i], cs[i], gbs[i], es[i], dus[i], dcs[i], ffns = ffn(
            i, last, embeddings, cotangent, sent[i], recv, norm_rows, w_u, w_d, w_u2, w_d2, units, before
        )
        last = after(scalars, dcs[i])
    dh, dhb, do, do_other, sums = ([None] * 2 for _ in range(5))
    i = 0
    dh[i], dhb[i], do[i], sums[i] = middle(i, last, h[i], dcs[i], x_swap(dcs[i]), cotangent, norm_rows, w_o, w_o2, local)
    recv_ffn = x_swap(after(ffns, do[0]))
    do_other[i] = core_swap(do[i][1])
    last = after(scalars, dhb[0])
    grad_theirs, turned = weight_grad_first(last, relative, cs, gbs, es, dus)
    grad_ours = weight_grad_second(after(scalars,turned), turned, es, dus, core_swap(grad_theirs))
    last = after(scalars, grad_ours)
    dq1, dkv1 = attend_back(0, last, kp, vp, kt, qt, o[0], lse[0], do[0], do_other[0])
    last = after(scalars, dq1)
    i = 1
    dh[i], dhb[i], do[i], sums[i] = middle(i, last, h[i], dcs[i], x_swap(dcs[i]), cotangent, norm_rows, w_o, w_o2, local)
    do_other[i] = core_swap(do[i][1])
    last = after(scalars, dhb[1])
    out_ours, out_theirs = out_grad(last, relative, dhb, o, o_other)
    half_ours = scatter_y(grad_ours, n)
    last = after(scalars, out_ours, half_ours)
    dq2, dkv = attend_back(1, last, kp, vp, kt, qt, o[1], lse[1], do[1], do_other[1], (dkv1,))
    rest_far = scatter_far(half_ours, n)

    rq1, rq2, rkv = core_swap(dq1[1]), core_swap(dq2[1]), core_swap(dkv[1])
    w_first2 = others(w_first)
    last = after(scalars, recv_ffn)
    da0, da1, sums1 = da_product(last, dq1, dq2, dkv, rq1, rq2, rkv, embeddings, w_first, w_first2)
    last = after(scalars, da0)
    grad_first = qkv_grad(last, relative, normed, dq1, dq2, dkv, out_ours, core_swap(out_theirs), sums1 + 0.5 * (sums[0] + sums[1]))
    half_first = scatter_y(grad_first, n)
    mixed = mix(after(scalars, grad_first), h, ffns, recv_ffn)
    mixed_other = core_swap(mixed)
    dx0 = dx_block(0, after(scalars, mixed), da0, x_swap(da0), embeddings, dh[0], norm_rows)

    rest_far, half_first = after((rest_far, half_first), dx0)
    rest_z = scatter_near(rest_far, n)
    first_z = scatter_z(half_first, n)
    mixed = assemble(after(scalars, rest_far, half_first), mixed, mixed_other)
    dx1 = dx_block(1, after(scalars, mixed), da1, x_swap(da1), embeddings, dh[1], norm_rows)
    s_up, s_down = finish("finish_rest", after(rest_z, dx1), [(r, units), (units, r)], local)
    grad_input = assemble(scalars, dx0, core_swap(dx0), dx1, core_swap(dx1))
    s_out, s_qkv, both = finish("finish_first", after(first_z, dx1), [(local, r), (3, r, local), (r, 128)], local)
    both = both[:, :4]
    both = both + core_swap(both)
    both = (both + x_swap(both)).T
    gains = jnp.stack([both[0], both[2]])
    shifts = jnp.stack([both[1], both[3]])
    return (mixed, grad_input, s_qkv, s_out, s_up, s_down, gains, shifts, both[3])


def solution(mesh):
    return jax.shard_map(
        functools.partial(body, mesh.shape["dp"]),
        mesh=mesh,
        in_specs=(
            P("dp", None),
            P("dp", None),
            P("dp"),
            P("dp", None),
            P(None, "dp", "tensor"),
            P("tensor", "dp"),
            P("dp", "tensor"),
            P("tensor", "dp"),
            P(None, "dp"),
            P(None, "dp"),
        ),
        out_specs=(
            P("dp", None),
            P("dp", None),
            P(None, "dp", "tensor"),
            P("tensor", "dp"),
            P("dp", "tensor"),
            P("tensor", "dp"),
            P(None, "dp"),
            P(None, "dp"),
            P("dp"),
        ),
        check_vma=False,
    )
```

```python
import functools
import math

import jax
import jax.numpy as jnp
from jax import lax
from jax.experimental import pallas as pl
from jax.experimental.pallas import tpu as pltpu
from jax.sharding import PartitionSpec as P

HD = 64
EPSILON = 1e-05
NEGATIVE = -1e30
LOG2E = math.log2(math.e)
bf = jnp.bfloat16
f32 = jnp.float32
NN = ((1,), (0,))
NT = ((1,), (1,))
ANY = pl.BlockSpec(memory_space=pltpu.HBM)
SDS = jax.ShapeDtypeStruct


def dot(a, b, dims=NN):
    return lax.dot_general(a, b, (dims, ((), ())), preferred_element_type=f32)


def swap(value, axis, mask, size):
    return lax.ppermute(value, axis, [(i, i ^ mask) for i in range(size)])


def core_swap(value):
    return swap(value, "tensor", 1, 4)


def x_swap(value):
    return swap(value, "tensor", 2, 4)


def in_hbm(value):
    return pltpu.with_memory_space_constraint(value, pltpu.HBM)


def after(value, *others):
    return lax.optimization_barrier((value,) + others)[0]


def params(mib=32):
    return pltpu.CompilerParams(vmem_limit_bytes=mib << 20)


SCALE = 0.001


def cost(us):
    return pl.CostEstimate(flops=int(us * SCALE * 1.15e9), bytes_accessed=int(us * SCALE * 1e6), transcendentals=0)


def whole(shape):
    return pl.BlockSpec(shape, lambda *_: (0,) * len(shape))


def row_copies(refs, d, count, dst, columns, sem):
    copies = []
    if len(refs) == 1 and len(refs[0].shape) == 4:
        refs = [refs[0].at[0], refs[0].at[1]]
    elif len(refs) == 1:
        copies.append(pltpu.make_async_copy(refs[0].at[:, columns], dst, sem))
        return copies
    r = count // 8
    for y, ref in enumerate(refs):
        for s in range(4):
            at = pl.multiple_of((d ^ (2 * s + y)) * r, r)
            copies.append(pltpu.make_async_copy(ref.at[s, 0:r, columns], dst.at[pl.ds(at, r), :], sem))
    return copies


def wait_for(dst, sem):
    pltpu.make_async_copy(dst, dst, sem).wait()


def split3(v):
    a = v.astype(bf)
    rest = v - a.astype(f32)
    b = rest.astype(bf)
    c = (rest - b.astype(f32)).astype(bf)
    return [a.astype(f32), b.astype(f32), c.astype(f32)]


def with_tail(block, rows):
    q = block.shape[1]
    index = lax.broadcasted_iota(jnp.int32, (HD, q), 0)
    tail = jnp.zeros((HD, q), f32)
    for i, row in enumerate(rows):
        tail = jnp.where(index == i, row, tail)
    return jnp.concatenate([block, tail.astype(bf)], axis=0)


def normalize(v):
    center = v - jnp.mean(v, axis=-1, keepdims=True)
    variance = jnp.mean(center * center, axis=-1, keepdims=True)
    r = lax.rsqrt(variance + EPSILON)
    return center * r, r


def norm_back(dn, n, r, gain):
    scaled = dn * gain
    return r * (scaled - jnp.mean(scaled, axis=-1, keepdims=True) - n * jnp.mean(scaled * n, axis=-1, keepdims=True))


def project_kernel(heads, pieces, c_ref, x_ref, *refs):
    w_refs = refs[:pieces]
    a_ref, kp_ref, vp_ref, kt_ref, vt_ref, qt_ref, norm_ref, w_scr, wt_scr, wk_scr, wv_scr, sem = refs[pieces:]
    step = pl.program_id(0)
    rows, width = x_ref.shape
    local = HD * heads

    @pl.when(step == 0)
    def _():
        for copy in row_copies(w_refs, c_ref[1], width, w_scr, slice(0, w_scr.shape[1]), sem):
            copy.start()
        wait_for(w_scr, sem)
        wt_scr[...] = w_scr[...].T
        norm_ref[...] = wt_scr[3 * local : 3 * local + 16, :].astype(f32)[0:8]
        zero = jnp.zeros((width, HD), bf)
        for h in range(heads):
            at = slice(2 * HD * h, 2 * HD * (h + 1))
            wk_scr[:, at] = jnp.concatenate([w_scr[:, local + HD * h : local + HD * (h + 1)], zero], axis=1)
            wv_scr[:, at] = jnp.concatenate([w_scr[:, 2 * local + HD * h : 2 * local + HD * (h + 1)], zero], axis=1)

    n, _ = normalize(x_ref[...].astype(f32))
    a = (n * norm_ref[0:1, :] + norm_ref[2:3, :]).astype(bf)
    a_ref[...] = a
    token = (step ^ c_ref[0]) * rows + lax.broadcasted_iota(jnp.int32, (rows, 2 * local), 0)
    lane = lax.broadcasted_iota(jnp.int32, (rows, 2 * local), 1) % (2 * HD)
    ones = jnp.where((lane > HD) & (lane < HD + 4), 1.0, 0.0)
    bias = jnp.where((lane == HD) & (token >= c_ref[2]), NEGATIVE, ones)
    kp_ref[...] = (dot(a, wk_scr[...]) + bias).astype(bf)
    vp_ref[...] = (dot(a, wv_scr[...]) + ones).astype(bf)
    both = dot(wt_scr[0 : 3 * local, :], a, NT)
    qt_ref[...] = (both[0:local] * 0.125).astype(bf)
    kt_ref[...] = both[local : 2 * local].astype(bf)
    vt_ref[...] = both[2 * local : 3 * local].astype(bf)


def project(scalars, x, w, local):
    count, width = x.shape
    heads = local // HD
    rows = count // 4
    packed = w[0].shape[-1]
    block = lambda i, c: (i ^ c[0], 0)
    turned = lambda i, c: (0, i ^ c[0])
    spec = pltpu.PrefetchScalarGridSpec(
        num_scalar_prefetch=1,
        grid=(4,),
        in_specs=[pl.BlockSpec((rows, width), block)] + [ANY] * len(w),
        out_specs=[
            pl.BlockSpec((rows, width), lambda i, c: (i, 0)),
            pl.BlockSpec((rows, 2 * local), block),
            pl.BlockSpec((rows, 2 * local), block),
            pl.BlockSpec((local, rows), turned),
            pl.BlockSpec((local, rows), turned),
            pl.BlockSpec((local, rows), turned),
            whole((8, width)),
        ],
        scratch_shapes=[
            pltpu.VMEM((width, packed), bf),
            pltpu.VMEM((packed, width), bf),
            pltpu.VMEM((width, 2 * local), bf),
            pltpu.VMEM((width, 2 * local), bf),
            pltpu.SemaphoreType.DMA,
        ],
    )
    return pl.pallas_call(
        functools.partial(project_kernel, heads, len(w)),
        grid_spec=spec,
        out_shape=[SDS((count, width), bf), SDS((count, 2 * local), bf), SDS((count, 2 * local), bf)]
        + [SDS((local, count), bf)] * 3
        + [SDS((8, width), f32)],
        compiler_params=params(),
        cost_estimate=cost(10),
        name="project",
    )(scalars, x, *w)


def attend_kernel(chunk, c_ref, kp_ref, kp_next, vt_ref, q1_ref, q2_ref, q1_next, o_ref, lse_ref, a_scr, b_scr, top_scr):
    keys = kp_ref.shape[0]
    q = q1_ref.shape[1]
    spans = [slice(i * chunk, (i + 1) * chunk) for i in range(keys // chunk)]
    one = [jnp.ones((1, q), f32)]

    def scores(k_ref, queries, at, scr, top):
        s = dot(k_ref[at, :], queries)
        scr[at, :] = s
        here = jnp.max(s, axis=0, keepdims=True)
        return here if top is None else jnp.maximum(top, here)

    @pl.when(pl.program_id(0) == 0)
    def _():
        queries = with_tail(q1_ref[...], one)
        top = None
        for at in spans:
            top = scores(kp_ref, queries, at, a_scr, top)
        top_scr[...] = jnp.broadcast_to(top, (8, q))

    before = top_scr[0:1, :]
    turns = ((0, a_scr, b_scr, kp_ref, q2_ref), (1, b_scr, a_scr, kp_next, q1_next))
    for i, ready, filling, k_ref, q_ref in turns:
        queries = with_tail(q_ref[...], one)
        top = total = out = None
        for at in spans:
            top = scores(k_ref, queries, at, filling, top)
            p = jnp.exp2((ready[at, :] - before) * LOG2E)
            here = jnp.sum(p, axis=0, keepdims=True)
            part = dot(vt_ref[:, at], p.astype(bf))
            total = here if total is None else total + here
            out = part if out is None else out + part
        o_ref[i] = (out / total).astype(bf)
        lse_ref[0, i] = jnp.broadcast_to(before + jnp.log(total), (8, q))
        before = top
    top_scr[...] = jnp.broadcast_to(before, (8, q))


def attend(scalars, kp, vt, qt, part):
    count = kp.shape[0]
    heads = qt.shape[0] // HD
    q = count // 4
    follow = lambda h: jnp.minimum(h + 1, heads - 1)
    spec = pltpu.PrefetchScalarGridSpec(
        num_scalar_prefetch=1,
        grid=(heads,),
        in_specs=[
            pl.BlockSpec((count, 2 * HD), lambda h, c: (0, h)),
            pl.BlockSpec((count, 2 * HD), lambda h, c: (0, follow(h))),
            pl.BlockSpec((HD, count), lambda h, c: (h, 0)),
            pl.BlockSpec((HD, q), lambda h, c: (h, (2 * part) ^ c[0])),
            pl.BlockSpec((HD, q), lambda h, c: (h, (2 * part + 1) ^ c[0])),
            pl.BlockSpec((HD, q), lambda h, c: (follow(h), (2 * part) ^ c[0])),
        ],
        out_specs=[
            pl.BlockSpec((2, HD, q), lambda h, c: (0, h, 0)),
            pl.BlockSpec((1, 2, 8, q), lambda h, c: (h, 0, 0, 0)),
        ],
        scratch_shapes=[pltpu.VMEM((count, q), f32), pltpu.VMEM((count, q), f32), pltpu.VMEM((8, q), f32)],
    )
    return pl.pallas_call(
        functools.partial(attend_kernel, min(512, count)),
        grid_spec=spec,
        out_shape=[SDS((2, heads * HD, q), bf), SDS((heads, 2, 8, q), f32)],
        compiler_params=params(),
        cost_estimate=cost(10),
        name=f"attend{part}",
    )(scalars, kp, kp, vt, qt, qt, qt)


def out_kernel(pieces, c_ref, o_ref, other_ref, *refs):
    mine, theirs, (part_ref, w_scr, sem) = refs[:pieces], refs[pieces : 2 * pieces], refs[2 * pieces :]
    width = part_ref.shape[0]
    for k, group in enumerate((mine, theirs)):
        for copy in row_copies(group, c_ref[1], width, w_scr.at[k], slice(0, 256), sem.at[k]):
            copy.start()
    local = o_ref.shape[1]
    wait_for(w_scr.at[0], sem.at[0])
    part = dot(w_scr[0, :, 0:local], o_ref[0])
    wait_for(w_scr.at[1], sem.at[1])
    part_ref[...] = (part + dot(w_scr[1, :, 0:local], other_ref[...])).astype(bf)


def out_product(scalars, o, other, mine, theirs, width):
    local, q = other.shape
    spec = pltpu.PrefetchScalarGridSpec(
        num_scalar_prefetch=1,
        grid=(1,),
        in_specs=[whole(o.shape), whole(other.shape)] + [ANY] * (2 * len(mine)),
        out_specs=whole((width, q)),
        scratch_shapes=[pltpu.VMEM((2, width, 256), bf), pltpu.SemaphoreType.DMA((2,))],
    )
    return pl.pallas_call(
        functools.partial(out_kernel, len(mine)),
        grid_spec=spec,
        out_shape=SDS((width, q), bf),
        compiler_params=params(),
        cost_estimate=cost(2.2),
        name="out_product",
    )(scalars, o, other, *mine, *theirs)


def ffn_kernel(part, pieces, steps, c_ref, x_ref, g_ref, own_ref, recv_ref, norm_ref, *refs):
    groups = [refs[i * pieces : (i + 1) * pieces] for i in range(4)]
    h_ref, c_out, gb_ref, e_ref, du_ref, dc_ref, ffn_ref, w_scr, sem = refs[4 * pieces + part :]
    step = pl.program_id(0)
    rows, width = x_ref.shape
    units = e_ref.shape[2]

    @pl.when(step == 0)
    def _():
        for j, group in enumerate(groups):
            for copy in row_copies(group, c_ref[1], width, w_scr.at[j], slice(0, units), sem.at[j]):
                copy.start()

    h = x_ref[...].astype(f32) + (own_ref[...].astype(f32) + recv_ref[...].astype(f32)).T
    h_ref[...] = h
    n2, _ = normalize(h)
    c = (n2 * norm_ref[1:2, :] + norm_ref[3:4, :]).astype(bf)
    c_out[...] = c
    token = (((2 * part) ^ c_ref[0]) * steps + step) * rows + lax.broadcasted_iota(jnp.int32, (rows, 1), 0)
    gb = jnp.where(token < c_ref[3], g_ref[...].astype(f32), 0.0).astype(bf)
    gb_ref[...] = gb

    @pl.when(step == 0)
    def _():
        for j in range(4):
            wait_for(w_scr.at[j], sem.at[j])

    u = [dot(c, w_scr[2 * k]) for k in range(2)]
    de = [dot(gb, w_scr[2 * k + 1]) for k in range(2)]
    ffn = dc = None
    for k in range(2):
        phi = 0.5 * (1.0 + lax.erf(u[k] * math.sqrt(0.5)))
        e = (u[k] * phi).astype(bf)
        e_ref[k] = e
        du = (de[k] * (phi + u[k] * jnp.exp(-0.5 * u[k] * u[k]) * (1.0 / math.sqrt(2.0 * math.pi)))).astype(bf)
        du_ref[k] = du
        one, two = dot(du, w_scr[2 * k], NT), dot(e, w_scr[2 * k + 1], NT)
        dc = one if dc is None else dc + one
        ffn = two if ffn is None else ffn + two
    dc_ref[...] = dc.astype(bf)
    ffn_ref[0] = ffn.astype(bf)


def ffn(part, scalars, x, g, own, recv, norms, up, down, up_other, down_other, units, before=(), steps=2):
    width, count = own.shape
    rows = count // steps
    token_block = pl.BlockSpec((rows, width), lambda i, c: (((2 * part) ^ c[0]) * steps + i, 0))
    turned = pl.BlockSpec((width, rows), lambda i, c: (0, i))
    block = pl.BlockSpec((rows, width), lambda i, c: (i, 0))
    unit_block = pl.BlockSpec((2, rows, units), lambda i, c: (0, i, 0))
    weights = [*up, *down, *up_other, *down_other]
    spec = pltpu.PrefetchScalarGridSpec(
        num_scalar_prefetch=1,
        grid=(steps,),
        in_specs=[token_block, token_block, turned, turned, whole(norms.shape)] + [ANY] * len(weights) + [pl.BlockSpec(memory_space=pl.ANY)] * part,
        out_specs=[block, block, block, unit_block, unit_block, block, pl.BlockSpec((1, rows, width), lambda i, c: (part, i, 0))],
        scratch_shapes=[pltpu.VMEM((4, width, units), bf), pltpu.SemaphoreType.DMA((4,))],
    )
    return pl.pallas_call(
        functools.partial(ffn_kernel, part, len(up), steps),
        grid_spec=spec,
        out_shape=[SDS((count, width), f32), SDS((count, width), bf), SDS((count, width), bf)]
        + [SDS((2, count, units), bf)] * 2
        + [SDS((count, width), bf), SDS((2, count, width), bf)],
        input_output_aliases={6 + len(weights): 6} if part else {},
        compiler_params=params(),
        cost_estimate=cost(10),
        name=f"ffn{part}",
    )(scalars, x, g, own, recv, norms, *weights, *before)


def middle_kernel(part, pieces, steps, c_ref, h_ref, own_ref, recv_ref, g_ref, norm_ref, *refs):
    mine, theirs = refs[:pieces], refs[pieces : 2 * pieces]
    dh_ref, dhb_ref, do_ref, sum_ref, w_scr, sem = refs[2 * pieces :]
    step = pl.program_id(0)
    rows, width = h_ref.shape
    local = do_ref.shape[1]

    @pl.when(step == 0)
    def _():
        sum_ref[...] = jnp.zeros((8, width), f32)
        for k, group in enumerate((mine, theirs)):
            for copy in row_copies(group, c_ref[1], width, w_scr.at[k], slice(0, 256), sem.at[k]):
                copy.start()

    n2, r2 = normalize(h_ref[...])
    dc = own_ref[...].astype(f32) + recv_ref[...].astype(f32)
    token = (((2 * part) ^ c_ref[0]) * steps + step) * rows + lax.broadcasted_iota(jnp.int32, (rows, 1), 0)
    g = jnp.where(token < c_ref[3], g_ref[...].astype(f32), 0.0)
    dh = g + norm_back(dc, n2, r2, norm_ref[1:2, :])
    dh_ref[...] = dh
    dhb = dh.astype(bf)
    dhb_ref[...] = dhb
    sum_ref[2:3, :] += jnp.sum(dc * n2, axis=0, keepdims=True)
    sum_ref[3:4, :] += jnp.sum(dc, axis=0, keepdims=True)

    @pl.when(step == 0)
    def _():
        for k in range(2):
            wait_for(w_scr.at[k], sem.at[k])

    for k in range(2):
        do_ref[k] = dot(dhb, w_scr[k]).T[0:local].astype(bf)


def middle(part, scalars, h, own, recv, g, norms, mine, theirs, local, steps=2):
    count, width = h.shape
    rows = count // steps
    block = pl.BlockSpec((rows, width), lambda i, c: (i, 0))
    spec = pltpu.PrefetchScalarGridSpec(
        num_scalar_prefetch=1,
        grid=(steps,),
        in_specs=[block] * 3 + [pl.BlockSpec((rows, width), lambda i, c: (((2 * part) ^ c[0]) * steps + i, 0)), whole(norms.shape)] + [ANY] * (2 * len(mine)),
        out_specs=[block, block, pl.BlockSpec((2, local, rows), lambda i, c: (0, 0, i)), whole((8, width))],
        scratch_shapes=[pltpu.VMEM((2, width, 256), bf), pltpu.SemaphoreType.DMA((2,))],
    )
    return pl.pallas_call(
        functools.partial(middle_kernel, part, len(mine), steps),
        grid_spec=spec,
        out_shape=[SDS(h.shape, f32), SDS(h.shape, bf), SDS((2, local, count), bf), SDS((8, width), f32)],
        compiler_params=params(),
        cost_estimate=cost(3.5),
        name=f"middle{part}",
    )(scalars, h, own, recv, g, norms, *mine, *theirs)


def relative_rows(scr, d, index, count, relative):
    r = count // 8
    y, s = index // 4, index % 4
    at = pl.multiple_of((d ^ (2 * s + y)) * r, r) if relative else index * r
    return scr[pl.ds(at, r), :]


def turn(values, c_ref, scr, turned_ref, j, relative):
    rows, width = values[0].shape
    r = width // 8
    for i in range(2):
        scr[:, i * rows : (i + 1) * rows] = values[i][...].T
    for b in range(8):
        turned_ref[j, b * r : (b + 1) * r, :] = relative_rows(scr, c_ref[1], b, width, relative)


def weight_grad_kernel(first, relative, c_ref, *refs):
    if first:
        c1, c2, gb1, gb2, e1, e2, du1, du2, grad_ref, turned_ref, scr = refs
        turn((c1, c2), c_ref, scr, turned_ref, 0, relative)
        turn((gb1, gb2), c_ref, scr, turned_ref, 1, relative)
    else:
        turned_ref, e1, e2, du1, du2, recv_ref, grad_ref = refs
    rows, units = du1.shape[1:]
    a, b = slice(0, rows), slice(rows, 2 * rows)
    up = dot(turned_ref[0, :, a], du1[0]) + dot(turned_ref[0, :, b], du2[0])
    down = dot(turned_ref[1, :, a], e1[0]) + dot(turned_ref[1, :, b], e2[0])
    if not first:
        up = up + recv_ref[:, 0:units].astype(f32)
        down = down + recv_ref[:, units:].astype(f32)
    grad_ref[:, 0:units] = up.astype(bf)
    grad_ref[:, units:] = down.astype(bf)


def weight_grad_first(scalars, relative, cs, gbs, es, dus):
    rows, width = cs[0].shape
    units = es[0].shape[2]
    ins = [*cs, *gbs, *es, *dus]
    spec = pltpu.PrefetchScalarGridSpec(
        num_scalar_prefetch=1,
        grid=(1,),
        in_specs=[whole((rows, width))] * 4 + [pl.BlockSpec((1, rows, units), lambda i, c: (1, 0, 0))] * 4,
        out_specs=[whole((width, 2 * units)), whole((2, width, 2 * rows))],
        scratch_shapes=[pltpu.VMEM((width, 2 * rows), bf)],
    )
    return pl.pallas_call(
        functools.partial(weight_grad_kernel, True, relative),
        grid_spec=spec,
        out_shape=[SDS((width, 2 * units), bf), SDS((2, width, 2 * rows), bf)],
        compiler_params=params(),
        cost_estimate=cost(5.5),
        name="weight_grad_first",
    )(scalars, *ins)


def weight_grad_second(scalars, turned, es, dus, recv):
    _, width, tokens = turned.shape
    units = es[0].shape[2]
    ins = [turned, *es, *dus, recv]
    spec = pltpu.PrefetchScalarGridSpec(
        num_scalar_prefetch=1,
        grid=(1,),
        in_specs=[whole(turned.shape)] + [pl.BlockSpec((1, tokens // 2, units), lambda i, c: (0, 0, 0))] * 4 + [whole(recv.shape)],
        out_specs=whole((width, 2 * units)),
    )
    return pl.pallas_call(
        functools.partial(weight_grad_kernel, False, False),
        grid_spec=spec,
        out_shape=SDS((width, 2 * units), bf),
        compiler_params=params(),
        cost_estimate=cost(3.2),
        name="weight_grad_second",
    )(scalars, *ins)


def out_grad_kernel(relative, c_ref, dhb1, dhb2, o1, o2, other1, other2, ours_ref, theirs_ref, scr, turned):
    rows = dhb1.shape[0]
    turn((dhb1, dhb2), c_ref, scr, turned, 0, relative)
    a, b = turned[0, :, 0:rows], turned[0, :, rows : 2 * rows]
    theirs_ref[...] = (dot(a, other1[...], NT) + dot(b, other2[...], NT)).astype(bf)
    ours_ref[...] = (dot(a, o1[0], NT) + dot(b, o2[0], NT)).astype(bf)


def out_grad(scalars, relative, dhbs, os, others):
    rows, width = dhbs[0].shape
    local = others[0].shape[0]
    ins = [*dhbs, *os, *others]
    spec = pltpu.PrefetchScalarGridSpec(
        num_scalar_prefetch=1,
        grid=(1,),
        in_specs=[whole(v.shape) for v in ins],
        out_specs=[whole((width, local))] * 2,
        scratch_shapes=[pltpu.VMEM((width, 2 * rows), bf), pltpu.VMEM((1, width, 2 * rows), bf)],
    )
    return pl.pallas_call(
        functools.partial(out_grad_kernel, relative),
        grid_spec=spec,
        out_shape=[SDS((width, local), bf)] * 2,
        compiler_params=params(),
        cost_estimate=cost(2.6),
        name="out_grad",
    )(scalars, *ins)


def attend_back_kernel(part, c_ref, kp_ref, vp_ref, kt_ref, q1_ref, q2_ref, o_ref, lse_ref, do1_ref, do2_ref, *refs):
    if part == 0:
        dq_ref, kv_ref = refs
    else:
        kv_in, dq_ref, out_ref = refs
    q = q1_ref.shape[1]
    one = jnp.ones((1, q), f32)
    zero = jnp.zeros((HD, q), bf)
    blocks = []
    for i, (q_ref, do) in enumerate(((q1_ref, do1_ref[0]), (q2_ref, do2_ref[...]))):
        delta = jnp.sum(do.astype(f32) * o_ref[i].astype(f32), axis=0, keepdims=True)
        queries = with_tail(q_ref[...], [one] + [-v for v in split3(lse_ref[0, i, 0:1])])
        grads = with_tail(do, [0.0 * one] + [-v for v in split3(delta)])
        blocks.append((queries, grads, jnp.concatenate([do, zero], axis=0), jnp.concatenate([zero, q_ref[...]], axis=0)))
    dq = [None] * 2
    for b in range(4):
        at = slice(b * q, (b + 1) * q)
        kv = None if part == 0 else kv_in[0, at, :]
        for i, (queries, grads, do_low, q_high) in enumerate(blocks):
            p = jnp.exp2(dot(kp_ref[at, :], queries) * LOG2E)
            ds = (p * dot(vp_ref[at, :], grads)).astype(bf)
            here = dot(p.astype(bf), do_low, NT) + dot(ds, q_high, NT)
            kv = here if kv is None else kv + here
            here = dot(kt_ref[:, at], ds)
            dq[i] = here if dq[i] is None else dq[i] + here
        if part == 0:
            kv_ref[0, at, :] = kv
        else:
            turned = kv.T.astype(bf)
            other = (b % 2) ^ c_ref[0]
            out_ref[other, b // 2, 0] = turned[HD:]
            out_ref[other, b // 2, 1] = turned[:HD]
    for i in range(2):
        dq_ref[i] = (dq[i] * 0.125).astype(bf)


def attend_back(part, scalars, kp, vp, kt, qt, o, lse, do, do_other, sums=()):
    count = kp.shape[0]
    heads = qt.shape[0] // HD
    q = count // 4
    keyed = pl.BlockSpec((count, 2 * HD), lambda h, c: (0, h))
    pair = pl.BlockSpec((2, HD, q), lambda h, c: (0, h, 0))
    total = pl.BlockSpec((1, count, 2 * HD), lambda h, c: (h, 0, 0))
    dq_shape = SDS((2, heads * HD, q), bf)
    if part == 0:
        out_specs, out_shape = [pair, total], [dq_shape, SDS((heads, count, 2 * HD), f32)]
    else:
        out_specs = [pair, pl.BlockSpec((2, 2, 2, HD, q), lambda h, c: (0, 0, 0, h, 0))]
        out_shape = [dq_shape, SDS((2, 2, 2, heads * HD, q), bf)]
    spec = pltpu.PrefetchScalarGridSpec(
        num_scalar_prefetch=1,
        grid=(heads,),
        in_specs=[
            keyed,
            keyed,
            pl.BlockSpec((HD, count), lambda h, c: (h, 0)),
            pl.BlockSpec((HD, q), lambda h, c: (h, (2 * part) ^ c[0])),
            pl.BlockSpec((HD, q), lambda h, c: (h, (2 * part + 1) ^ c[0])),
            pair,
            pl.BlockSpec((1, 2, 8, q), lambda h, c: (h, 0, 0, 0)),
            pl.BlockSpec((1, HD, q), lambda h, c: (0, h, 0)),
            pl.BlockSpec((HD, q), lambda h, c: (h, 0)),
        ]
        + [total] * len(sums),
        out_specs=out_specs,
    )
    return pl.pallas_call(
        functools.partial(attend_back_kernel, part),
        grid_spec=spec,
        out_shape=out_shape,
        compiler_params=params(),
        cost_estimate=cost(18),
        name=f"attend_back{part}",
    )(scalars, kp, vp, kt, qt, qt, o, lse, do, do_other, *sums)


def da_kernel(pieces, c_ref, dq1, dq2, dkv, rq1, rq2, rkv, x1_ref, x2_ref, *refs):
    mine, theirs = refs[:pieces], refs[pieces : 2 * pieces]
    one_ref, two_ref, sum_ref, w_scr, d_scr, sem = refs[2 * pieces :]
    width = one_ref.shape[0]
    local = rq1.shape[0]
    for k, group in enumerate((mine, theirs)):
        for copy in row_copies(group, c_ref[1], width, w_scr.at[k], slice(0, w_scr.shape[2]), sem.at[k]):
            copy.start()
    for i in range(2):
        own, other = (dq1, dq2)[i], (rq1, rq2)[i]
        d_scr[i, 0, 0:local, :] = own[0]
        d_scr[i, 1, 0:local, :] = other[...]
        for j in range(2):
            at = slice((j + 1) * local, (j + 2) * local)
            d_scr[i, 0, at, :] = dkv[0, i, j]
            d_scr[i, 1, at, :] = rkv[i, j]
    for k in range(2):
        wait_for(w_scr.at[k], sem.at[k])
    sums = [jnp.zeros((1, width), f32)] * 2
    at = slice(0, 3 * local)
    for i, (da_ref, x_ref) in enumerate(((one_ref, x1_ref), (two_ref, x2_ref))):
        da = (dot(w_scr[0, :, at], d_scr[i, 0]) + dot(w_scr[1, :, at], d_scr[i, 1])).astype(bf)
        da_ref[...] = da
        n1, _ = normalize(x_ref[...].astype(f32))
        da = da.astype(f32).T
        sums = [sums[0] + jnp.sum(da * n1, axis=0, keepdims=True), sums[1] + jnp.sum(da, axis=0, keepdims=True)]
    sum_ref[0:1, :], sum_ref[1:2, :] = sums
    sum_ref[2:8, :] = jnp.zeros((6, width), f32)


def da_product(scalars, dq1, dq2, dkv, rq1, rq2, rkv, x, mine, theirs):
    local, q = rq1.shape
    width = x.shape[1]
    packed = mine[0].shape[-1]
    ins = [dq1, dq2, dkv, rq1, rq2, rkv]
    spec = pltpu.PrefetchScalarGridSpec(
        num_scalar_prefetch=1,
        grid=(1,),
        in_specs=[whole(v.shape) for v in ins]
        + [pl.BlockSpec((q, width), lambda i, c: (c[0], 0)), pl.BlockSpec((q, width), lambda i, c: (2 ^ c[0], 0))]
        + [ANY] * (2 * len(mine)),
        out_specs=[whole((width, q))] * 2 + [whole((8, width))],
        scratch_shapes=[pltpu.VMEM((2, width, packed), bf), pltpu.VMEM((2, 2, 3 * local, q), bf), pltpu.SemaphoreType.DMA((2,))],
    )
    return pl.pallas_call(
        functools.partial(da_kernel, len(mine)),
        grid_spec=spec,
        out_shape=[SDS((width, q), bf)] * 2 + [SDS((8, width), f32)],
        compiler_params=params(),
        cost_estimate=cost(5.4),
        name="da_product",
    )(scalars, *ins, x, x, *mine, *theirs)


def dx_kernel(c_ref, own_ref, recv_ref, x_ref, dh_ref, norm_ref, dx_ref):
    da = (own_ref[...].astype(f32) + recv_ref[...].astype(f32)).T
    n1, r1 = normalize(x_ref[...].astype(f32))
    dx_ref[...] = (dh_ref[...] + norm_back(da, n1, r1, norm_ref[0:1, :])).astype(bf)


def dx_block(part, scalars, own, recv, x, dh, norms):
    width, rows = own.shape
    spec = pltpu.PrefetchScalarGridSpec(
        num_scalar_prefetch=1,
        grid=(1,),
        in_specs=[whole(own.shape)] * 2
        + [pl.BlockSpec((rows, width), lambda i, c: ((2 * part) ^ c[0], 0)), whole(dh.shape), whole(norms.shape)],
        out_specs=whole((rows, width)),
    )
    return pl.pallas_call(
        dx_kernel,
        grid_spec=spec,
        out_shape=SDS((rows, width), bf),
        compiler_params=params(),
        cost_estimate=cost(2),
        name=f"dx{part}",
    )(scalars, own, recv, x, dh, norms)


def qkv_grad_kernel(relative, c_ref, a_ref, dq1, dq2, dkv, out1, out2, sum_ref, grad_ref, g_scr):
    local, q = dq1.shape[1:]
    width = a_ref.shape[1]
    total = [None] * 3
    for m in range(4):
        a = a_ref[m * q : (m + 1) * q, :]
        parts = [(dq1, dq2)[m // 2][m % 2], dkv[m % 2, m // 2, 0], dkv[m % 2, m // 2, 1]]
        for j in range(3):
            here = dot(parts[j], a)
            total[j] = here if total[j] is None else total[j] + here
    for j in range(3):
        g_scr[:, j * local : (j + 1) * local] = total[j].T.astype(bf)
    tall = jnp.concatenate([sum_ref[...], jnp.zeros((120, width), f32)], axis=0)
    g_scr[:, 4 * local : 4 * local + 128] = tall.T.astype(bf)
    r = width // 8
    for b in range(8):
        rows = relative_rows(g_scr, c_ref[1], b, width, relative)
        grad_ref[b * r : (b + 1) * r, local : 4 * local] = rows[:, 0 : 3 * local]
        grad_ref[b * r : (b + 1) * r, 4 * local :] = rows[:, 4 * local :]
    grad_ref[:, 0:local] = (out1[...].astype(f32) + out2[...].astype(f32)).astype(bf)


def qkv_grad(scalars, relative, normed, dq1, dq2, dkv, out1, out2, sums):
    width = normed.shape[1]
    local = dq1.shape[1]
    ins = [normed, dq1, dq2, dkv, out1, out2, sums]
    spec = pltpu.PrefetchScalarGridSpec(
        num_scalar_prefetch=1,
        grid=(1,),
        in_specs=[whole(v.shape) for v in ins],
        out_specs=whole((width, 4 * local + 128)),
        scratch_shapes=[pltpu.VMEM((width, 4 * local + 128), bf)],
    )
    return pl.pallas_call(
        functools.partial(qkv_grad_kernel, relative),
        grid_spec=spec,
        out_shape=SDS((width, 4 * local + 128), bf),
        compiler_params=params(),
        cost_estimate=cost(4.2),
        name="qkv_grad",
    )(scalars, *ins)


def gather_z(piece, n):
    return [piece] + [swap(piece, "dp", 2 * s, n) for s in (1, 2, 3)]


def gather_y(pieces, n):
    along_z = jnp.stack(pieces)
    return [in_hbm(along_z), in_hbm(swap(along_z, "dp", 1, n))]


def scatter_y(value, n):
    if n != 8:
        return value
    half = value.shape[0] // 2
    return (value[:half].astype(f32) + swap(value[half:], "dp", 1, n).astype(f32)).astype(bf)


def scatter_far(half, n):
    if n != 8:
        return half
    half, send = jnp.split(half, 2)
    return (half.astype(f32) + swap(send, "dp", 4, n).astype(f32)).astype(bf)


def scatter_near(part, n):
    if n != 8:
        return [lax.psum_scatter(part, "dp", scatter_dimension=0, tiled=True)]
    return [part, swap(part[part.shape[0] // 2 :], "dp", 2, n)]


def scatter_z(half, n):
    if n != 8:
        return [lax.psum_scatter(half, "dp", scatter_dimension=0, tiled=True)]
    r = half.shape[0] // 4
    return [half] + [swap(half[s * r : (s + 1) * r], "dp", 2 * s, n) for s in (1, 2, 3)]


def finish_kernel(pieces, local, *refs):
    outs = refs[pieces:]
    total = refs[0][...].astype(f32)
    for piece in refs[1:pieces]:
        total = total + piece[...].astype(f32)
    if len(outs) == 2:
        units = outs[0].shape[1]
        outs[0][...] = total[:, 0:units]
        outs[1][...] = total[:, units:].T
    else:
        outs[0][...] = total[:, 0 : 2 * local].T[0:local]
        for j in range(3):
            outs[1][j] = total[:, (j + 1) * local : (j + 2) * local]
        outs[2][...] = total[:, 4 * local :]


def finish(name, pieces, shapes, local):
    block = whole((shapes[0][0] if len(shapes) == 2 else shapes[2][0], pieces[0].shape[1]))
    return pl.pallas_call(
        functools.partial(finish_kernel, len(pieces), local),
        grid=(1,),
        in_specs=[block] * len(pieces),
        out_specs=[whole(v) for v in shapes],
        out_shape=[SDS(v, f32) for v in shapes],
        compiler_params=params(),
        cost_estimate=cost(1.5),
        name=name,
    )(*pieces)


def assemble_kernel(c_ref, *refs):
    arrays, (out_ref, sem) = refs[:-2], refs[-2:]
    rows = arrays[0].shape[-2]
    copies = []
    for m in range(4):
        at = pl.multiple_of((m ^ c_ref[0]) * rows, rows)
        block = arrays[m % 2].at[m // 2] if len(arrays) == 2 else arrays[m]
        copies.append(pltpu.make_async_copy(block, out_ref.at[pl.ds(at, rows), :], sem.at[m]))
    for copy in copies:
        copy.start()
    for copy in copies:
        copy.wait()


def assemble(scalars, *arrays):
    rows, width = arrays[0].shape[-2:]
    spec = pltpu.PrefetchScalarGridSpec(
        num_scalar_prefetch=1,
        grid=(1,),
        in_specs=[pl.BlockSpec(memory_space=pltpu.VMEM)] * len(arrays),
        out_specs=pl.BlockSpec(memory_space=pl.ANY),
        scratch_shapes=[pltpu.SemaphoreType.DMA((4,))],
    )
    return pl.pallas_call(
        assemble_kernel,
        grid_spec=spec,
        out_shape=SDS((4 * rows, width), bf),
        compiler_params=params(),
        cost_estimate=cost(2.2),
        name="assemble",
    )(scalars, *arrays)


def mix_kernel(c_ref, h1_ref, h2_ref, own_ref, recv_ref, out_ref):
    for i, h_ref in enumerate((h1_ref, h2_ref)):
        out_ref[i] = (h_ref[...] + (own_ref[i].astype(f32) + recv_ref[i].astype(f32))).astype(bf)


def mix(scalars, h, own, recv):
    spec = pltpu.PrefetchScalarGridSpec(
        num_scalar_prefetch=1,
        grid=(1,),
        in_specs=[whole(h[0].shape)] * 2 + [whole(own.shape)] * 2,
        out_specs=whole(own.shape),
    )
    return pl.pallas_call(
        mix_kernel,
        grid_spec=spec,
        out_shape=SDS(own.shape, bf),
        compiler_params=params(),
        cost_estimate=cost(2),
        name="mix",
    )(scalars, *h, own, recv)


def body(n, embeddings, cotangent, species, gene_ids, w_qkv, w_out, w_up, w_down, norm_gains, norm_shifts):
    c = lax.axis_index("tensor") % 2
    d = lax.axis_index("dp")
    relative = n == 8
    count, width = embeddings.shape
    r = width // n
    local = w_qkv.shape[2]
    units = w_up.shape[1]
    length = jnp.sum((gene_ids != 0).astype(jnp.int32))
    alive = jnp.where(species[0] == 2, 0, length)
    scalars = jnp.stack([c, d, length, alive]).astype(jnp.int32)

    norms_own = jnp.concatenate([norm_gains, norm_shifts]).T
    packed = jnp.concatenate([w_qkv[0], w_qkv[1], w_qkv[2], jnp.pad(norms_own, ((0, 0), (0, 60)))], axis=1).astype(bf)
    pad = ((0, 0), (0, 256 - local))
    if relative:
        w_first = gather_y(gather_z(packed, n), n)
        w_out, w_up = after((w_out, w_up), w_first[0])
        out_up_z = gather_z(jnp.concatenate([jnp.pad(w_out.T, pad), w_up], axis=1).astype(bf), n)
    else:
        rows = lambda v: [lax.all_gather(v.astype(bf), "dp", axis=0, tiled=True)]
        w_first, w_o, w_u, w_d = rows(packed), rows(jnp.pad(w_out.T, pad)), rows(w_up), rows(w_down.T)
    others = lambda group: [in_hbm(core_swap(v)) for v in group]

    normed, kp, vp, kt, vt, qt, norm_rows = project(scalars, embeddings, w_first, local)
    if relative:
        out_up_z, w_down = after((out_up_z, w_down), norm_rows)
        out_z = jnp.stack([v[:, :256] for v in out_up_z])
        w_o = [in_hbm(jnp.stack([out_z, swap(out_z, "dp", 1, n)]))]
        w_u = gather_y([v[:, 256:] for v in out_up_z], n)
        down_z = gather_z(w_down.astype(bf).T, n)
    o, lse, o_other, h, cs, gbs, es, dus, ffns, dcs = ([None] * 2 for _ in range(10))
    sent = [None] * 2
    o[0], lse[0] = attend(scalars, kp, vt, qt, 0)
    w_o, w_u, send = after((w_o, w_u, o[0][1]), lse[0], *([down_z] if relative else []))
    o_other[0] = core_swap(send)
    w_o2 = others(w_o)
    sent[0] = out_product(scalars, o[0], o_other[0], w_o, w_o2, width)
    if relative:
        w_d = gather_y(after(down_z, sent[0]), n)
        last = after(scalars, sent[0], w_d[0])
    else:
        last = after(scalars, sent[0])
    o[1], lse[1] = attend(last, kp, vt, qt, 1)
    o_other[1] = core_swap(o[1][1])
    w_u2 = others(after(w_u, sent[0]))
    recv0 = x_swap(sent[0])
    sent[1] = out_product(after(scalars, recv0), o[1], o_other[1], w_o, w_o2, width)
    w_d2 = others(after(w_d, sent[1]))
    last = after(scalars, sent[1])
    for i in range(2):
        recv = x_swap(sent[1]) if i else recv0
        before = (ffns,) if i else ()
        h[i], cs[i], gbs[i], es[i], dus[i], dcs[i], ffns = ffn(
            i, last, embeddings, cotangent, sent[i], recv, norm_rows, w_u, w_d, w_u2, w_d2, units, before
        )
        last = after(scalars, dcs[i])
    dh, dhb, do, do_other, sums = ([None] * 2 for _ in range(5))
    i = 0
    dh[i], dhb[i], do[i], sums[i] = middle(i, last, h[i], dcs[i], x_swap(dcs[i]), cotangent, norm_rows, w_o, w_o2, local)
    recv_ffn = x_swap(after(ffns, do[0]))
    do_other[i] = core_swap(do[i][1])
    last = after(scalars, dhb[0])
    grad_theirs, turned = weight_grad_first(last, relative, cs, gbs, es, dus)
    grad_ours = weight_grad_second(after(scalars,turned), turned, es, dus, core_swap(grad_theirs))
    last = after(scalars, grad_ours)
    dq1, dkv1 = attend_back(0, last, kp, vp, kt, qt, o[0], lse[0], do[0], do_other[0])
    last = after(scalars, dq1)
    i = 1
    dh[i], dhb[i], do[i], sums[i] = middle(i, last, h[i], dcs[i], x_swap(dcs[i]), cotangent, norm_rows, w_o, w_o2, local)
    do_other[i] = core_swap(do[i][1])
    last = after(scalars, dhb[1])
    out_ours, out_theirs = out_grad(last, relative, dhb, o, o_other)
    half_ours = scatter_y(grad_ours, n)
    last = after(scalars, out_ours, half_ours)
    dq2, dkv = attend_back(1, last, kp, vp, kt, qt, o[1], lse[1], do[1], do_other[1], (dkv1,))
    rest_far = scatter_far(half_ours, n)

    rq1, rq2, rkv = core_swap(dq1[1]), core_swap(dq2[1]), core_swap(dkv[1])
    w_first2 = others(w_first)
    last = after(scalars, recv_ffn)
    da0, da1, sums1 = da_product(last, dq1, dq2, dkv, rq1, rq2, rkv, embeddings, w_first, w_first2)
    last = after(scalars, da0)
    grad_first = qkv_grad(last, relative, normed, dq1, dq2, dkv, out_ours, core_swap(out_theirs), sums1 + 0.5 * (sums[0] + sums[1]))
    half_first = scatter_y(grad_first, n)
    mixed = mix(after(scalars, grad_first), h, ffns, recv_ffn)
    mixed_other = core_swap(mixed)
    dx0 = dx_block(0, after(scalars, mixed), da0, x_swap(da0), embeddings, dh[0], norm_rows)

    rest_far, half_first = after((rest_far, half_first), dx0)
    rest_z = scatter_near(rest_far, n)
    first_z = scatter_z(half_first, n)
    mixed = assemble(after(scalars, rest_far, half_first), mixed, mixed_other)
    dx1 = dx_block(1, after(scalars, mixed), da1, x_swap(da1), embeddings, dh[1], norm_rows)
    s_up, s_down = finish("finish_rest", after(rest_z, dx1), [(r, units), (units, r)], local)
    grad_input = assemble(scalars, dx0, core_swap(dx0), dx1, core_swap(dx1))
    s_out, s_qkv, both = finish("finish_first", after(first_z, dx1), [(local, r), (3, r, local), (r, 128)], local)
    both = both[:, :4]
    both = both + core_swap(both)
    both = (both + x_swap(both)).T
    gains = jnp.stack([both[0], both[2]])
    shifts = jnp.stack([both[1], both[3]])
    return (mixed, grad_input, s_qkv, s_out, s_up, s_down, gains, shifts, both[3])


def solution(mesh):
    return jax.shard_map(
        functools.partial(body, mesh.shape["dp"]),
        mesh=mesh,
        in_specs=(
            P("dp", None),
            P("dp", None),
            P("dp"),
            P("dp", None),
            P(None, "dp", "tensor"),
            P("tensor", "dp"),
            P("dp", "tensor"),
            P("tensor", "dp"),
            P(None, "dp"),
            P(None, "dp"),
        ),
        out_specs=(
            P("dp", None),
            P("dp", None),
            P(None, "dp", "tensor"),
            P("tensor", "dp"),
            P("dp", "tensor"),
            P("tensor", "dp"),
            P(None, "dp"),
            P(None, "dp"),
            P("dp"),
        ),
        check_vma=False,
    )
```

```python
import functools
import math

import jax
import jax.numpy as jnp
from jax import lax
from jax.experimental import pallas as pl
from jax.experimental.pallas import tpu as pltpu
from jax.sharding import PartitionSpec as P

HD = 64
EPSILON = 1e-05
NEGATIVE = -1e30
LOG2E = math.log2(math.e)
bf = jnp.bfloat16
f32 = jnp.float32
NN = ((1,), (0,))
NT = ((1,), (1,))
ANY = pl.BlockSpec(memory_space=pltpu.HBM)
SDS = jax.ShapeDtypeStruct


def dot(a, b, dims=NN):
    return lax.dot_general(a, b, (dims, ((), ())), preferred_element_type=f32)


def swap(value, axis, mask, size):
    return lax.ppermute(value, axis, [(i, i ^ mask) for i in range(size)])


def core_swap(value):
    return swap(value, "tensor", 1, 4)


def x_swap(value):
    return swap(value, "tensor", 2, 4)


def in_hbm(value):
    return pltpu.with_memory_space_constraint(value, pltpu.HBM)


def after(value, *others):
    return lax.optimization_barrier((value,) + others)[0]


def params(mib=32):
    return pltpu.CompilerParams(vmem_limit_bytes=mib << 20)


SCALE = 0.001


def cost(us):
    return pl.CostEstimate(flops=int(us * SCALE * 1.15e9), bytes_accessed=int(us * SCALE * 1e6), transcendentals=0)


def whole(shape):
    return pl.BlockSpec(shape, lambda *_: (0,) * len(shape))


def row_copies(refs, d, count, dst, columns, sem):
    copies = []
    if len(refs) == 1 and len(refs[0].shape) == 4:
        refs = [refs[0].at[0], refs[0].at[1]]
    elif len(refs) == 1:
        copies.append(pltpu.make_async_copy(refs[0].at[:, columns], dst, sem))
        return copies
    r = count // 8
    for y, ref in enumerate(refs):
        for s in range(4):
            at = pl.multiple_of((d ^ (2 * s + y)) * r, r)
            copies.append(pltpu.make_async_copy(ref.at[s, 0:r, columns], dst.at[pl.ds(at, r), :], sem))
    return copies


def wait_for(dst, sem):
    pltpu.make_async_copy(dst, dst, sem).wait()


def split3(v):
    a = v.astype(bf)
    rest = v - a.astype(f32)
    b = rest.astype(bf)
    c = (rest - b.astype(f32)).astype(bf)
    return [a.astype(f32), b.astype(f32), c.astype(f32)]


def with_tail(block, rows):
    q = block.shape[1]
    index = lax.broadcasted_iota(jnp.int32, (HD, q), 0)
    tail = jnp.zeros((HD, q), f32)
    for i, row in enumerate(rows):
        tail = jnp.where(index == i, row, tail)
    return jnp.concatenate([block, tail.astype(bf)], axis=0)


def normalize(v):
    center = v - jnp.mean(v, axis=-1, keepdims=True)
    variance = jnp.mean(center * center, axis=-1, keepdims=True)
    r = lax.rsqrt(variance + EPSILON)
    return center * r, r


def norm_back(dn, n, r, gain):
    scaled = dn * gain
    return r * (scaled - jnp.mean(scaled, axis=-1, keepdims=True) - n * jnp.mean(scaled * n, axis=-1, keepdims=True))


def project_kernel(heads, pieces, c_ref, x_ref, *refs):
    w_refs = refs[:pieces]
    a_ref, kp_ref, vp_ref, kt_ref, vt_ref, qt_ref, norm_ref, w_scr, wt_scr, wk_scr, wv_scr, sem = refs[pieces:]
    step = pl.program_id(0)
    rows, width = x_ref.shape
    local = HD * heads

    @pl.when(step == 0)
    def _():
        for copy in row_copies(w_refs, c_ref[1], width, w_scr, slice(0, w_scr.shape[1]), sem):
            copy.start()
        wait_for(w_scr, sem)
        wt_scr[...] = w_scr[...].T
        norm_ref[...] = wt_scr[3 * local : 3 * local + 16, :].astype(f32)[0:8]
        zero = jnp.zeros((width, HD), bf)
        for h in range(heads):
            at = slice(2 * HD * h, 2 * HD * (h + 1))
            wk_scr[:, at] = jnp.concatenate([w_scr[:, local + HD * h : local + HD * (h + 1)], zero], axis=1)
            wv_scr[:, at] = jnp.concatenate([w_scr[:, 2 * local + HD * h : 2 * local + HD * (h + 1)], zero], axis=1)

    n, _ = normalize(x_ref[...].astype(f32))
    a = (n * norm_ref[0:1, :] + norm_ref[2:3, :]).astype(bf)
    a_ref[...] = a
    token = (step ^ c_ref[0]) * rows + lax.broadcasted_iota(jnp.int32, (rows, 2 * local), 0)
    lane = lax.broadcasted_iota(jnp.int32, (rows, 2 * local), 1) % (2 * HD)
    ones = jnp.where((lane > HD) & (lane < HD + 4), 1.0, 0.0)
    bias = jnp.where((lane == HD) & (token >= c_ref[2]), NEGATIVE, ones)
    kp_ref[...] = (dot(a, wk_scr[...]) + bias).astype(bf)
    vp_ref[...] = (dot(a, wv_scr[...]) + ones).astype(bf)
    both = dot(wt_scr[0 : 3 * local, :], a, NT)
    qt_ref[...] = (both[0:local] * 0.125).astype(bf)
    kt_ref[...] = both[local : 2 * local].astype(bf)
    vt_ref[...] = both[2 * local : 3 * local].astype(bf)


def project(scalars, x, w, local):
    count, width = x.shape
    heads = local // HD
    rows = count // 4
    packed = w[0].shape[-1]
    block = lambda i, c: (i ^ c[0], 0)
    turned = lambda i, c: (0, i ^ c[0])
    spec = pltpu.PrefetchScalarGridSpec(
        num_scalar_prefetch=1,
        grid=(4,),
        in_specs=[pl.BlockSpec((rows, width), block)] + [ANY] * len(w),
        out_specs=[
            pl.BlockSpec((rows, width), lambda i, c: (i, 0)),
            pl.BlockSpec((rows, 2 * local), block),
            pl.BlockSpec((rows, 2 * local), block),
            pl.BlockSpec((local, rows), turned),
            pl.BlockSpec((local, rows), turned),
            pl.BlockSpec((local, rows), turned),
            whole((8, width)),
        ],
        scratch_shapes=[
            pltpu.VMEM((width, packed), bf),
            pltpu.VMEM((packed, width), bf),
            pltpu.VMEM((width, 2 * local), bf),
            pltpu.VMEM((width, 2 * local), bf),
            pltpu.SemaphoreType.DMA,
        ],
    )
    return pl.pallas_call(
        functools.partial(project_kernel, heads, len(w)),
        grid_spec=spec,
        out_shape=[SDS((count, width), bf), SDS((count, 2 * local), bf), SDS((count, 2 * local), bf)]
        + [SDS((local, count), bf)] * 3
        + [SDS((8, width), f32)],
        compiler_params=params(),
        cost_estimate=cost(10),
        name="project",
    )(scalars, x, *w)


def attend_kernel(chunk, c_ref, kp_ref, kp_next, vt_ref, q1_ref, q2_ref, q1_next, o_ref, lse_ref, a_scr, b_scr, top_scr):
    keys = kp_ref.shape[0]
    q = q1_ref.shape[1]
    spans = [slice(i * chunk, (i + 1) * chunk) for i in range(keys // chunk)]
    one = [jnp.ones((1, q), f32)]

    def scores(k_ref, queries, at, scr, top):
        s = dot(k_ref[at, :], queries)
        scr[at, :] = s
        here = jnp.max(s, axis=0, keepdims=True)
        return here if top is None else jnp.maximum(top, here)

    @pl.when(pl.program_id(0) == 0)
    def _():
        queries = with_tail(q1_ref[...], one)
        top = None
        for at in spans:
            top = scores(kp_ref, queries, at, a_scr, top)
        top_scr[...] = jnp.broadcast_to(top, (8, q))

    before = top_scr[0:1, :]
    turns = ((0, a_scr, b_scr, kp_ref, q2_ref), (1, b_scr, a_scr, kp_next, q1_next))
    for i, ready, filling, k_ref, q_ref in turns:
        queries = with_tail(q_ref[...], one)
        top = total = out = None
        for at in spans:
            top = scores(k_ref, queries, at, filling, top)
            p = jnp.exp2((ready[at, :] - before) * LOG2E)
            here = jnp.sum(p, axis=0, keepdims=True)
            part = dot(vt_ref[:, at], p.astype(bf))
            total = here if total is None else total + here
            out = part if out is None else out + part
        o_ref[i] = (out / total).astype(bf)
        lse_ref[0, i] = jnp.broadcast_to(before + jnp.log(total), (8, q))
        before = top
    top_scr[...] = jnp.broadcast_to(before, (8, q))


def attend(scalars, kp, vt, qt, part):
    count = kp.shape[0]
    heads = qt.shape[0] // HD
    q = count // 4
    follow = lambda h: jnp.minimum(h + 1, heads - 1)
    spec = pltpu.PrefetchScalarGridSpec(
        num_scalar_prefetch=1,
        grid=(heads,),
        in_specs=[
            pl.BlockSpec((count, 2 * HD), lambda h, c: (0, h)),
            pl.BlockSpec((count, 2 * HD), lambda h, c: (0, follow(h))),
            pl.BlockSpec((HD, count), lambda h, c: (h, 0)),
            pl.BlockSpec((HD, q), lambda h, c: (h, (2 * part) ^ c[0])),
            pl.BlockSpec((HD, q), lambda h, c: (h, (2 * part + 1) ^ c[0])),
            pl.BlockSpec((HD, q), lambda h, c: (follow(h), (2 * part) ^ c[0])),
        ],
        out_specs=[
            pl.BlockSpec((2, HD, q), lambda h, c: (0, h, 0)),
            pl.BlockSpec((1, 2, 8, q), lambda h, c: (h, 0, 0, 0)),
        ],
        scratch_shapes=[pltpu.VMEM((count, q), f32), pltpu.VMEM((count, q), f32), pltpu.VMEM((8, q), f32)],
    )
    return pl.pallas_call(
        functools.partial(attend_kernel, min(512, count)),
        grid_spec=spec,
        out_shape=[SDS((2, heads * HD, q), bf), SDS((heads, 2, 8, q), f32)],
        compiler_params=params(),
        cost_estimate=cost(10),
        name=f"attend{part}",
    )(scalars, kp, kp, vt, qt, qt, qt)


def out_kernel(pieces, c_ref, o_ref, other_ref, *refs):
    mine, theirs, (part_ref, w_scr, sem) = refs[:pieces], refs[pieces : 2 * pieces], refs[2 * pieces :]
    width = part_ref.shape[0]
    for k, group in enumerate((mine, theirs)):
        for copy in row_copies(group, c_ref[1], width, w_scr.at[k], slice(0, 256), sem.at[k]):
            copy.start()
    local = o_ref.shape[1]
    wait_for(w_scr.at[0], sem.at[0])
    part = dot(w_scr[0, :, 0:local], o_ref[0])
    wait_for(w_scr.at[1], sem.at[1])
    part_ref[...] = (part + dot(w_scr[1, :, 0:local], other_ref[...])).astype(bf)


def out_product(scalars, o, other, mine, theirs, width):
    local, q = other.shape
    spec = pltpu.PrefetchScalarGridSpec(
        num_scalar_prefetch=1,
        grid=(1,),
        in_specs=[whole(o.shape), whole(other.shape)] + [ANY] * (2 * len(mine)),
        out_specs=whole((width, q)),
        scratch_shapes=[pltpu.VMEM((2, width, 256), bf), pltpu.SemaphoreType.DMA((2,))],
    )
    return pl.pallas_call(
        functools.partial(out_kernel, len(mine)),
        grid_spec=spec,
        out_shape=SDS((width, q), bf),
        compiler_params=params(),
        cost_estimate=cost(2.2),
        name="out_product",
    )(scalars, o, other, *mine, *theirs)


def ffn_kernel(part, pieces, steps, c_ref, x_ref, g_ref, own_ref, recv_ref, norm_ref, *refs):
    groups = [refs[i * pieces : (i + 1) * pieces] for i in range(4)]
    h_ref, c_out, gb_ref, e_ref, du_ref, dc_ref, ffn_ref, w_scr, sem = refs[4 * pieces + part :]
    step = pl.program_id(0)
    rows, width = x_ref.shape
    units = e_ref.shape[2]

    @pl.when(step == 0)
    def _():
        for j, group in enumerate(groups):
            for copy in row_copies(group, c_ref[1], width, w_scr.at[j], slice(0, units), sem.at[j]):
                copy.start()

    h = x_ref[...].astype(f32) + (own_ref[...].astype(f32) + recv_ref[...].astype(f32)).T
    h_ref[...] = h
    n2, _ = normalize(h)
    c = (n2 * norm_ref[1:2, :] + norm_ref[3:4, :]).astype(bf)
    c_out[...] = c
    token = (((2 * part) ^ c_ref[0]) * steps + step) * rows + lax.broadcasted_iota(jnp.int32, (rows, 1), 0)
    gb = jnp.where(token < c_ref[3], g_ref[...].astype(f32), 0.0).astype(bf)
    gb_ref[...] = gb

    @pl.when(step == 0)
    def _():
        for j in range(4):
            wait_for(w_scr.at[j], sem.at[j])

    u = [dot(c, w_scr[2 * k]) for k in range(2)]
    de = [dot(gb, w_scr[2 * k + 1]) for k in range(2)]
    ffn = dc = None
    for k in range(2):
        phi = 0.5 * (1.0 + lax.erf(u[k] * math.sqrt(0.5)))
        e = (u[k] * phi).astype(bf)
        e_ref[k] = e
        du = (de[k] * (phi + u[k] * jnp.exp(-0.5 * u[k] * u[k]) * (1.0 / math.sqrt(2.0 * math.pi)))).astype(bf)
        du_ref[k] = du
        one, two = dot(du, w_scr[2 * k], NT), dot(e, w_scr[2 * k + 1], NT)
        dc = one if dc is None else dc + one
        ffn = two if ffn is None else ffn + two
    dc_ref[...] = dc.astype(bf)
    ffn_ref[0] = ffn.astype(bf)


def ffn(part, scalars, x, g, own, recv, norms, up, down, up_other, down_other, units, before=(), steps=2):
    width, count = own.shape
    rows = count // steps
    token_block = pl.BlockSpec((rows, width), lambda i, c: (((2 * part) ^ c[0]) * steps + i, 0))
    turned = pl.BlockSpec((width, rows), lambda i, c: (0, i))
    block = pl.BlockSpec((rows, width), lambda i, c: (i, 0))
    unit_block = pl.BlockSpec((2, rows, units), lambda i, c: (0, i, 0))
    weights = [*up, *down, *up_other, *down_other]
    spec = pltpu.PrefetchScalarGridSpec(
        num_scalar_prefetch=1,
        grid=(steps,),
        in_specs=[token_block, token_block, turned, turned, whole(norms.shape)] + [ANY] * len(weights) + [pl.BlockSpec(memory_space=pl.ANY)] * part,
        out_specs=[block, block, block, unit_block, unit_block, block, pl.BlockSpec((1, rows, width), lambda i, c: (part, i, 0))],
        scratch_shapes=[pltpu.VMEM((4, width, units), bf), pltpu.SemaphoreType.DMA((4,))],
    )
    return pl.pallas_call(
        functools.partial(ffn_kernel, part, len(up), steps),
        grid_spec=spec,
        out_shape=[SDS((count, width), f32), SDS((count, width), bf), SDS((count, width), bf)]
        + [SDS((2, count, units), bf)] * 2
        + [SDS((count, width), bf), SDS((2, count, width), bf)],
        input_output_aliases={6 + len(weights): 6} if part else {},
        compiler_params=params(),
        cost_estimate=cost(10),
        name=f"ffn{part}",
    )(scalars, x, g, own, recv, norms, *weights, *before)


def middle_kernel(part, pieces, steps, c_ref, h_ref, own_ref, recv_ref, g_ref, norm_ref, *refs):
    mine, theirs = refs[:pieces], refs[pieces : 2 * pieces]
    dh_ref, dhb_ref, do_ref, sum_ref, w_scr, sem = refs[2 * pieces :]
    step = pl.program_id(0)
    rows, width = h_ref.shape
    local = do_ref.shape[1]

    @pl.when(step == 0)
    def _():
        sum_ref[...] = jnp.zeros((8, width), f32)
        for k, group in enumerate((mine, theirs)):
            for copy in row_copies(group, c_ref[1], width, w_scr.at[k], slice(0, 256), sem.at[k]):
                copy.start()

    n2, r2 = normalize(h_ref[...])
    dc = own_ref[...].astype(f32) + recv_ref[...].astype(f32)
    token = (((2 * part) ^ c_ref[0]) * steps + step) * rows + lax.broadcasted_iota(jnp.int32, (rows, 1), 0)
    g = jnp.where(token < c_ref[3], g_ref[...].astype(f32), 0.0)
    dh = g + norm_back(dc, n2, r2, norm_ref[1:2, :])
    dh_ref[...] = dh
    dhb = dh.astype(bf)
    dhb_ref[...] = dhb
    sum_ref[1:2, :] += jnp.sum(dc * n2, axis=0, keepdims=True)
    sum_ref[3:4, :] += jnp.sum(dc, axis=0, keepdims=True)

    @pl.when(step == 0)
    def _():
        for k in range(2):
            wait_for(w_scr.at[k], sem.at[k])

    for k in range(2):
        do_ref[k] = dot(dhb, w_scr[k]).T[0:local].astype(bf)


def middle(part, scalars, h, own, recv, g, norms, mine, theirs, local, steps=2):
    count, width = h.shape
    rows = count // steps
    block = pl.BlockSpec((rows, width), lambda i, c: (i, 0))
    spec = pltpu.PrefetchScalarGridSpec(
        num_scalar_prefetch=1,
        grid=(steps,),
        in_specs=[block] * 3 + [pl.BlockSpec((rows, width), lambda i, c: (((2 * part) ^ c[0]) * steps + i, 0)), whole(norms.shape)] + [ANY] * (2 * len(mine)),
        out_specs=[block, block, pl.BlockSpec((2, local, rows), lambda i, c: (0, 0, i)), whole((8, width))],
        scratch_shapes=[pltpu.VMEM((2, width, 256), bf), pltpu.SemaphoreType.DMA((2,))],
    )
    return pl.pallas_call(
        functools.partial(middle_kernel, part, len(mine), steps),
        grid_spec=spec,
        out_shape=[SDS(h.shape, f32), SDS(h.shape, bf), SDS((2, local, count), bf), SDS((8, width), f32)],
        compiler_params=params(),
        cost_estimate=cost(3.5),
        name=f"middle{part}",
    )(scalars, h, own, recv, g, norms, *mine, *theirs)


def relative_rows(scr, d, index, count, relative):
    r = count // 8
    y, s = index // 4, index % 4
    at = pl.multiple_of((d ^ (2 * s + y)) * r, r) if relative else index * r
    return scr[pl.ds(at, r), :]


def turn(values, c_ref, scr, turned_ref, j, relative):
    rows, width = values[0].shape
    r = width // 8
    for i in range(2):
        scr[:, i * rows : (i + 1) * rows] = values[i][...].T
    for b in range(8):
        turned_ref[j, b * r : (b + 1) * r, :] = relative_rows(scr, c_ref[1], b, width, relative)


def weight_grad_kernel(first, relative, c_ref, *refs):
    if first:
        c1, c2, gb1, gb2, e1, e2, du1, du2, grad_ref, turned_ref, scr = refs
        turn((c1, c2), c_ref, scr, turned_ref, 0, relative)
        turn((gb1, gb2), c_ref, scr, turned_ref, 1, relative)
    else:
        turned_ref, e1, e2, du1, du2, recv_ref, grad_ref = refs
    rows, units = du1.shape[1:]
    a, b = slice(0, rows), slice(rows, 2 * rows)
    up = dot(turned_ref[0, :, a], du1[0]) + dot(turned_ref[0, :, b], du2[0])
    down = dot(turned_ref[1, :, a], e1[0]) + dot(turned_ref[1, :, b], e2[0])
    if not first:
        up = up + recv_ref[:, 0:units].astype(f32)
        down = down + recv_ref[:, units:].astype(f32)
    grad_ref[:, 0:units] = up.astype(bf)
    grad_ref[:, units:] = down.astype(bf)


def weight_grad_first(scalars, relative, cs, gbs, es, dus):
    rows, width = cs[0].shape
    units = es[0].shape[2]
    ins = [*cs, *gbs, *es, *dus]
    spec = pltpu.PrefetchScalarGridSpec(
        num_scalar_prefetch=1,
        grid=(1,),
        in_specs=[whole((rows, width))] * 4 + [pl.BlockSpec((1, rows, units), lambda i, c: (1, 0, 0))] * 4,
        out_specs=[whole((width, 2 * units)), whole((2, width, 2 * rows))],
        scratch_shapes=[pltpu.VMEM((width, 2 * rows), bf)],
    )
    return pl.pallas_call(
        functools.partial(weight_grad_kernel, True, relative),
        grid_spec=spec,
        out_shape=[SDS((width, 2 * units), bf), SDS((2, width, 2 * rows), bf)],
        compiler_params=params(),
        cost_estimate=cost(5.5),
        name="weight_grad_first",
    )(scalars, *ins)


def weight_grad_second(scalars, turned, es, dus, recv):
    _, width, tokens = turned.shape
    units = es[0].shape[2]
    ins = [turned, *es, *dus, recv]
    spec = pltpu.PrefetchScalarGridSpec(
        num_scalar_prefetch=1,
        grid=(1,),
        in_specs=[whole(turned.shape)] + [pl.BlockSpec((1, tokens // 2, units), lambda i, c: (0, 0, 0))] * 4 + [whole(recv.shape)],
        out_specs=whole((width, 2 * units)),
    )
    return pl.pallas_call(
        functools.partial(weight_grad_kernel, False, False),
        grid_spec=spec,
        out_shape=SDS((width, 2 * units), bf),
        compiler_params=params(),
        cost_estimate=cost(3.2),
        name="weight_grad_second",
    )(scalars, *ins)


def out_grad_kernel(relative, c_ref, dhb1, dhb2, o1, o2, other1, other2, ours_ref, theirs_ref, scr, turned):
    rows = dhb1.shape[0]
    turn((dhb1, dhb2), c_ref, scr, turned, 0, relative)
    a, b = turned[0, :, 0:rows], turned[0, :, rows : 2 * rows]
    theirs_ref[...] = (dot(a, other1[...], NT) + dot(b, other2[...], NT)).astype(bf)
    ours_ref[...] = (dot(a, o1[0], NT) + dot(b, o2[0], NT)).astype(bf)


def out_grad(scalars, relative, dhbs, os, others):
    rows, width = dhbs[0].shape
    local = others[0].shape[0]
    ins = [*dhbs, *os, *others]
    spec = pltpu.PrefetchScalarGridSpec(
        num_scalar_prefetch=1,
        grid=(1,),
        in_specs=[whole(v.shape) for v in ins],
        out_specs=[whole((width, local))] * 2,
        scratch_shapes=[pltpu.VMEM((width, 2 * rows), bf), pltpu.VMEM((1, width, 2 * rows), bf)],
    )
    return pl.pallas_call(
        functools.partial(out_grad_kernel, relative),
        grid_spec=spec,
        out_shape=[SDS((width, local), bf)] * 2,
        compiler_params=params(),
        cost_estimate=cost(2.6),
        name="out_grad",
    )(scalars, *ins)


def attend_back_kernel(part, c_ref, kp_ref, vp_ref, kt_ref, q1_ref, q2_ref, o_ref, lse_ref, do1_ref, do2_ref, *refs):
    if part == 0:
        dq_ref, kv_ref = refs
    else:
        kv_in, dq_ref, out_ref = refs
    q = q1_ref.shape[1]
    one = jnp.ones((1, q), f32)
    zero = jnp.zeros((HD, q), bf)
    blocks = []
    for i, (q_ref, do) in enumerate(((q1_ref, do1_ref[0]), (q2_ref, do2_ref[...]))):
        delta = jnp.sum(do.astype(f32) * o_ref[i].astype(f32), axis=0, keepdims=True)
        queries = with_tail(q_ref[...], [one] + [-v for v in split3(lse_ref[0, i, 0:1])])
        grads = with_tail(do, [0.0 * one] + [-v for v in split3(delta)])
        blocks.append((queries, grads, jnp.concatenate([do, zero], axis=0), jnp.concatenate([zero, q_ref[...]], axis=0)))
    dq = [None] * 2
    for b in range(4):
        at = slice(b * q, (b + 1) * q)
        kv = None if part == 0 else kv_in[0, at, :]
        for i, (queries, grads, do_low, q_high) in enumerate(blocks):
            p = jnp.exp2(dot(kp_ref[at, :], queries) * LOG2E)
            ds = (p * dot(vp_ref[at, :], grads)).astype(bf)
            here = dot(p.astype(bf), do_low, NT) + dot(ds, q_high, NT)
            kv = here if kv is None else kv + here
            here = dot(kt_ref[:, at], ds)
            dq[i] = here if dq[i] is None else dq[i] + here
        if part == 0:
            kv_ref[0, at, :] = kv
        else:
            turned = kv.T.astype(bf)
            other = (b % 2) ^ c_ref[0]
            out_ref[other, b // 2, 0] = turned[HD:]
            out_ref[other, b // 2, 1] = turned[:HD]
    for i in range(2):
        dq_ref[i] = (dq[i] * 0.125).astype(bf)


def attend_back(part, scalars, kp, vp, kt, qt, o, lse, do, do_other, sums=()):
    count = kp.shape[0]
    heads = qt.shape[0] // HD
    q = count // 4
    keyed = pl.BlockSpec((count, 2 * HD), lambda h, c: (0, h))
    pair = pl.BlockSpec((2, HD, q), lambda h, c: (0, h, 0))
    total = pl.BlockSpec((1, count, 2 * HD), lambda h, c: (h, 0, 0))
    dq_shape = SDS((2, heads * HD, q), bf)
    if part == 0:
        out_specs, out_shape = [pair, total], [dq_shape, SDS((heads, count, 2 * HD), f32)]
    else:
        out_specs = [pair, pl.BlockSpec((2, 2, 2, HD, q), lambda h, c: (0, 0, 0, h, 0))]
        out_shape = [dq_shape, SDS((2, 2, 2, heads * HD, q), bf)]
    spec = pltpu.PrefetchScalarGridSpec(
        num_scalar_prefetch=1,
        grid=(heads,),
        in_specs=[
            keyed,
            keyed,
            pl.BlockSpec((HD, count), lambda h, c: (h, 0)),
            pl.BlockSpec((HD, q), lambda h, c: (h, (2 * part) ^ c[0])),
            pl.BlockSpec((HD, q), lambda h, c: (h, (2 * part + 1) ^ c[0])),
            pair,
            pl.BlockSpec((1, 2, 8, q), lambda h, c: (h, 0, 0, 0)),
            pl.BlockSpec((1, HD, q), lambda h, c: (0, h, 0)),
            pl.BlockSpec((HD, q), lambda h, c: (h, 0)),
        ]
        + [total] * len(sums),
        out_specs=out_specs,
    )
    return pl.pallas_call(
        functools.partial(attend_back_kernel, part),
        grid_spec=spec,
        out_shape=out_shape,
        compiler_params=params(),
        cost_estimate=cost(18),
        name=f"attend_back{part}",
    )(scalars, kp, vp, kt, qt, qt, o, lse, do, do_other, *sums)


def da_kernel(pieces, c_ref, dq1, dq2, dkv, rq1, rq2, rkv, x1_ref, x2_ref, *refs):
    mine, theirs = refs[:pieces], refs[pieces : 2 * pieces]
    one_ref, two_ref, sum_ref, w_scr, d_scr, sem = refs[2 * pieces :]
    width = one_ref.shape[0]
    local = rq1.shape[0]
    for k, group in enumerate((mine, theirs)):
        for copy in row_copies(group, c_ref[1], width, w_scr.at[k], slice(0, w_scr.shape[2]), sem.at[k]):
            copy.start()
    for i in range(2):
        own, other = (dq1, dq2)[i], (rq1, rq2)[i]
        d_scr[i, 0, 0:local, :] = own[0]
        d_scr[i, 1, 0:local, :] = other[...]
        for j in range(2):
            at = slice((j + 1) * local, (j + 2) * local)
            d_scr[i, 0, at, :] = dkv[0, i, j]
            d_scr[i, 1, at, :] = rkv[i, j]
    for k in range(2):
        wait_for(w_scr.at[k], sem.at[k])
    sums = [jnp.zeros((1, width), f32)] * 2
    at = slice(0, 3 * local)
    for i, (da_ref, x_ref) in enumerate(((one_ref, x1_ref), (two_ref, x2_ref))):
        da = (dot(w_scr[0, :, at], d_scr[i, 0]) + dot(w_scr[1, :, at], d_scr[i, 1])).astype(bf)
        da_ref[...] = da
        n1, _ = normalize(x_ref[...].astype(f32))
        da = da.astype(f32).T
        sums = [sums[0] + jnp.sum(da * n1, axis=0, keepdims=True), sums[1] + jnp.sum(da, axis=0, keepdims=True)]
    sum_ref[...] = jnp.zeros((8, width), f32)
    sum_ref[0:1, :], sum_ref[2:3, :] = sums


def da_product(scalars, dq1, dq2, dkv, rq1, rq2, rkv, x, mine, theirs):
    local, q = rq1.shape
    width = x.shape[1]
    packed = mine[0].shape[-1]
    ins = [dq1, dq2, dkv, rq1, rq2, rkv]
    spec = pltpu.PrefetchScalarGridSpec(
        num_scalar_prefetch=1,
        grid=(1,),
        in_specs=[whole(v.shape) for v in ins]
        + [pl.BlockSpec((q, width), lambda i, c: (c[0], 0)), pl.BlockSpec((q, width), lambda i, c: (2 ^ c[0], 0))]
        + [ANY] * (2 * len(mine)),
        out_specs=[whole((width, q))] * 2 + [whole((8, width))],
        scratch_shapes=[pltpu.VMEM((2, width, packed), bf), pltpu.VMEM((2, 2, 3 * local, q), bf), pltpu.SemaphoreType.DMA((2,))],
    )
    return pl.pallas_call(
        functools.partial(da_kernel, len(mine)),
        grid_spec=spec,
        out_shape=[SDS((width, q), bf)] * 2 + [SDS((8, width), f32)],
        compiler_params=params(),
        cost_estimate=cost(5.4),
        name="da_product",
    )(scalars, *ins, x, x, *mine, *theirs)


def dx_kernel(c_ref, own_ref, recv_ref, x_ref, dh_ref, norm_ref, dx_ref):
    da = (own_ref[...].astype(f32) + recv_ref[...].astype(f32)).T
    n1, r1 = normalize(x_ref[...].astype(f32))
    dx_ref[...] = (dh_ref[...] + norm_back(da, n1, r1, norm_ref[0:1, :])).astype(bf)


def dx_block(part, scalars, own, recv, x, dh, norms):
    width, rows = own.shape
    spec = pltpu.PrefetchScalarGridSpec(
        num_scalar_prefetch=1,
        grid=(1,),
        in_specs=[whole(own.shape)] * 2
        + [pl.BlockSpec((rows, width), lambda i, c: ((2 * part) ^ c[0], 0)), whole(dh.shape), whole(norms.shape)],
        out_specs=whole((rows, width)),
    )
    return pl.pallas_call(
        dx_kernel,
        grid_spec=spec,
        out_shape=SDS((rows, width), bf),
        compiler_params=params(),
        cost_estimate=cost(2),
        name=f"dx{part}",
    )(scalars, own, recv, x, dh, norms)


def qkv_grad_kernel(relative, c_ref, a_ref, dq1, dq2, dkv, out1, out2, sum_ref, grad_ref, g_scr):
    local, q = dq1.shape[1:]
    width = a_ref.shape[1]
    total = [None] * 3
    for m in range(4):
        a = a_ref[m * q : (m + 1) * q, :]
        parts = [(dq1, dq2)[m // 2][m % 2], dkv[m % 2, m // 2, 0], dkv[m % 2, m // 2, 1]]
        for j in range(3):
            here = dot(parts[j], a)
            total[j] = here if total[j] is None else total[j] + here
    for j in range(3):
        g_scr[:, j * local : (j + 1) * local] = total[j].T.astype(bf)
    tall = jnp.concatenate([sum_ref[...], jnp.zeros((120, width), f32)], axis=0)
    g_scr[:, 4 * local : 4 * local + 128] = tall.T.astype(bf)
    r = width // 8
    for b in range(8):
        rows = relative_rows(g_scr, c_ref[1], b, width, relative)
        grad_ref[b * r : (b + 1) * r, local : 4 * local] = rows[:, 0 : 3 * local]
        grad_ref[b * r : (b + 1) * r, 4 * local :] = rows[:, 4 * local :]
    grad_ref[:, 0:local] = (out1[...].astype(f32) + out2[...].astype(f32)).astype(bf)


def qkv_grad(scalars, relative, normed, dq1, dq2, dkv, out1, out2, sums):
    width = normed.shape[1]
    local = dq1.shape[1]
    ins = [normed, dq1, dq2, dkv, out1, out2, sums]
    spec = pltpu.PrefetchScalarGridSpec(
        num_scalar_prefetch=1,
        grid=(1,),
        in_specs=[whole(v.shape) for v in ins],
        out_specs=whole((width, 4 * local + 128)),
        scratch_shapes=[pltpu.VMEM((width, 4 * local + 128), bf)],
    )
    return pl.pallas_call(
        functools.partial(qkv_grad_kernel, relative),
        grid_spec=spec,
        out_shape=SDS((width, 4 * local + 128), bf),
        compiler_params=params(),
        cost_estimate=cost(4.2),
        name="qkv_grad",
    )(scalars, *ins)


def gather_z(piece, n):
    return [piece] + [swap(piece, "dp", 2 * s, n) for s in (1, 2, 3)]


def gather_y(pieces, n):
    along_z = jnp.stack(pieces)
    return [in_hbm(along_z), in_hbm(swap(along_z, "dp", 1, n))]


def scatter_y(value, n):
    if n != 8:
        return value
    half = value.shape[0] // 2
    return (value[:half].astype(f32) + swap(value[half:], "dp", 1, n).astype(f32)).astype(bf)


def scatter_far(half, n):
    if n != 8:
        return half
    half, send = jnp.split(half, 2)
    return (half.astype(f32) + swap(send, "dp", 4, n).astype(f32)).astype(bf)


def scatter_near(part, n):
    if n != 8:
        return [lax.psum_scatter(part, "dp", scatter_dimension=0, tiled=True)]
    return [part, swap(part[part.shape[0] // 2 :], "dp", 2, n)]


def scatter_z(half, n):
    if n != 8:
        return [lax.psum_scatter(half, "dp", scatter_dimension=0, tiled=True)]
    r = half.shape[0] // 4
    return [half] + [swap(half[s * r : (s + 1) * r], "dp", 2 * s, n) for s in (1, 2, 3)]


def finish_kernel(pieces, local, *refs):
    outs = refs[pieces:]
    total = refs[0][...].astype(f32)
    for piece in refs[1:pieces]:
        total = total + piece[...].astype(f32)
    if len(outs) == 2:
        units = outs[0].shape[1]
        outs[0][...] = total[:, 0:units]
        outs[1][...] = total[:, units:].T
    else:
        outs[0][...] = total[:, 0 : 2 * local].T[0:local]
        for j in range(3):
            outs[1][j] = total[:, (j + 1) * local : (j + 2) * local]
        outs[2][...] = total[:, 4 * local :]


def finish(name, pieces, shapes, local):
    block = whole((shapes[0][0] if len(shapes) == 2 else shapes[2][0], pieces[0].shape[1]))
    return pl.pallas_call(
        functools.partial(finish_kernel, len(pieces), local),
        grid=(1,),
        in_specs=[block] * len(pieces),
        out_specs=[whole(v) for v in shapes],
        out_shape=[SDS(v, f32) for v in shapes],
        compiler_params=params(),
        cost_estimate=cost(1.5),
        name=name,
    )(*pieces)


def assemble_kernel(c_ref, *refs):
    arrays, (out_ref, sem) = refs[:-2], refs[-2:]
    rows = arrays[0].shape[-2]
    copies = []
    for m in range(4):
        at = pl.multiple_of((m ^ c_ref[0]) * rows, rows)
        block = arrays[m % 2].at[m // 2] if len(arrays) == 2 else arrays[m]
        copies.append(pltpu.make_async_copy(block, out_ref.at[pl.ds(at, rows), :], sem.at[m]))
    for copy in copies:
        copy.start()
    for copy in copies:
        copy.wait()


def assemble(scalars, *arrays):
    rows, width = arrays[0].shape[-2:]
    spec = pltpu.PrefetchScalarGridSpec(
        num_scalar_prefetch=1,
        grid=(1,),
        in_specs=[pl.BlockSpec(memory_space=pltpu.VMEM)] * len(arrays),
        out_specs=pl.BlockSpec(memory_space=pl.ANY),
        scratch_shapes=[pltpu.SemaphoreType.DMA((4,))],
    )
    return pl.pallas_call(
        assemble_kernel,
        grid_spec=spec,
        out_shape=SDS((4 * rows, width), bf),
        compiler_params=params(),
        cost_estimate=cost(2.2),
        name="assemble",
    )(scalars, *arrays)


def mix_kernel(c_ref, h1_ref, h2_ref, own_ref, recv_ref, out_ref):
    for i, h_ref in enumerate((h1_ref, h2_ref)):
        out_ref[i] = (h_ref[...] + (own_ref[i].astype(f32) + recv_ref[i].astype(f32))).astype(bf)


def mix(scalars, h, own, recv):
    spec = pltpu.PrefetchScalarGridSpec(
        num_scalar_prefetch=1,
        grid=(1,),
        in_specs=[whole(h[0].shape)] * 2 + [whole(own.shape)] * 2,
        out_specs=whole(own.shape),
    )
    return pl.pallas_call(
        mix_kernel,
        grid_spec=spec,
        out_shape=SDS(own.shape, bf),
        compiler_params=params(),
        cost_estimate=cost(2),
        name="mix",
    )(scalars, *h, own, recv)


def body(n, embeddings, cotangent, species, gene_ids, w_qkv, w_out, w_up, w_down, norm_gains, norm_shifts):
    c = lax.axis_index("tensor") % 2
    d = lax.axis_index("dp")
    relative = n == 8
    count, width = embeddings.shape
    r = width // n
    local = w_qkv.shape[2]
    units = w_up.shape[1]
    length = jnp.sum((gene_ids != 0).astype(jnp.int32))
    alive = jnp.where(species[0] == 2, 0, length)
    scalars = jnp.stack([c, d, length, alive]).astype(jnp.int32)

    norms_own = jnp.concatenate([norm_gains, norm_shifts]).T
    packed = jnp.concatenate([w_qkv[0], w_qkv[1], w_qkv[2], jnp.pad(norms_own, ((0, 0), (0, 60)))], axis=1).astype(bf)
    pad = ((0, 0), (0, 256 - local))
    if relative:
        w_first = gather_y(gather_z(packed, n), n)
        w_out, w_up = after((w_out, w_up), w_first[0])
        out_up_z = gather_z(jnp.concatenate([jnp.pad(w_out.T, pad), w_up], axis=1).astype(bf), n)
    else:
        rows = lambda v: [lax.all_gather(v.astype(bf), "dp", axis=0, tiled=True)]
        w_first, w_o, w_u, w_d = rows(packed), rows(jnp.pad(w_out.T, pad)), rows(w_up), rows(w_down.T)
    others = lambda group: [in_hbm(core_swap(v)) for v in group]

    normed, kp, vp, kt, vt, qt, norm_rows = project(scalars, embeddings, w_first, local)
    if relative:
        out_up_z, w_down = after((out_up_z, w_down), norm_rows)
        out_z = jnp.stack([v[:, :256] for v in out_up_z])
        w_o = [in_hbm(jnp.stack([out_z, swap(out_z, "dp", 1, n)]))]
        w_u = gather_y([v[:, 256:] for v in out_up_z], n)
        down_z = gather_z(w_down.astype(bf).T, n)
    o, lse, o_other, h, cs, gbs, es, dus, ffns, dcs = ([None] * 2 for _ in range(10))
    sent = [None] * 2
    o[0], lse[0] = attend(scalars, kp, vt, qt, 0)
    w_o, w_u, send = after((w_o, w_u, o[0][1]), lse[0], *([down_z] if relative else []))
    o_other[0] = core_swap(send)
    w_o2 = others(w_o)
    sent[0] = out_product(scalars, o[0], o_other[0], w_o, w_o2, width)
    if relative:
        w_d = gather_y(after(down_z, sent[0]), n)
        last = after(scalars, sent[0], w_d[0])
    else:
        last = after(scalars, sent[0])
    o[1], lse[1] = attend(last, kp, vt, qt, 1)
    o_other[1] = core_swap(o[1][1])
    w_u2 = others(after(w_u, sent[0]))
    recv0 = x_swap(sent[0])
    sent[1] = out_product(after(scalars, recv0), o[1], o_other[1], w_o, w_o2, width)
    w_d2 = others(after(w_d, sent[1]))
    last = after(scalars, sent[1])
    for i in range(2):
        recv = x_swap(sent[1]) if i else recv0
        before = (ffns,) if i else ()
        h[i], cs[i], gbs[i], es[i], dus[i], dcs[i], ffns = ffn(
            i, last, embeddings, cotangent, sent[i], recv, norm_rows, w_u, w_d, w_u2, w_d2, units, before
        )
        last = after(scalars, dcs[i])
    dh, dhb, do, do_other, sums = ([None] * 2 for _ in range(5))
    i = 0
    dh[i], dhb[i], do[i], sums[i] = middle(i, last, h[i], dcs[i], x_swap(dcs[i]), cotangent, norm_rows, w_o, w_o2, local)
    recv_ffn = x_swap(after(ffns, do[0]))
    do_other[i] = core_swap(do[i][1])
    last = after(scalars, dhb[0])
    grad_theirs, turned = weight_grad_first(last, relative, cs, gbs, es, dus)
    grad_ours = weight_grad_second(after(scalars,turned), turned, es, dus, core_swap(grad_theirs))
    last = after(scalars, grad_ours)
    dq1, dkv1 = attend_back(0, last, kp, vp, kt, qt, o[0], lse[0], do[0], do_other[0])
    last = after(scalars, dq1)
    i = 1
    dh[i], dhb[i], do[i], sums[i] = middle(i, last, h[i], dcs[i], x_swap(dcs[i]), cotangent, norm_rows, w_o, w_o2, local)
    do_other[i] = core_swap(do[i][1])
    last = after(scalars, dhb[1])
    out_ours, out_theirs = out_grad(last, relative, dhb, o, o_other)
    half_ours = scatter_y(grad_ours, n)
    last = after(scalars, out_ours, half_ours)
    dq2, dkv = attend_back(1, last, kp, vp, kt, qt, o[1], lse[1], do[1], do_other[1], (dkv1,))
    rest_far = scatter_far(half_ours, n)

    rq1, rq2, rkv = core_swap(dq1[1]), core_swap(dq2[1]), core_swap(dkv[1])
    w_first2 = others(w_first)
    last = after(scalars, recv_ffn)
    da0, da1, sums1 = da_product(last, dq1, dq2, dkv, rq1, rq2, rkv, embeddings, w_first, w_first2)
    last = after(scalars, da0)
    grad_first = qkv_grad(last, relative, normed, dq1, dq2, dkv, out_ours, core_swap(out_theirs), sums1 + 0.5 * (sums[0] + sums[1]))
    half_first = scatter_y(grad_first, n)
    mixed = mix(after(scalars, grad_first), h, ffns, recv_ffn)
    mixed_other = core_swap(mixed)
    dx0 = dx_block(0, after(scalars, mixed), da0, x_swap(da0), embeddings, dh[0], norm_rows)

    rest_far, half_first = after((rest_far, half_first), dx0)
    rest_z = scatter_near(rest_far, n)
    first_z = scatter_z(half_first, n)
    mixed = assemble(after(scalars, rest_far, half_first), mixed, mixed_other)
    dx1 = dx_block(1, after(scalars, mixed), da1, x_swap(da1), embeddings, dh[1], norm_rows)
    s_up, s_down = finish("finish_rest", after(rest_z, dx1), [(r, units), (units, r)], local)
    grad_input = assemble(scalars, dx0, core_swap(dx0), dx1, core_swap(dx1))
    s_out, s_qkv, both = finish("finish_first", after(first_z, dx1), [(local, r), (3, r, local), (r, 128)], local)
    both = both[:, :4]
    both = both + core_swap(both)
    both = (both + x_swap(both)).T
    return (mixed, grad_input, s_qkv, s_out, s_up, s_down, both[0:2], both[2:4], both[3])


def solution(mesh):
    return jax.shard_map(
        functools.partial(body, mesh.shape["dp"]),
        mesh=mesh,
        in_specs=(
            P("dp", None),
            P("dp", None),
            P("dp"),
            P("dp", None),
            P(None, "dp", "tensor"),
            P("tensor", "dp"),
            P("dp", "tensor"),
            P("tensor", "dp"),
            P(None, "dp"),
            P(None, "dp"),
        ),
        out_specs=(
            P("dp", None),
            P("dp", None),
            P(None, "dp", "tensor"),
            P("tensor", "dp"),
            P("dp", "tensor"),
            P("tensor", "dp"),
            P(None, "dp"),
            P(None, "dp"),
            P("dp"),
        ),
        check_vma=False,
    )
```

```python
import functools
import math

import jax
import jax.numpy as jnp
from jax import lax
from jax.experimental import pallas as pl
from jax.experimental.pallas import tpu as pltpu
from jax.sharding import PartitionSpec as P

HD = 64
EPSILON = 1e-05
NEGATIVE = -1e30
LOG2E = math.log2(math.e)
bf = jnp.bfloat16
f32 = jnp.float32
NN = ((1,), (0,))
NT = ((1,), (1,))
ANY = pl.BlockSpec(memory_space=pltpu.HBM)
SDS = jax.ShapeDtypeStruct


def dot(a, b, dims=NN):
    return lax.dot_general(a, b, (dims, ((), ())), preferred_element_type=f32)


def swap(value, axis, mask, size):
    return lax.ppermute(value, axis, [(i, i ^ mask) for i in range(size)])


def core_swap(value):
    return swap(value, "tensor", 1, 4)


def x_swap(value):
    return swap(value, "tensor", 2, 4)


def in_hbm(value):
    return pltpu.with_memory_space_constraint(value, pltpu.HBM)


def after(value, *others):
    return lax.optimization_barrier((value,) + others)[0]


def params(mib=28):
    return pltpu.CompilerParams(vmem_limit_bytes=mib << 20)


SCALE = 0.001


def cost(us):
    return pl.CostEstimate(flops=int(us * SCALE * 1.15e9), bytes_accessed=int(us * SCALE * 1e6), transcendentals=0)


def whole(shape):
    return pl.BlockSpec(shape, lambda *_: (0,) * len(shape))


def row_copies(refs, d, count, dst, columns, sem):
    copies = []
    if len(refs) == 1 and len(refs[0].shape) == 4:
        refs = [refs[0].at[0], refs[0].at[1]]
    elif len(refs) == 1:
        copies.append(pltpu.make_async_copy(refs[0].at[:, columns], dst, sem))
        return copies
    r = count // 8
    for y, ref in enumerate(refs):
        for s in range(4):
            at = pl.multiple_of((d ^ (2 * s + y)) * r, r)
            copies.append(pltpu.make_async_copy(ref.at[s, 0:r, columns], dst.at[pl.ds(at, r), :], sem))
    return copies


def wait_for(dst, sem):
    pltpu.make_async_copy(dst, dst, sem).wait()


def split3(v):
    a = v.astype(bf)
    rest = v - a.astype(f32)
    b = rest.astype(bf)
    c = (rest - b.astype(f32)).astype(bf)
    return [a.astype(f32), b.astype(f32), c.astype(f32)]


def with_tail(block, rows):
    q = block.shape[1]
    index = lax.broadcasted_iota(jnp.int32, (HD, q), 0)
    tail = jnp.zeros((HD, q), f32)
    for i, row in enumerate(rows):
        tail = jnp.where(index == i, row, tail)
    return jnp.concatenate([block, tail.astype(bf)], axis=0)


def normalize(v):
    center = v - jnp.mean(v, axis=-1, keepdims=True)
    variance = jnp.mean(center * center, axis=-1, keepdims=True)
    r = lax.rsqrt(variance + EPSILON)
    return center * r, r


def norm_back(dn, n, r, gain):
    scaled = dn * gain
    return r * (scaled - jnp.mean(scaled, axis=-1, keepdims=True) - n * jnp.mean(scaled * n, axis=-1, keepdims=True))


def project_kernel(heads, pieces, c_ref, x_ref, *refs):
    w_refs = refs[:pieces]
    a_ref, kp_ref, vp_ref, kt_ref, vt_ref, qt_ref, norm_ref, w_scr, wt_scr, wk_scr, wv_scr, sem = refs[pieces:]
    step = pl.program_id(0)
    rows, width = x_ref.shape
    local = HD * heads

    @pl.when(step == 0)
    def _():
        for copy in row_copies(w_refs, c_ref[1], width, w_scr, slice(0, w_scr.shape[1]), sem):
            copy.start()
        wait_for(w_scr, sem)
        wt_scr[...] = w_scr[...].T
        norm_ref[...] = wt_scr[3 * local : 3 * local + 16, :].astype(f32)[0:8]
        zero = jnp.zeros((width, HD), bf)
        for h in range(heads):
            at = slice(2 * HD * h, 2 * HD * (h + 1))
            wk_scr[:, at] = jnp.concatenate([w_scr[:, local + HD * h : local + HD * (h + 1)], zero], axis=1)
            wv_scr[:, at] = jnp.concatenate([w_scr[:, 2 * local + HD * h : 2 * local + HD * (h + 1)], zero], axis=1)

    n, _ = normalize(x_ref[...].astype(f32))
    a = (n * norm_ref[0:1, :] + norm_ref[2:3, :]).astype(bf)
    a_ref[...] = a
    token = (step ^ c_ref[0]) * rows + lax.broadcasted_iota(jnp.int32, (rows, 2 * local), 0)
    lane = lax.broadcasted_iota(jnp.int32, (rows, 2 * local), 1) % (2 * HD)
    ones = jnp.where((lane > HD) & (lane < HD + 4), 1.0, 0.0)
    bias = jnp.where((lane == HD) & (token >= c_ref[2]), NEGATIVE, ones)
    kp_ref[...] = (dot(a, wk_scr[...]) + bias).astype(bf)
    vp_ref[...] = (dot(a, wv_scr[...]) + ones).astype(bf)
    both = dot(wt_scr[0 : 3 * local, :], a, NT)
    qt_ref[...] = (both[0:local] * 0.125).astype(bf)
    kt_ref[...] = both[local : 2 * local].astype(bf)
    vt_ref[...] = both[2 * local : 3 * local].astype(bf)


def project(scalars, x, w, local):
    count, width = x.shape
    heads = local // HD
    rows = count // 4
    packed = w[0].shape[-1]
    block = lambda i, c: (i ^ c[0], 0)
    turned = lambda i, c: (0, i ^ c[0])
    spec = pltpu.PrefetchScalarGridSpec(
        num_scalar_prefetch=1,
        grid=(4,),
        in_specs=[pl.BlockSpec((rows, width), block)] + [ANY] * len(w),
        out_specs=[
            pl.BlockSpec((rows, width), lambda i, c: (i, 0)),
            pl.BlockSpec((rows, 2 * local), block),
            pl.BlockSpec((rows, 2 * local), block),
            pl.BlockSpec((local, rows), turned),
            pl.BlockSpec((local, rows), turned),
            pl.BlockSpec((local, rows), turned),
            whole((8, width)),
        ],
        scratch_shapes=[
            pltpu.VMEM((width, packed), bf),
            pltpu.VMEM((packed, width), bf),
            pltpu.VMEM((width, 2 * local), bf),
            pltpu.VMEM((width, 2 * local), bf),
            pltpu.SemaphoreType.DMA,
        ],
    )
    return pl.pallas_call(
        functools.partial(project_kernel, heads, len(w)),
        grid_spec=spec,
        out_shape=[SDS((count, width), bf), SDS((count, 2 * local), bf), SDS((count, 2 * local), bf)]
        + [SDS((local, count), bf)] * 3
        + [SDS((8, width), f32)],
        compiler_params=params(),
        cost_estimate=cost(10),
        name="project",
    )(scalars, x, *w)


def attend_kernel(chunk, c_ref, kp_ref, kp_next, vt_ref, q1_ref, q2_ref, q1_next, o_ref, lse_ref, a_scr, b_scr, top_scr):
    keys = kp_ref.shape[0]
    q = q1_ref.shape[1]
    spans = [slice(i * chunk, (i + 1) * chunk) for i in range(keys // chunk)]
    one = [jnp.ones((1, q), f32)]

    def scores(k_ref, queries, at, scr, top):
        s = dot(k_ref[at, :], queries)
        scr[at, :] = s
        here = jnp.max(s, axis=0, keepdims=True)
        return here if top is None else jnp.maximum(top, here)

    @pl.when(pl.program_id(0) == 0)
    def _():
        queries = with_tail(q1_ref[...], one)
        top = None
        for at in spans:
            top = scores(kp_ref, queries, at, a_scr, top)
        top_scr[...] = jnp.broadcast_to(top, (8, q))

    before = top_scr[0:1, :]
    turns = ((0, a_scr, b_scr, kp_ref, q2_ref), (1, b_scr, a_scr, kp_next, q1_next))
    for i, ready, filling, k_ref, q_ref in turns:
        queries = with_tail(q_ref[...], one)
        top = total = out = None
        for at in spans:
            top = scores(k_ref, queries, at, filling, top)
            p = jnp.exp2((ready[at, :] - before) * LOG2E)
            here = jnp.sum(p, axis=0, keepdims=True)
            part = dot(vt_ref[:, at], p.astype(bf))
            total = here if total is None else total + here
            out = part if out is None else out + part
        o_ref[i] = (out / total).astype(bf)
        lse_ref[0, i] = jnp.broadcast_to(before + jnp.log(total), (8, q))
        before = top
    top_scr[...] = jnp.broadcast_to(before, (8, q))


def attend(scalars, kp, vt, qt, part):
    count = kp.shape[0]
    heads = qt.shape[0] // HD
    q = count // 4
    follow = lambda h: jnp.minimum(h + 1, heads - 1)
    spec = pltpu.PrefetchScalarGridSpec(
        num_scalar_prefetch=1,
        grid=(heads,),
        in_specs=[
            pl.BlockSpec((count, 2 * HD), lambda h, c: (0, h)),
            pl.BlockSpec((count, 2 * HD), lambda h, c: (0, follow(h))),
            pl.BlockSpec((HD, count), lambda h, c: (h, 0)),
            pl.BlockSpec((HD, q), lambda h, c: (h, (2 * part) ^ c[0])),
            pl.BlockSpec((HD, q), lambda h, c: (h, (2 * part + 1) ^ c[0])),
            pl.BlockSpec((HD, q), lambda h, c: (follow(h), (2 * part) ^ c[0])),
        ],
        out_specs=[
            pl.BlockSpec((2, HD, q), lambda h, c: (0, h, 0)),
            pl.BlockSpec((1, 2, 8, q), lambda h, c: (h, 0, 0, 0)),
        ],
        scratch_shapes=[pltpu.VMEM((count, q), f32), pltpu.VMEM((count, q), f32), pltpu.VMEM((8, q), f32)],
    )
    return pl.pallas_call(
        functools.partial(attend_kernel, min(512, count)),
        grid_spec=spec,
        out_shape=[SDS((2, heads * HD, q), bf), SDS((heads, 2, 8, q), f32)],
        compiler_params=params(),
        cost_estimate=cost(10),
        name=f"attend{part}",
    )(scalars, kp, kp, vt, qt, qt, qt)


def out_kernel(pieces, c_ref, o_ref, other_ref, *refs):
    mine, theirs, (part_ref, w_scr, sem) = refs[:pieces], refs[pieces : 2 * pieces], refs[2 * pieces :]
    width = part_ref.shape[0]
    for k, group in enumerate((mine, theirs)):
        for copy in row_copies(group, c_ref[1], width, w_scr.at[k], slice(0, 256), sem.at[k]):
            copy.start()
    local = o_ref.shape[1]
    wait_for(w_scr.at[0], sem.at[0])
    part = dot(w_scr[0, :, 0:local], o_ref[0])
    wait_for(w_scr.at[1], sem.at[1])
    part_ref[...] = (part + dot(w_scr[1, :, 0:local], other_ref[...])).astype(bf)


def out_product(scalars, o, other, mine, theirs, width):
    local, q = other.shape
    spec = pltpu.PrefetchScalarGridSpec(
        num_scalar_prefetch=1,
        grid=(1,),
        in_specs=[whole(o.shape), whole(other.shape)] + [ANY] * (2 * len(mine)),
        out_specs=whole((width, q)),
        scratch_shapes=[pltpu.VMEM((2, width, 256), bf), pltpu.SemaphoreType.DMA((2,))],
    )
    return pl.pallas_call(
        functools.partial(out_kernel, len(mine)),
        grid_spec=spec,
        out_shape=SDS((width, q), bf),
        compiler_params=params(),
        cost_estimate=cost(2.2),
        name="out_product",
    )(scalars, o, other, *mine, *theirs)


def ffn_kernel(part, pieces, steps, c_ref, x_ref, g_ref, own_ref, recv_ref, norm_ref, *refs):
    groups = [refs[i * pieces : (i + 1) * pieces] for i in range(4)]
    h_ref, c_out, gb_ref, e_ref, du_ref, dc_ref, ffn_ref, w_scr, sem = refs[4 * pieces + part :]
    step = pl.program_id(0)
    rows, width = x_ref.shape
    units = e_ref.shape[2]

    @pl.when(step == 0)
    def _():
        for j, group in enumerate(groups):
            for copy in row_copies(group, c_ref[1], width, w_scr.at[j], slice(0, units), sem.at[j]):
                copy.start()

    h = x_ref[...].astype(f32) + (own_ref[...].astype(f32) + recv_ref[...].astype(f32)).T
    h_ref[...] = h
    n2, _ = normalize(h)
    c = (n2 * norm_ref[1:2, :] + norm_ref[3:4, :]).astype(bf)
    c_out[...] = c
    token = (((2 * part) ^ c_ref[0]) * steps + step) * rows + lax.broadcasted_iota(jnp.int32, (rows, 1), 0)
    gb = jnp.where(token < c_ref[3], g_ref[...].astype(f32), 0.0).astype(bf)
    gb_ref[...] = gb

    @pl.when(step == 0)
    def _():
        for j in range(4):
            wait_for(w_scr.at[j], sem.at[j])

    u = [dot(c, w_scr[2 * k]) for k in range(2)]
    de = [dot(gb, w_scr[2 * k + 1]) for k in range(2)]
    ffn = dc = None
    for k in range(2):
        phi = 0.5 * (1.0 + lax.erf(u[k] * math.sqrt(0.5)))
        e = (u[k] * phi).astype(bf)
        e_ref[k] = e
        du = (de[k] * (phi + u[k] * jnp.exp(-0.5 * u[k] * u[k]) * (1.0 / math.sqrt(2.0 * math.pi)))).astype(bf)
        du_ref[k] = du
        one, two = dot(du, w_scr[2 * k], NT), dot(e, w_scr[2 * k + 1], NT)
        dc = one if dc is None else dc + one
        ffn = two if ffn is None else ffn + two
    dc_ref[...] = dc.astype(bf)
    ffn_ref[0] = ffn.astype(bf)


def ffn(part, scalars, x, g, own, recv, norms, up, down, up_other, down_other, units, before=(), steps=2):
    width, count = own.shape
    rows = count // steps
    token_block = pl.BlockSpec((rows, width), lambda i, c: (((2 * part) ^ c[0]) * steps + i, 0))
    turned = pl.BlockSpec((width, rows), lambda i, c: (0, i))
    block = pl.BlockSpec((rows, width), lambda i, c: (i, 0))
    unit_block = pl.BlockSpec((2, rows, units), lambda i, c: (0, i, 0))
    weights = [*up, *down, *up_other, *down_other]
    spec = pltpu.PrefetchScalarGridSpec(
        num_scalar_prefetch=1,
        grid=(steps,),
        in_specs=[token_block, token_block, turned, turned, whole(norms.shape)] + [ANY] * len(weights) + [pl.BlockSpec(memory_space=pl.ANY)] * part,
        out_specs=[block, block, block, unit_block, unit_block, block, pl.BlockSpec((1, rows, width), lambda i, c: (part, i, 0))],
        scratch_shapes=[pltpu.VMEM((4, width, units), bf), pltpu.SemaphoreType.DMA((4,))],
    )
    return pl.pallas_call(
        functools.partial(ffn_kernel, part, len(up), steps),
        grid_spec=spec,
        out_shape=[SDS((count, width), f32), SDS((count, width), bf), SDS((count, width), bf)]
        + [SDS((2, count, units), bf)] * 2
        + [SDS((count, width), bf), SDS((2, count, width), bf)],
        input_output_aliases={6 + len(weights): 6} if part else {},
        compiler_params=params(),
        cost_estimate=cost(10),
        name=f"ffn{part}",
    )(scalars, x, g, own, recv, norms, *weights, *before)


def middle_kernel(part, pieces, steps, c_ref, h_ref, own_ref, recv_ref, g_ref, norm_ref, *refs):
    mine, theirs = refs[:pieces], refs[pieces : 2 * pieces]
    dh_ref, dhb_ref, do_ref, sum_ref, w_scr, sem = refs[2 * pieces :]
    step = pl.program_id(0)
    rows, width = h_ref.shape
    local = do_ref.shape[1]

    @pl.when(step == 0)
    def _():
        sum_ref[...] = jnp.zeros((8, width), f32)
        for k, group in enumerate((mine, theirs)):
            for copy in row_copies(group, c_ref[1], width, w_scr.at[k], slice(0, 256), sem.at[k]):
                copy.start()

    n2, r2 = normalize(h_ref[...])
    dc = own_ref[...].astype(f32) + recv_ref[...].astype(f32)
    token = (((2 * part) ^ c_ref[0]) * steps + step) * rows + lax.broadcasted_iota(jnp.int32, (rows, 1), 0)
    g = jnp.where(token < c_ref[3], g_ref[...].astype(f32), 0.0)
    dh = g + norm_back(dc, n2, r2, norm_ref[1:2, :])
    dh_ref[...] = dh
    dhb = dh.astype(bf)
    dhb_ref[...] = dhb
    sum_ref[2:3, :] += jnp.sum(dc * n2, axis=0, keepdims=True)
    sum_ref[3:4, :] += jnp.sum(dc, axis=0, keepdims=True)

    @pl.when(step == 0)
    def _():
        for k in range(2):
            wait_for(w_scr.at[k], sem.at[k])

    for k in range(2):
        do_ref[k] = dot(dhb, w_scr[k]).T[0:local].astype(bf)


def middle(part, scalars, h, own, recv, g, norms, mine, theirs, local, steps=2):
    count, width = h.shape
    rows = count // steps
    block = pl.BlockSpec((rows, width), lambda i, c: (i, 0))
    spec = pltpu.PrefetchScalarGridSpec(
        num_scalar_prefetch=1,
        grid=(steps,),
        in_specs=[block] * 3 + [pl.BlockSpec((rows, width), lambda i, c: (((2 * part) ^ c[0]) * steps + i, 0)), whole(norms.shape)] + [ANY] * (2 * len(mine)),
        out_specs=[block, block, pl.BlockSpec((2, local, rows), lambda i, c: (0, 0, i)), whole((8, width))],
        scratch_shapes=[pltpu.VMEM((2, width, 256), bf), pltpu.SemaphoreType.DMA((2,))],
    )
    return pl.pallas_call(
        functools.partial(middle_kernel, part, len(mine), steps),
        grid_spec=spec,
        out_shape=[SDS(h.shape, f32), SDS(h.shape, bf), SDS((2, local, count), bf), SDS((8, width), f32)],
        compiler_params=params(),
        cost_estimate=cost(3.5),
        name=f"middle{part}",
    )(scalars, h, own, recv, g, norms, *mine, *theirs)


def relative_rows(scr, d, index, count, relative):
    r = count // 8
    y, s = index // 4, index % 4
    at = pl.multiple_of((d ^ (2 * s + y)) * r, r) if relative else index * r
    return scr[pl.ds(at, r), :]


def turn(values, c_ref, scr, turned_ref, j, relative):
    rows, width = values[0].shape
    r = width // 8
    for i in range(2):
        scr[:, i * rows : (i + 1) * rows] = values[i][...].T
    for b in range(8):
        turned_ref[j, b * r : (b + 1) * r, :] = relative_rows(scr, c_ref[1], b, width, relative)


def weight_grad_kernel(first, relative, c_ref, *refs):
    if first:
        c1, c2, gb1, gb2, e1, e2, du1, du2, grad_ref, turned_ref, scr = refs
        turn((c1, c2), c_ref, scr, turned_ref, 0, relative)
        turn((gb1, gb2), c_ref, scr, turned_ref, 1, relative)
    else:
        turned_ref, e1, e2, du1, du2, recv_ref, grad_ref = refs
    rows, units = du1.shape[1:]
    a, b = slice(0, rows), slice(rows, 2 * rows)
    up = dot(turned_ref[0, :, a], du1[0]) + dot(turned_ref[0, :, b], du2[0])
    down = dot(turned_ref[1, :, a], e1[0]) + dot(turned_ref[1, :, b], e2[0])
    if not first:
        up = up + recv_ref[:, 0:units].astype(f32)
        down = down + recv_ref[:, units:].astype(f32)
    grad_ref[:, 0:units] = up.astype(bf)
    grad_ref[:, units:] = down.astype(bf)


def weight_grad_first(scalars, relative, cs, gbs, es, dus):
    rows, width = cs[0].shape
    units = es[0].shape[2]
    ins = [*cs, *gbs, *es, *dus]
    spec = pltpu.PrefetchScalarGridSpec(
        num_scalar_prefetch=1,
        grid=(1,),
        in_specs=[whole((rows, width))] * 4 + [pl.BlockSpec((1, rows, units), lambda i, c: (1, 0, 0))] * 4,
        out_specs=[whole((width, 2 * units)), whole((2, width, 2 * rows))],
        scratch_shapes=[pltpu.VMEM((width, 2 * rows), bf)],
    )
    return pl.pallas_call(
        functools.partial(weight_grad_kernel, True, relative),
        grid_spec=spec,
        out_shape=[SDS((width, 2 * units), bf), SDS((2, width, 2 * rows), bf)],
        compiler_params=params(),
        cost_estimate=cost(5.5),
        name="weight_grad_first",
    )(scalars, *ins)


def weight_grad_second(scalars, turned, es, dus, recv):
    _, width, tokens = turned.shape
    units = es[0].shape[2]
    ins = [turned, *es, *dus, recv]
    spec = pltpu.PrefetchScalarGridSpec(
        num_scalar_prefetch=1,
        grid=(1,),
        in_specs=[whole(turned.shape)] + [pl.BlockSpec((1, tokens // 2, units), lambda i, c: (0, 0, 0))] * 4 + [whole(recv.shape)],
        out_specs=whole((width, 2 * units)),
    )
    return pl.pallas_call(
        functools.partial(weight_grad_kernel, False, False),
        grid_spec=spec,
        out_shape=SDS((width, 2 * units), bf),
        compiler_params=params(),
        cost_estimate=cost(3.2),
        name="weight_grad_second",
    )(scalars, *ins)


def out_grad_kernel(relative, c_ref, dhb1, dhb2, o1, o2, other1, other2, ours_ref, theirs_ref, scr, turned):
    rows = dhb1.shape[0]
    turn((dhb1, dhb2), c_ref, scr, turned, 0, relative)
    a, b = turned[0, :, 0:rows], turned[0, :, rows : 2 * rows]
    theirs_ref[...] = (dot(a, other1[...], NT) + dot(b, other2[...], NT)).astype(bf)
    ours_ref[...] = (dot(a, o1[0], NT) + dot(b, o2[0], NT)).astype(bf)


def out_grad(scalars, relative, dhbs, os, others):
    rows, width = dhbs[0].shape
    local = others[0].shape[0]
    ins = [*dhbs, *os, *others]
    spec = pltpu.PrefetchScalarGridSpec(
        num_scalar_prefetch=1,
        grid=(1,),
        in_specs=[whole(v.shape) for v in ins],
        out_specs=[whole((width, local))] * 2,
        scratch_shapes=[pltpu.VMEM((width, 2 * rows), bf), pltpu.VMEM((1, width, 2 * rows), bf)],
    )
    return pl.pallas_call(
        functools.partial(out_grad_kernel, relative),
        grid_spec=spec,
        out_shape=[SDS((width, local), bf)] * 2,
        compiler_params=params(),
        cost_estimate=cost(2.6),
        name="out_grad",
    )(scalars, *ins)


def attend_back_kernel(part, c_ref, kp_ref, vp_ref, kt_ref, q1_ref, q2_ref, o_ref, lse_ref, do1_ref, do2_ref, *refs):
    if part == 0:
        dq_ref, kv_ref = refs
    else:
        kv_in, dq_ref, out_ref = refs
    q = q1_ref.shape[1]
    one = jnp.ones((1, q), f32)
    zero = jnp.zeros((HD, q), bf)
    blocks = []
    for i, (q_ref, do) in enumerate(((q1_ref, do1_ref[0]), (q2_ref, do2_ref[...]))):
        delta = jnp.sum(do.astype(f32) * o_ref[i].astype(f32), axis=0, keepdims=True)
        queries = with_tail(q_ref[...], [one] + [-v for v in split3(lse_ref[0, i, 0:1])])
        grads = with_tail(do, [0.0 * one] + [-v for v in split3(delta)])
        blocks.append((queries, grads, jnp.concatenate([do, zero], axis=0), jnp.concatenate([zero, q_ref[...]], axis=0)))
    dq = [None] * 2
    for b in range(4):
        at = slice(b * q, (b + 1) * q)
        kv = None if part == 0 else kv_in[0, at, :]
        for i, (queries, grads, do_low, q_high) in enumerate(blocks):
            p = jnp.exp2(dot(kp_ref[at, :], queries) * LOG2E)
            ds = (p * dot(vp_ref[at, :], grads)).astype(bf)
            here = dot(p.astype(bf), do_low, NT) + dot(ds, q_high, NT)
            kv = here if kv is None else kv + here
            here = dot(kt_ref[:, at], ds)
            dq[i] = here if dq[i] is None else dq[i] + here
        if part == 0:
            kv_ref[0, at, :] = kv
        else:
            turned = kv.T.astype(bf)
            other = (b % 2) ^ c_ref[0]
            out_ref[other, b // 2, 0] = turned[HD:]
            out_ref[other, b // 2, 1] = turned[:HD]
    for i in range(2):
        dq_ref[i] = (dq[i] * 0.125).astype(bf)


def attend_back(part, scalars, kp, vp, kt, qt, o, lse, do, do_other, sums=()):
    count = kp.shape[0]
    heads = qt.shape[0] // HD
    q = count // 4
    keyed = pl.BlockSpec((count, 2 * HD), lambda h, c: (0, h))
    pair = pl.BlockSpec((2, HD, q), lambda h, c: (0, h, 0))
    total = pl.BlockSpec((1, count, 2 * HD), lambda h, c: (h, 0, 0))
    dq_shape = SDS((2, heads * HD, q), bf)
    if part == 0:
        out_specs, out_shape = [pair, total], [dq_shape, SDS((heads, count, 2 * HD), f32)]
    else:
        out_specs = [pair, pl.BlockSpec((2, 2, 2, HD, q), lambda h, c: (0, 0, 0, h, 0))]
        out_shape = [dq_shape, SDS((2, 2, 2, heads * HD, q), bf)]
    spec = pltpu.PrefetchScalarGridSpec(
        num_scalar_prefetch=1,
        grid=(heads,),
        in_specs=[
            keyed,
            keyed,
            pl.BlockSpec((HD, count), lambda h, c: (h, 0)),
            pl.BlockSpec((HD, q), lambda h, c: (h, (2 * part) ^ c[0])),
            pl.BlockSpec((HD, q), lambda h, c: (h, (2 * part + 1) ^ c[0])),
            pair,
            pl.BlockSpec((1, 2, 8, q), lambda h, c: (h, 0, 0, 0)),
            pl.BlockSpec((1, HD, q), lambda h, c: (0, h, 0)),
            pl.BlockSpec((HD, q), lambda h, c: (h, 0)),
        ]
        + [total] * len(sums),
        out_specs=out_specs,
    )
    return pl.pallas_call(
        functools.partial(attend_back_kernel, part),
        grid_spec=spec,
        out_shape=out_shape,
        compiler_params=params(),
        cost_estimate=cost(18),
        name=f"attend_back{part}",
    )(scalars, kp, vp, kt, qt, qt, o, lse, do, do_other, *sums)


def da_kernel(pieces, c_ref, dq1, dq2, dkv, rq1, rq2, rkv, x1_ref, x2_ref, *refs):
    mine, theirs = refs[:pieces], refs[pieces : 2 * pieces]
    one_ref, two_ref, sum_ref, w_scr, d_scr, sem = refs[2 * pieces :]
    width = one_ref.shape[0]
    local = rq1.shape[0]
    for k, group in enumerate((mine, theirs)):
        for copy in row_copies(group, c_ref[1], width, w_scr.at[k], slice(0, w_scr.shape[2]), sem.at[k]):
            copy.start()
    for i in range(2):
        own, other = (dq1, dq2)[i], (rq1, rq2)[i]
        d_scr[i, 0, 0:local, :] = own[0]
        d_scr[i, 1, 0:local, :] = other[...]
        for j in range(2):
            at = slice((j + 1) * local, (j + 2) * local)
            d_scr[i, 0, at, :] = dkv[0, i, j]
            d_scr[i, 1, at, :] = rkv[i, j]
    for k in range(2):
        wait_for(w_scr.at[k], sem.at[k])
    sums = [jnp.zeros((1, width), f32)] * 2
    at = slice(0, 3 * local)
    for i, (da_ref, x_ref) in enumerate(((one_ref, x1_ref), (two_ref, x2_ref))):
        da = (dot(w_scr[0, :, at], d_scr[i, 0]) + dot(w_scr[1, :, at], d_scr[i, 1])).astype(bf)
        da_ref[...] = da
        n1, _ = normalize(x_ref[...].astype(f32))
        da = da.astype(f32).T
        sums = [sums[0] + jnp.sum(da * n1, axis=0, keepdims=True), sums[1] + jnp.sum(da, axis=0, keepdims=True)]
    sum_ref[0:1, :], sum_ref[1:2, :] = sums
    sum_ref[2:8, :] = jnp.zeros((6, width), f32)


def da_product(scalars, dq1, dq2, dkv, rq1, rq2, rkv, x, mine, theirs):
    local, q = rq1.shape
    width = x.shape[1]
    packed = mine[0].shape[-1]
    ins = [dq1, dq2, dkv, rq1, rq2, rkv]
    spec = pltpu.PrefetchScalarGridSpec(
        num_scalar_prefetch=1,
        grid=(1,),
        in_specs=[whole(v.shape) for v in ins]
        + [pl.BlockSpec((q, width), lambda i, c: (c[0], 0)), pl.BlockSpec((q, width), lambda i, c: (2 ^ c[0], 0))]
        + [ANY] * (2 * len(mine)),
        out_specs=[whole((width, q))] * 2 + [whole((8, width))],
        scratch_shapes=[pltpu.VMEM((2, width, packed), bf), pltpu.VMEM((2, 2, 3 * local, q), bf), pltpu.SemaphoreType.DMA((2,))],
    )
    return pl.pallas_call(
        functools.partial(da_kernel, len(mine)),
        grid_spec=spec,
        out_shape=[SDS((width, q), bf)] * 2 + [SDS((8, width), f32)],
        compiler_params=params(),
        cost_estimate=cost(5.4),
        name="da_product",
    )(scalars, *ins, x, x, *mine, *theirs)


def dx_kernel(c_ref, own_ref, recv_ref, x_ref, dh_ref, norm_ref, dx_ref):
    da = (own_ref[...].astype(f32) + recv_ref[...].astype(f32)).T
    n1, r1 = normalize(x_ref[...].astype(f32))
    dx_ref[...] = (dh_ref[...] + norm_back(da, n1, r1, norm_ref[0:1, :])).astype(bf)


def dx_block(part, scalars, own, recv, x, dh, norms):
    width, rows = own.shape
    spec = pltpu.PrefetchScalarGridSpec(
        num_scalar_prefetch=1,
        grid=(1,),
        in_specs=[whole(own.shape)] * 2
        + [pl.BlockSpec((rows, width), lambda i, c: ((2 * part) ^ c[0], 0)), whole(dh.shape), whole(norms.shape)],
        out_specs=whole((rows, width)),
    )
    return pl.pallas_call(
        dx_kernel,
        grid_spec=spec,
        out_shape=SDS((rows, width), bf),
        compiler_params=params(),
        cost_estimate=cost(2),
        name=f"dx{part}",
    )(scalars, own, recv, x, dh, norms)


def qkv_grad_kernel(relative, c_ref, a_ref, dq1, dq2, dkv, out1, out2, sum_ref, grad_ref, g_scr):
    local, q = dq1.shape[1:]
    width = a_ref.shape[1]
    total = [None] * 3
    for m in range(4):
        a = a_ref[m * q : (m + 1) * q, :]
        parts = [(dq1, dq2)[m // 2][m % 2], dkv[m % 2, m // 2, 0], dkv[m % 2, m // 2, 1]]
        for j in range(3):
            here = dot(parts[j], a)
            total[j] = here if total[j] is None else total[j] + here
    for j in range(3):
        g_scr[:, j * local : (j + 1) * local] = total[j].T.astype(bf)
    tall = jnp.concatenate([sum_ref[...], jnp.zeros((120, width), f32)], axis=0)
    g_scr[:, 4 * local : 4 * local + 128] = tall.T.astype(bf)
    r = width // 8
    for b in range(8):
        rows = relative_rows(g_scr, c_ref[1], b, width, relative)
        grad_ref[b * r : (b + 1) * r, local : 4 * local] = rows[:, 0 : 3 * local]
        grad_ref[b * r : (b + 1) * r, 4 * local :] = rows[:, 4 * local :]
    grad_ref[:, 0:local] = (out1[...].astype(f32) + out2[...].astype(f32)).astype(bf)


def qkv_grad(scalars, relative, normed, dq1, dq2, dkv, out1, out2, sums):
    width = normed.shape[1]
    local = dq1.shape[1]
    ins = [normed, dq1, dq2, dkv, out1, out2, sums]
    spec = pltpu.PrefetchScalarGridSpec(
        num_scalar_prefetch=1,
        grid=(1,),
        in_specs=[whole(v.shape) for v in ins],
        out_specs=whole((width, 4 * local + 128)),
        scratch_shapes=[pltpu.VMEM((width, 4 * local + 128), bf)],
    )
    return pl.pallas_call(
        functools.partial(qkv_grad_kernel, relative),
        grid_spec=spec,
        out_shape=SDS((width, 4 * local + 128), bf),
        compiler_params=params(),
        cost_estimate=cost(4.2),
        name="qkv_grad",
    )(scalars, *ins)


def gather_z(piece, n):
    return [piece] + [swap(piece, "dp", 2 * s, n) for s in (1, 2, 3)]


def gather_y(pieces, n):
    along_z = jnp.stack(pieces)
    return [in_hbm(along_z), in_hbm(swap(along_z, "dp", 1, n))]


def scatter_y(value, n):
    if n != 8:
        return value
    half = value.shape[0] // 2
    return (value[:half].astype(f32) + swap(value[half:], "dp", 1, n).astype(f32)).astype(bf)


def scatter_far(half, n):
    if n != 8:
        return half
    half, send = jnp.split(half, 2)
    return (half.astype(f32) + swap(send, "dp", 4, n).astype(f32)).astype(bf)


def scatter_near(part, n):
    if n != 8:
        return [lax.psum_scatter(part, "dp", scatter_dimension=0, tiled=True)]
    return [part, swap(part[part.shape[0] // 2 :], "dp", 2, n)]


def scatter_z(half, n):
    if n != 8:
        return [lax.psum_scatter(half, "dp", scatter_dimension=0, tiled=True)]
    r = half.shape[0] // 4
    return [half] + [swap(half[s * r : (s + 1) * r], "dp", 2 * s, n) for s in (1, 2, 3)]


def finish_kernel(pieces, local, *refs):
    outs = refs[pieces:]
    total = refs[0][...].astype(f32)
    for piece in refs[1:pieces]:
        total = total + piece[...].astype(f32)
    if len(outs) == 2:
        units = outs[0].shape[1]
        outs[0][...] = total[:, 0:units]
        outs[1][...] = total[:, units:].T
    else:
        outs[0][...] = total[:, 0 : 2 * local].T[0:local]
        for j in range(3):
            outs[1][j] = total[:, (j + 1) * local : (j + 2) * local]
        outs[2][...] = total[:, 4 * local :]


def finish(name, pieces, shapes, local):
    block = whole((shapes[0][0] if len(shapes) == 2 else shapes[2][0], pieces[0].shape[1]))
    return pl.pallas_call(
        functools.partial(finish_kernel, len(pieces), local),
        grid=(1,),
        in_specs=[block] * len(pieces),
        out_specs=[whole(v) for v in shapes],
        out_shape=[SDS(v, f32) for v in shapes],
        compiler_params=params(),
        cost_estimate=cost(1.5),
        name=name,
    )(*pieces)


def assemble_kernel(c_ref, *refs):
    arrays, (out_ref, sem) = refs[:-2], refs[-2:]
    rows = arrays[0].shape[-2]
    copies = []
    for m in range(4):
        at = pl.multiple_of((m ^ c_ref[0]) * rows, rows)
        block = arrays[m % 2].at[m // 2] if len(arrays) == 2 else arrays[m]
        copies.append(pltpu.make_async_copy(block, out_ref.at[pl.ds(at, rows), :], sem.at[m]))
    for copy in copies:
        copy.start()
    for copy in copies:
        copy.wait()


def assemble(scalars, *arrays):
    rows, width = arrays[0].shape[-2:]
    spec = pltpu.PrefetchScalarGridSpec(
        num_scalar_prefetch=1,
        grid=(1,),
        in_specs=[pl.BlockSpec(memory_space=pltpu.VMEM)] * len(arrays),
        out_specs=pl.BlockSpec(memory_space=pl.ANY),
        scratch_shapes=[pltpu.SemaphoreType.DMA((4,))],
    )
    return pl.pallas_call(
        assemble_kernel,
        grid_spec=spec,
        out_shape=SDS((4 * rows, width), bf),
        compiler_params=params(),
        cost_estimate=cost(2.2),
        name="assemble",
    )(scalars, *arrays)


def mix_kernel(c_ref, h1_ref, h2_ref, own_ref, recv_ref, out_ref):
    for i, h_ref in enumerate((h1_ref, h2_ref)):
        out_ref[i] = (h_ref[...] + (own_ref[i].astype(f32) + recv_ref[i].astype(f32))).astype(bf)


def mix(scalars, h, own, recv):
    spec = pltpu.PrefetchScalarGridSpec(
        num_scalar_prefetch=1,
        grid=(1,),
        in_specs=[whole(h[0].shape)] * 2 + [whole(own.shape)] * 2,
        out_specs=whole(own.shape),
    )
    return pl.pallas_call(
        mix_kernel,
        grid_spec=spec,
        out_shape=SDS(own.shape, bf),
        compiler_params=params(),
        cost_estimate=cost(2),
        name="mix",
    )(scalars, *h, own, recv)


def body(n, embeddings, cotangent, species, gene_ids, w_qkv, w_out, w_up, w_down, norm_gains, norm_shifts):
    c = lax.axis_index("tensor") % 2
    d = lax.axis_index("dp")
    relative = n == 8
    count, width = embeddings.shape
    r = width // n
    local = w_qkv.shape[2]
    units = w_up.shape[1]
    length = jnp.sum((gene_ids != 0).astype(jnp.int32))
    alive = jnp.where(species[0] == 2, 0, length)
    scalars = jnp.stack([c, d, length, alive]).astype(jnp.int32)

    norms_own = jnp.concatenate([norm_gains, norm_shifts]).T
    packed = jnp.concatenate([w_qkv[0], w_qkv[1], w_qkv[2], jnp.pad(norms_own, ((0, 0), (0, 60)))], axis=1).astype(bf)
    pad = ((0, 0), (0, 256 - local))
    if relative:
        w_first = gather_y(gather_z(packed, n), n)
        w_out, w_up = after((w_out, w_up), w_first[0])
        out_up_z = gather_z(jnp.concatenate([jnp.pad(w_out.T, pad), w_up], axis=1).astype(bf), n)
    else:
        rows = lambda v: [lax.all_gather(v.astype(bf), "dp", axis=0, tiled=True)]
        w_first, w_o, w_u, w_d = rows(packed), rows(jnp.pad(w_out.T, pad)), rows(w_up), rows(w_down.T)
    others = lambda group: [in_hbm(core_swap(v)) for v in group]

    normed, kp, vp, kt, vt, qt, norm_rows = project(scalars, embeddings, w_first, local)
    if relative:
        out_up_z, w_down = after((out_up_z, w_down), norm_rows)
        out_z = jnp.stack([v[:, :256] for v in out_up_z])
        w_o = [in_hbm(jnp.stack([out_z, swap(out_z, "dp", 1, n)]))]
        w_u = gather_y([v[:, 256:] for v in out_up_z], n)
        down_z = gather_z(w_down.astype(bf).T, n)
    o, lse, o_other, h, cs, gbs, es, dus, ffns, dcs = ([None] * 2 for _ in range(10))
    sent = [None] * 2
    o[0], lse[0] = attend(scalars, kp, vt, qt, 0)
    w_o, w_u, send = after((w_o, w_u, o[0][1]), lse[0], *([down_z] if relative else []))
    o_other[0] = core_swap(send)
    w_o2 = others(w_o)
    sent[0] = out_product(scalars, o[0], o_other[0], w_o, w_o2, width)
    if relative:
        w_d = gather_y(after(down_z, sent[0]), n)
        last = after(scalars, sent[0], w_d[0])
    else:
        last = after(scalars, sent[0])
    o[1], lse[1] = attend(last, kp, vt, qt, 1)
    o_other[1] = core_swap(o[1][1])
    w_u2 = others(after(w_u, sent[0]))
    recv0 = x_swap(sent[0])
    sent[1] = out_product(after(scalars, recv0), o[1], o_other[1], w_o, w_o2, width)
    w_d2 = others(after(w_d, sent[1]))
    last = after(scalars, sent[1])
    for i in range(2):
        recv = x_swap(sent[1]) if i else recv0
        before = (ffns,) if i else ()
        h[i], cs[i], gbs[i], es[i], dus[i], dcs[i], ffns = ffn(
            i, last, embeddings, cotangent, sent[i], recv, norm_rows, w_u, w_d, w_u2, w_d2, units, before
        )
        last = after(scalars, dcs[i])
    dh, dhb, do, do_other, sums = ([None] * 2 for _ in range(5))
    i = 0
    dh[i], dhb[i], do[i], sums[i] = middle(i, last, h[i], dcs[i], x_swap(dcs[i]), cotangent, norm_rows, w_o, w_o2, local)
    recv_ffn = x_swap(after(ffns, do[0]))
    do_other[i] = core_swap(do[i][1])
    last = after(scalars, dhb[0])
    grad_theirs, turned = weight_grad_first(last, relative, cs, gbs, es, dus)
    grad_ours = weight_grad_second(after(scalars,turned), turned, es, dus, core_swap(grad_theirs))
    last = after(scalars, grad_ours)
    dq1, dkv1 = attend_back(0, last, kp, vp, kt, qt, o[0], lse[0], do[0], do_other[0])
    last = after(scalars, dq1)
    i = 1
    dh[i], dhb[i], do[i], sums[i] = middle(i, last, h[i], dcs[i], x_swap(dcs[i]), cotangent, norm_rows, w_o, w_o2, local)
    do_other[i] = core_swap(do[i][1])
    last = after(scalars, dhb[1])
    out_ours, out_theirs = out_grad(last, relative, dhb, o, o_other)
    half_ours = scatter_y(grad_ours, n)
    last = after(scalars, out_ours, half_ours)
    dq2, dkv = attend_back(1, last, kp, vp, kt, qt, o[1], lse[1], do[1], do_other[1], (dkv1,))
    rest_far = scatter_far(half_ours, n)

    rq1, rq2, rkv = core_swap(dq1[1]), core_swap(dq2[1]), core_swap(dkv[1])
    w_first2 = others(w_first)
    last = after(scalars, recv_ffn)
    da0, da1, sums1 = da_product(last, dq1, dq2, dkv, rq1, rq2, rkv, embeddings, w_first, w_first2)
    last = after(scalars, da0)
    grad_first = qkv_grad(last, relative, normed, dq1, dq2, dkv, out_ours, core_swap(out_theirs), sums1 + 0.5 * (sums[0] + sums[1]))
    half_first = scatter_y(grad_first, n)
    mixed = mix(after(scalars, grad_first), h, ffns, recv_ffn)
    mixed_other = core_swap(mixed)
    dx0 = dx_block(0, after(scalars, mixed), da0, x_swap(da0), embeddings, dh[0], norm_rows)

    rest_far, half_first = after((rest_far, half_first), dx0)
    rest_z = scatter_near(rest_far, n)
    first_z = scatter_z(half_first, n)
    mixed = assemble(after(scalars, rest_far, half_first), mixed, mixed_other)
    dx1 = dx_block(1, after(scalars, mixed), da1, x_swap(da1), embeddings, dh[1], norm_rows)
    s_up, s_down = finish("finish_rest", after(rest_z, dx1), [(r, units), (units, r)], local)
    grad_input = assemble(scalars, dx0, core_swap(dx0), dx1, core_swap(dx1))
    s_out, s_qkv, both = finish("finish_first", after(first_z, dx1), [(local, r), (3, r, local), (r, 128)], local)
    both = both[:, :4]
    both = both + core_swap(both)
    both = (both + x_swap(both)).T
    gains = jnp.stack([both[0], both[2]])
    shifts = jnp.stack([both[1], both[3]])
    return (mixed, grad_input, s_qkv, s_out, s_up, s_down, gains, shifts, both[3])


def solution(mesh):
    return jax.shard_map(
        functools.partial(body, mesh.shape["dp"]),
        mesh=mesh,
        in_specs=(
            P("dp", None),
            P("dp", None),
            P("dp"),
            P("dp", None),
            P(None, "dp", "tensor"),
            P("tensor", "dp"),
            P("dp", "tensor"),
            P("tensor", "dp"),
            P(None, "dp"),
            P(None, "dp"),
        ),
        out_specs=(
            P("dp", None),
            P("dp", None),
            P(None, "dp", "tensor"),
            P("tensor", "dp"),
            P("dp", "tensor"),
            P("tensor", "dp"),
            P(None, "dp"),
            P(None, "dp"),
            P("dp"),
        ),
        check_vma=False,
    )
```
